32 devices in a mesh: row: 4 (over y, x), col: 8 (over z, core).
Axes of the slice: x: 2, y: 2, z: 4, core: 2. Of those that a mesh axis runs over, the one named last changes fastest.
Arguments:
- latent: bfloat16 [128, 256, 512], P('row', 'col'), may hold values from -12 to 12
- conv_scale: float32 [512], replicated, may hold values from 0.5 to 1.5
- conv_shift: float32 [512], replicated, may hold values from -3 to 3
- expand_weight: bfloat16 [512, 2048], replicated, may hold values from -0.25 to 0.25
- depth_kernel: float32 [9, 2048], replicated, may hold values from -2 to 2
- squeeze_down: bfloat16 [2048, 128], replicated, may hold values from -0.5 to 0.5
- squeeze_up: bfloat16 [128, 2048], replicated, may hold values from -0.5 to 0.5
- project_weight: bfloat16 [2048, 512], replicated, may hold values from -0.125 to 0.125
- block_gain: float32 [512], replicated, may hold values from 0.5 to 1.5
- block_projection: bfloat16 [512, 1536], replicated, may hold values from -0.25 to 0.25
- block_output: bfloat16 [512, 512], replicated, may hold values from -0.25 to 0.25
- block_table: float32 [16, 225], replicated, may hold values from -4 to 300
- first_gain: float32 [512], replicated, may hold values from 0.5 to 1.5
- first_expand: bfloat16 [512, 2048], replicated, may hold values from -0.25 to 0.25
- first_reduce: bfloat16 [2048, 512], replicated, may hold values from -0.125 to 0.125
- grid_gain: float32 [512], replicated, may hold values from 0.5 to 1.5
- grid_projection: bfloat16 [512, 1536], replicated, may hold values from -0.25 to 0.25
- grid_output: bfloat16 [512, 512], replicated, may hold values from -0.25 to 0.25
- grid_table: float32 [16, 225], replicated, may hold values from -4 to 300
- second_gain: float32 [512], replicated, may hold values from 0.5 to 1.5
- second_expand: bfloat16 [512, 2048], replicated, may hold values from -0.25 to 0.25
- second_reduce: bfloat16 [2048, 512], replicated, may hold values from -0.125 to 0.125
Outputs:
- nowcast_latent: bfloat16 [128, 256, 512], P('row', 'col')
The draws below stay inside these ranges and needn't reach their ends.
All inputs are finite; a program needn't handle non-finite values.
Results may differ from the reference program's by a relative error of at most 0.012.
Values may be sent and summed in bfloat16 or wider, within the bound.
A program may use at most 128 MiB of HBM per device.

```python
import jax
import jax.numpy as jnp
from jax import lax

C = 512
HEADS = 16
E = 2048
FF = 2048
SQUEEZE = 128
WIN = 8
HEIGHT = 128
WIDTH = 256
N_ROW = 4
N_COL = 8


def draw_latent(key, part):
    key = jax.random.fold_in(key, 7301)
    row_key = jax.random.fold_in(key, 0)
    col_key = jax.random.fold_in(key, 1)
    main_key = jax.random.fold_in(key, 2)
    offset_key = jax.random.fold_in(key, 4)
    patch_key = jax.random.fold_in(key, 5)
    rising = 3.0 ** (jnp.arange(HEIGHT, dtype=jnp.float32) / max(HEIGHT - 1, 1))
    row_factor = rising * jnp.exp(jax.random.uniform(row_key, (HEIGHT,), jnp.float32, -0.35, 0.35))
    col_factor = jnp.exp(jax.random.uniform(col_key, (WIDTH,), jnp.float32, -0.35, 0.35))
    base = jnp.clip(jax.random.normal(main_key, (HEIGHT, WIDTH, C), jnp.float32), -4.0, 4.0)
    centre_key, across_key, tall_key, broad_key = jax.random.split(patch_key, 4)
    centre_row = jax.random.uniform(centre_key, (4,), jnp.float32, 0.0, 1.0)
    centre_col = jax.random.uniform(across_key, (4,), jnp.float32, 0.05, 0.95)
    half_row = jax.random.uniform(tall_key, (4,), jnp.float32, 0.2, 0.45)
    half_col = jax.random.uniform(broad_key, (4,), jnp.float32, 0.06, 0.12)
    row_spot = (jnp.arange(HEIGHT, dtype=jnp.float32) + 0.5) / HEIGHT
    col_spot = (jnp.arange(WIDTH, dtype=jnp.float32) + 0.5) / WIDTH
    storm = jnp.zeros((HEIGHT, WIDTH), jnp.float32)
    for patch in range(4):
        row_inside = jax.nn.sigmoid((half_row[patch] - jnp.abs(row_spot - centre_row[patch])) / 0.02)
        col_inside = jax.nn.sigmoid((half_col[patch] - jnp.abs(col_spot - centre_col[patch])) / 0.01)
        storm = storm + row_inside[:, None] * col_inside[None, :]
    storm = jnp.clip(storm, 0.0, 1.0)
    channel_offset = jax.random.uniform(offset_key, (C,), jnp.float32, -2.5, 2.5)
    shaped = base * row_factor[:, None, None] * col_factor[None, :, None] / 1.7 * (1.0 + 0.5 * storm[:, :, None])
    shaped = shaped + (2.0 * storm - 1.0)[:, :, None] * channel_offset
    return jnp.clip(shaped, -12.0, 12.0).astype(jnp.bfloat16)


def relative_table(key, salt):
    key = jax.random.fold_in(key, salt)
    base_key = jax.random.fold_in(key, 0)
    spots = (2 * WIN - 1) ** 2
    base = jnp.clip(jax.random.normal(base_key, (HEADS, spots), jnp.float32), -4.0, 4.0)
    return base.astype(jnp.float32)


def draw_block_table(key, part):
    return relative_table(key, 8101)


def draw_grid_table(key, part):
    return relative_table(key, 8209)


def noise(rng, shape, deviation, bound, kind=jnp.bfloat16):
    return jnp.clip(deviation * jax.random.normal(rng, shape, jnp.float32), -bound, bound).astype(kind)


def setup_inputs(seed: int = 0) -> dict:
    streams_of = jax.random.split(jax.random.key(seed), 23)
    return {
        "latent": draw_latent(jax.random.fold_in(streams_of[22], 71), 0),
        "conv_scale": jnp.clip(1.0 + 0.1 * jax.random.normal(streams_of[1], (C,), jnp.float32), 0.5, 1.5),
        "conv_shift": noise(streams_of[2], (C,), 0.5, 3.0, jnp.float32),
        "expand_weight": noise(streams_of[3], (C, E), C ** -0.5, 0.25),
        "depth_kernel": noise(streams_of[4], (9, E), 9 ** -0.5, 2.0, jnp.float32),
        "squeeze_down": noise(streams_of[5], (E, SQUEEZE), SQUEEZE ** -0.5, 0.5),
        "squeeze_up": noise(streams_of[6], (SQUEEZE, E), SQUEEZE ** -0.5, 0.5),
        "project_weight": noise(streams_of[7], (E, C), E ** -0.5, 0.125),
        "block_gain": jnp.clip(1.0 + 0.1 * jax.random.normal(streams_of[8], (C,), jnp.float32), 0.5, 1.5),
        "block_projection": noise(streams_of[9], (C, 3 * C), C ** -0.5, 0.25),
        "block_output": noise(streams_of[10], (C, C), C ** -0.5, 0.25),
        "block_table": draw_block_table(jax.random.fold_in(streams_of[22], 71), 0),
        "first_gain": jnp.clip(1.0 + 0.1 * jax.random.normal(streams_of[12], (C,), jnp.float32), 0.5, 1.5),
        "first_expand": noise(streams_of[13], (C, FF), C ** -0.5, 0.25),
        "first_reduce": noise(streams_of[14], (FF, C), FF ** -0.5, 0.125),
        "grid_gain": jnp.clip(1.0 + 0.1 * jax.random.normal(streams_of[15], (C,), jnp.float32), 0.5, 1.5),
        "grid_projection": noise(streams_of[16], (C, 3 * C), C ** -0.5, 0.25),
        "grid_output": noise(streams_of[17], (C, C), C ** -0.5, 0.25),
        "grid_table": draw_grid_table(jax.random.fold_in(streams_of[22], 71), 0),
        "second_gain": jnp.clip(1.0 + 0.1 * jax.random.normal(streams_of[19], (C,), jnp.float32), 0.5, 1.5),
        "second_expand": noise(streams_of[20], (C, FF), C ** -0.5, 0.25),
        "second_reduce": noise(streams_of[21], (FF, C), FF ** -0.5, 0.125),
    }


def layer_norm_apply(values, norm_gain):
    widened = values.astype(jnp.float32)
    center = widened - lax.optimization_barrier(jnp.mean(widened, axis=-1, keepdims=True))
    spread = lax.optimization_barrier(jnp.mean(center * center, axis=-1, keepdims=True))
    return (center * lax.rsqrt(spread + 1e-05) * norm_gain).astype(jnp.bfloat16)

def position_bias(offset_bias_lookup):
    position = jnp.arange(WIN * WIN)
    down_pos = position // WIN
    across = position % WIN
    relative = (down_pos[:, None] - down_pos[None, :] + WIN - 1) * (2 * WIN - 1) + (across[:, None] - across[None, :] + WIN - 1)
    return offset_bias_lookup[:, relative]

def attend(triple, pos_bias):
    window_count, tokens, three_width = triple.shape
    feature_width = three_width // 3
    head_count = pos_bias.shape[0]
    head_size = feature_width // head_count
    queries = triple[..., :feature_width].reshape(window_count, tokens, head_count, head_size).astype(jnp.float32)
    key_row_list = triple[..., feature_width:2 * feature_width].reshape(window_count, tokens, head_count, head_size).astype(jnp.float32)
    values = triple[..., 2 * feature_width:].reshape(window_count, tokens, head_count, head_size).astype(jnp.float32)
    scores = jnp.einsum('nqhd,nkhd->nhqk', queries, key_row_list) * head_size ** (-0.5) + pos_bias[None]
    row_max = lax.optimization_barrier(jnp.max(scores, axis=-1, keepdims=True))
    weight_tensors = jnp.exp(scores - row_max)
    attention_weight_map = (weight_tensors / lax.optimization_barrier(jnp.sum(weight_tensors, axis=-1, keepdims=True))).astype(jnp.bfloat16)
    mixed = jnp.einsum('nhqk,nkhd->nqhd', attention_weight_map.astype(jnp.float32), values)
    return mixed.astype(jnp.bfloat16).reshape(window_count, tokens, feature_width)

def attention_sublayer(windows, norm_gain, in_weight, out_weight, pos_bias):
    normed = layer_norm_apply(windows, norm_gain)
    triple = jnp.dot(normed, in_weight, preferred_element_type=jnp.float32).astype(jnp.bfloat16)
    per_device = triple.shape[0] // (N_ROW * N_COL)
    grouped = triple.reshape(N_ROW * N_COL, per_device, WIN * WIN, triple.shape[-1])
    mixed = lax.map(lambda blocked: attend(blocked, pos_bias), grouped)
    mixed = mixed.reshape(windows.shape[0], WIN * WIN, -1)
    return (windows.astype(jnp.float32) + jnp.dot(mixed, out_weight, preferred_element_type=jnp.float32)).astype(jnp.bfloat16)

def feed_forward(values, norm_gain, in_weight, out_weight):
    normed = layer_norm_apply(values, norm_gain)
    hidden = jax.nn.gelu(jnp.dot(normed, in_weight, preferred_element_type=jnp.float32), approximate=True).astype(jnp.bfloat16)
    return (values.astype(jnp.float32) + jnp.dot(hidden, out_weight, preferred_element_type=jnp.float32)).astype(jnp.bfloat16)

def block_windows(field):
    feats = field.shape[-1]
    return field.reshape(HEIGHT // WIN, WIN, WIDTH // WIN, WIN, feats).transpose(0, 2, 1, 3, 4).reshape(-1, WIN * WIN, feats)

def block_field(windows):
    feats = windows.shape[-1]
    return windows.reshape(HEIGHT // WIN, WIDTH // WIN, WIN, WIN, feats).transpose(0, 2, 1, 3, 4).reshape(HEIGHT, WIDTH, feats)

def grid_windows(field):
    feats = field.shape[-1]
    return field.reshape(WIN, HEIGHT // WIN, WIN, WIDTH // WIN, feats).transpose(1, 3, 0, 2, 4).reshape(-1, WIN * WIN, feats)

def grid_field(windows):
    feats = windows.shape[-1]
    return windows.reshape(HEIGHT // WIN, WIDTH // WIN, WIN, WIN, feats).transpose(2, 0, 3, 1, 4).reshape(HEIGHT, WIDTH, feats)

def squeeze_gate(pooled, squeeze_down, squeeze_up):
    reduced = jax.nn.silu(jnp.dot(pooled[None, :], squeeze_down.astype(jnp.float32), precision=lax.Precision.HIGHEST))
    return jax.nn.sigmoid(jnp.dot(reduced, squeeze_up.astype(jnp.float32), precision=lax.Precision.HIGHEST))[0]

def reference(latent, conv_scale, conv_shift, expand_weight, depth_kernel, squeeze_down, squeeze_up, project_weight, block_gain, block_projection, block_output, block_table, first_gain, first_expand, first_reduce, grid_gain, grid_projection, grid_output, grid_table, second_gain, second_expand, second_reduce):
    conv_in = (latent.astype(jnp.float32) * conv_scale + conv_shift).astype(jnp.bfloat16)
    expanded = jax.nn.gelu(jnp.dot(conv_in, expand_weight, preferred_element_type=jnp.float32), approximate=True).astype(jnp.bfloat16)
    padded = jnp.pad(expanded, ((1, 1), (1, 1), (0, 0)))
    summed = jnp.zeros(expanded.shape, jnp.float32)
    for offset in range(9):
        down_step = offset // 3
        side_step = offset % 3
        summed = summed + padded[down_step:down_step + HEIGHT, side_step:side_step + WIDTH].astype(jnp.float32) * depth_kernel[offset]
    depthwise = jax.nn.gelu(summed, approximate=True)
    pooled = lax.optimization_barrier(jnp.sum(depthwise, axis=(0, 1))) / (HEIGHT * WIDTH)
    excite = squeeze_gate(pooled, squeeze_down, squeeze_up)
    gated = (depthwise * excite).astype(jnp.bfloat16)
    conv_out = (latent.astype(jnp.float32) + jnp.dot(gated, project_weight, preferred_element_type=jnp.float32)).astype(jnp.bfloat16)
    section = block_field(attention_sublayer(block_windows(conv_out), block_gain, block_projection, block_output, position_bias(block_table)))
    section = feed_forward(section, first_gain, first_expand, first_reduce)
    section = grid_field(attention_sublayer(grid_windows(section), grid_gain, grid_projection, grid_output, position_bias(grid_table)))
    return feed_forward(section, second_gain, second_expand, second_reduce)
```

```python
import functools

import jax
import jax.numpy as jnp
import numpy as np
from jax import lax
from jax.experimental import pallas as pl
from jax.experimental.pallas import tpu as pltpu
from jax.sharding import PartitionSpec as P

WIN = 8


def extended(cells, sides, width):
    for axis, dim in sides:
        count = lax.axis_size(axis)
        ends = count - 1
        head = lax.slice_in_dim(cells, 0, width, axis=dim)
        tail = lax.slice_in_dim(cells, cells.shape[dim] - width, cells.shape[dim], axis=dim)
        cells = jnp.concatenate(
            [
                lax.ppermute(tail, axis, [(i, (i + 1) % count) for i in range(ends)]),
                cells,
                lax.ppermute(head, axis, [((i + 1) % count, i) for i in range(ends)]),
            ],
            axis=dim,
        )
    return cells


def layer_norm_apply(values, norm_gain):
    widened = values.astype(jnp.float32)
    center = widened - jnp.mean(widened, axis=-1, keepdims=True)
    spread = jnp.mean(center * center, axis=-1, keepdims=True)
    return (center * lax.rsqrt(spread + 1e-05) * norm_gain).astype(jnp.bfloat16)


def position_bias(offset_bias_lookup):
    spots = offset_bias_lookup.shape[1]
    position = jnp.arange(WIN * WIN)
    down_pos = position // WIN
    across = position % WIN
    relative = (down_pos[:, None] - down_pos[None, :] + WIN - 1) * (2 * WIN - 1) + (
        across[:, None] - across[None, :] + WIN - 1
    )
    indicator_matrix = (relative[:, :, None] == jnp.arange(spots)[None, None, :]).astype(
        jnp.float32
    )
    return jnp.einsum(
        "bp,rjp->brj", offset_bias_lookup, indicator_matrix, precision=lax.Precision.HIGHEST
    )


def attend(triple, pos_bias):
    window_count, tokens, three_width = triple.shape
    feature_width = three_width // 3
    head_count = pos_bias.shape[0]
    head_size = feature_width // head_count
    queries = triple[..., :feature_width].reshape(window_count, tokens, head_count, head_size)
    key_row_list = triple[..., feature_width : 2 * feature_width].reshape(
        window_count, tokens, head_count, head_size
    )
    values = triple[..., 2 * feature_width :].reshape(window_count, tokens, head_count, head_size)
    scores = (
        jnp.einsum("nqhd,nkhd->nhqk", queries, key_row_list, preferred_element_type=jnp.float32)
        * head_size ** (-0.5)
        + pos_bias[None]
    )
    row_max = jnp.max(scores, axis=-1, keepdims=True)
    weight_tensors = jnp.exp(scores - row_max)
    attention_weight_map = (
        weight_tensors / jnp.sum(weight_tensors, axis=-1, keepdims=True)
    ).astype(jnp.bfloat16)
    mixed = jnp.einsum(
        "nhqk,nkhd->nqhd", attention_weight_map, values, preferred_element_type=jnp.float32
    )
    return mixed.astype(jnp.bfloat16).reshape(window_count, tokens, feature_width)


def attention_sublayer(windows, norm_gain, in_weight, out_weight, pos_bias):
    normed = layer_norm_apply(windows, norm_gain)
    triple = jnp.dot(normed, in_weight, preferred_element_type=jnp.float32).astype(jnp.bfloat16)
    mixed = attend(triple, pos_bias)
    return (
        windows.astype(jnp.float32) + jnp.dot(mixed, out_weight, preferred_element_type=jnp.float32)
    ).astype(jnp.bfloat16)


def feed_forward(values, norm_gain, in_weight, out_weight):
    normed = layer_norm_apply(values, norm_gain)
    hidden = jax.nn.gelu(
        jnp.dot(normed, in_weight, preferred_element_type=jnp.float32), approximate=True
    ).astype(jnp.bfloat16)
    return (
        values.astype(jnp.float32) + jnp.dot(hidden, out_weight, preferred_element_type=jnp.float32)
    ).astype(jnp.bfloat16)


def to_blocks(field):
    row_count, col_count, feats = field.shape
    return (
        field.reshape(row_count // WIN, WIN, col_count // WIN, WIN, feats)
        .transpose(0, 2, 1, 3, 4)
        .reshape(-1, WIN * WIN, feats)
    )


def from_blocks(windows, row_count, col_count):
    feats = windows.shape[-1]
    return (
        windows.reshape(row_count // WIN, col_count // WIN, WIN, WIN, feats)
        .transpose(0, 2, 1, 3, 4)
        .reshape(row_count, col_count, feats)
    )


def axis_shape(length, devices):
    fold = max(1, WIN // devices)
    rest = length // max(devices, WIN)
    span = min(devices, WIN)
    return (fold, rest, span, devices // span)


def grid_layout(field):
    row_devices = lax.axis_size("row")
    col_devices = lax.axis_size("col")
    row_count, col_count, feats = field.shape
    row_fold, row_rest, row_span, row_hop = axis_shape(row_count, row_devices)
    col_fold, col_rest, col_span, col_hop = axis_shape(col_count, col_devices)
    ordered_layout = field.reshape(
        row_fold, row_devices, row_rest, col_fold, col_devices, col_rest, feats
    )
    flat = ordered_layout.transpose(1, 4, 0, 2, 3, 5, 6).reshape(
        row_devices * col_devices, row_fold, row_rest, col_fold, col_rest, feats
    )
    flat = lax.all_to_all(flat, ("row", "col"), split_axis=0, concat_axis=0, tiled=True)
    moved = flat.reshape(
        row_devices, col_devices, row_fold, row_rest, col_fold, col_rest, feats
    ).transpose(2, 0, 3, 4, 1, 5, 6)
    moved = moved.reshape(
        row_fold, row_span, row_hop, row_rest, col_fold, col_span, col_hop, col_rest, feats
    )
    return moved.transpose(2, 3, 6, 7, 1, 0, 5, 4, 8).reshape(-1, WIN * WIN, feats)


def spatial_layout(windows, row_count, col_count):
    row_devices = lax.axis_size("row")
    col_devices = lax.axis_size("col")
    feats = windows.shape[-1]
    row_fold, row_rest, row_span, row_hop = axis_shape(row_count, row_devices)
    col_fold, col_rest, col_span, col_hop = axis_shape(col_count, col_devices)
    gridded = windows.reshape(
        row_hop, row_rest, col_hop, col_rest, row_span, row_fold, col_span, col_fold, feats
    )
    ordered_layout = gridded.transpose(5, 4, 0, 1, 7, 6, 2, 3, 8).reshape(
        row_fold, row_devices, row_rest, col_fold, col_devices, col_rest, feats
    )
    flat = ordered_layout.transpose(1, 4, 0, 2, 3, 5, 6).reshape(
        row_devices * col_devices, row_fold, row_rest, col_fold, col_rest, feats
    )
    flat = lax.all_to_all(flat, ("row", "col"), split_axis=0, concat_axis=0, tiled=True)
    moved = flat.reshape(
        row_devices, col_devices, row_fold, row_rest, col_fold, col_rest, feats
    ).transpose(2, 0, 3, 4, 1, 5, 6)
    return moved.reshape(row_count, col_count, feats)


def squeeze_gate(pooled, squeeze_down, squeeze_up):
    reduced = jax.nn.silu(
        jnp.dot(pooled[None, :], squeeze_down.astype(jnp.float32), precision=lax.Precision.HIGHEST)
    )
    return jax.nn.sigmoid(
        jnp.dot(reduced, squeeze_up.astype(jnp.float32), precision=lax.Precision.HIGHEST)
    )[0]


def axis_sum_kernel(axis, count, x_ref, o_ref, slots, send_sem, recv_sem):
    me = lax.axis_index(axis)
    barrier = pltpu.get_barrier_semaphore()
    peers = [lax.rem(me + step, count) for step in range(1, count)]
    for peer in peers:
        pl.semaphore_signal(
            barrier, inc=1, device_id={axis: peer}, device_id_type=pl.DeviceIdType.MESH
        )
    pl.semaphore_wait(barrier, count - 1)
    copies = []
    for step, peer in enumerate(peers):
        copy = pltpu.make_async_remote_copy(
            src_ref=x_ref,
            dst_ref=slots.at[step],
            send_sem=send_sem.at[step],
            recv_sem=recv_sem.at[step],
            device_id={axis: peer},
            device_id_type=pl.DeviceIdType.MESH,
        )
        copy.start()
        copies.append(copy)
    for copy in copies:
        copy.wait()
    total = x_ref[...]
    for step in range(count - 1):
        total = total + slots[step]
    o_ref[...] = total


def axis_sum(values, axis, collective_id):
    count = lax.axis_size(axis)
    if count == 1:
        return values
    return pl.pallas_call(
        functools.partial(axis_sum_kernel, axis, count),
        out_shape=jax.ShapeDtypeStruct(values.shape, values.dtype),
        in_specs=[pl.BlockSpec(memory_space=pltpu.VMEM)],
        out_specs=pl.BlockSpec(memory_space=pltpu.VMEM),
        scratch_shapes=[
            pltpu.VMEM((count - 1,) + values.shape, values.dtype),
            pltpu.SemaphoreType.DMA((count - 1,)),
            pltpu.SemaphoreType.DMA((count - 1,)),
        ],
        compiler_params=pltpu.CompilerParams(
            collective_id=collective_id, has_side_effects=True, vmem_limit_bytes=4 * 1024 * 1024
        ),
        name="axis_sum_" + axis,
    )(values)


LANES = 128
GROUP = 256


def normed_rows(widened, gain):
    center = widened - jnp.mean(widened, axis=-1, keepdims=True)
    spread = jnp.mean(center * center, axis=-1, keepdims=True)
    return (center * lax.rsqrt(spread + 1e-05) * gain).astype(jnp.bfloat16)


def mixer_kernel(
    layout, head_size, x_ref, gain_ref, bias_ref, late_gain_ref, proj_hbm, out_hbm, up_hbm, down_hbm,
    o_ref, triple, heads, proj_ref, out_w_ref, up_ref, down_ref, sems,
):
    kind, across = layout
    rows_total, feats = x_ref.shape
    tokens = WIN * WIN
    window_count = rows_total // tokens
    slabs = feats // LANES
    per_slab = LANES // head_size
    moves = [
        pltpu.make_async_copy(src, dst, sems.at[k])
        for k, (src, dst) in enumerate(
            ((proj_hbm, proj_ref), (out_hbm, out_w_ref), (up_hbm, up_ref), (down_hbm, down_ref))
        )
    ]
    moves[0].start()
    moves[0].wait()
    for move in moves[1:]:
        move.start()
    chunk = 256

    def project(step, carry):
        rows = pl.ds(pl.multiple_of(step * chunk, chunk), chunk)
        normed = normed_rows(x_ref[rows, :].astype(jnp.float32), gain_ref[...])
        for part in range(3 * slabs // 2):
            product = jnp.dot(
                normed, proj_ref[:, part * GROUP : (part + 1) * GROUP],
                preferred_element_type=jnp.float32,
            ).astype(jnp.bfloat16).astype(jnp.float32)
            triple[2 * part, rows, :] = product[:, :LANES]
            triple[2 * part + 1, rows, :] = product[:, LANES:]
        return carry

    lax.fori_loop(0, rows_total // chunk, project, 0)

    def places(window):
        if kind == "strided":
            return [pl.ds(window, tokens, stride=across)]
        per_row = across // WIN
        base = (window // per_row) * (WIN * across) + (window % per_row) * WIN
        return [pl.ds(pl.multiple_of(base + r * across, WIN), WIN) for r in range(WIN)]

    lane = lax.broadcasted_iota(jnp.int32, (tokens, GROUP), 1)
    head_of = (lane % LANES) // head_size
    scale = head_size ** (-0.5)

    def one_window(window):
        spots = places(window)

        def fetch(slab):
            pieces = [triple[slab, spot, :] for spot in spots]
            whole = pieces[0] if len(pieces) == 1 else jnp.concatenate(pieces, axis=0)
            return whole

        empty = jnp.zeros((tokens, LANES), jnp.bfloat16)
        for group in range(slabs // 2):
            first, second = 2 * group, 2 * group + 1
            query_0 = fetch(first).astype(jnp.bfloat16)
            query_1 = fetch(second).astype(jnp.bfloat16)
            keys = jnp.concatenate([fetch(slabs + first), fetch(slabs + second)], axis=1)
            vals = jnp.concatenate([fetch(2 * slabs + first), fetch(2 * slabs + second)], axis=1)
            block_q = jnp.concatenate(
                [
                    jnp.concatenate([query_0, empty], axis=1),
                    jnp.concatenate([empty, query_1], axis=1),
                ],
                axis=0,
            )
            block_k = jnp.concatenate(
                [jnp.where(head_of == j, keys, 0.0).astype(jnp.bfloat16) for j in range(per_slab)],
                axis=0,
            )
            block_v = jnp.concatenate(
                [jnp.where(head_of == j, vals, 0.0).astype(jnp.bfloat16) for j in range(per_slab)],
                axis=0,
            )
            scores = lax.dot_general(
                block_k, block_q, (((1,), (1,)), ((), ())), preferred_element_type=jnp.float32
            )
            scores = (scores * scale + bias_ref[group]).reshape(per_slab, tokens, 2 * tokens)
            weights = jnp.exp(scores - jnp.max(scores, axis=1, keepdims=True))
            shares = weights * (1.0 / jnp.sum(weights, axis=1, keepdims=True))
            shares = shares.reshape(per_slab * tokens, 2 * tokens).astype(jnp.bfloat16)
            mixed = lax.dot_general(
                shares, block_v, (((0,), (0,)), ((), ())), preferred_element_type=jnp.float32
            )
            for slab, part in (
                (first, mixed[:tokens, :LANES]), (second, mixed[tokens:, LANES:])
            ):
                if len(spots) == 1:
                    heads[slab, spots[0], :] = part
                else:
                    for r, spot in enumerate(spots):
                        heads[slab, spot, :] = part[r * WIN : (r + 1) * WIN]

    def attend_pair(step, carry):
        one_window(2 * step)
        one_window(2 * step + 1)
        return carry

    lax.fori_loop(0, window_count // 2, attend_pair, 0)
    for move in moves[1:]:
        move.wait()
    hidden_width = up_ref.shape[1]
    tile = 512

    def feed(step, carry):
        rows = pl.ds(pl.multiple_of(step * chunk, chunk), chunk)
        mixed = jnp.concatenate([heads[s, rows, :] for s in range(slabs)], axis=1).astype(jnp.bfloat16)
        value = (
            x_ref[rows, :].astype(jnp.float32)
            + jnp.dot(mixed, out_w_ref[...], preferred_element_type=jnp.float32)
        ).astype(jnp.bfloat16).astype(jnp.float32)
        normed = normed_rows(value, late_gain_ref[...])
        for k in range(hidden_width // tile):
            part = slice(k * tile, (k + 1) * tile)
            hidden = jax.nn.gelu(
                jnp.dot(normed, up_ref[:, part], preferred_element_type=jnp.float32),
                approximate=True,
            ).astype(jnp.bfloat16)
            value = value + jnp.dot(hidden, down_ref[part, :], preferred_element_type=jnp.float32)
        o_ref[rows, :] = value.astype(jnp.bfloat16)
        return carry

    lax.fori_loop(0, rows_total // chunk, feed, 0)


def mixer(x, layout, gain, in_weight, out_weight, bias, late_gain, up, down, heads_count):
    rows, feats = x.shape
    vmem = pl.BlockSpec(memory_space=pltpu.VMEM)
    hbm = pl.BlockSpec(memory_space=pltpu.HBM)
    flops = 8 * rows * feats * (4 * feats + 2 * up.shape[1])
    return pl.pallas_call(
        functools.partial(mixer_kernel, layout, feats // heads_count),
        out_shape=jax.ShapeDtypeStruct((rows, feats), jnp.bfloat16),
        in_specs=[vmem] * 4 + [hbm] * 4,
        out_specs=vmem,
        scratch_shapes=[
            pltpu.VMEM((3 * feats // LANES, rows, LANES), jnp.float32),
            pltpu.VMEM((feats // LANES, rows, LANES), jnp.float32),
            pltpu.VMEM(in_weight.shape, jnp.bfloat16),
            pltpu.VMEM(out_weight.shape, jnp.bfloat16),
            pltpu.VMEM(up.shape, jnp.bfloat16),
            pltpu.VMEM(down.shape, jnp.bfloat16),
            pltpu.SemaphoreType.DMA((4,)),
        ],
        compiler_params=pltpu.CompilerParams(vmem_limit_bytes=60 * 1024 * 1024),
        cost_estimate=pl.CostEstimate(
            flops=flops, bytes_accessed=12 * 1024 * 1024, transcendentals=0
        ),
        name="mixer_" + layout[0],
    )(x, gain[None], bias, late_gain[None], in_weight, out_weight, up, down)


def key_major_bias(table, down, across):
    head_count, spots = table.shape
    relative = (down[None, :] - down[:, None] + WIN - 1) * (2 * WIN - 1) + (
        across[None, :] - across[:, None] + WIN - 1
    )
    tokens = WIN * WIN
    chosen = (jnp.arange(spots)[:, None] == jnp.asarray(relative.reshape(-1))[None, :]).astype(
        jnp.float32
    )
    spread = jnp.dot(table, chosen, precision=lax.Precision.HIGHEST)
    return (
        spread.reshape(head_count // 8, 2, 4, tokens, tokens)
        .transpose(0, 2, 3, 1, 4)
        .reshape(head_count // 8, 4 * tokens, 2 * tokens)
    )


def split_sublayers(conv_out, run_block, run_grid, block_table, grid_table):
    row_devices = lax.axis_size("row")
    col_devices = lax.axis_size("col")
    row_count, col_count, feats = conv_out.shape
    plain = np.arange(WIN * WIN)
    block_bias = key_major_bias(block_table, plain // WIN, plain % WIN)
    if row_devices > WIN or col_devices > WIN:
        section = run_block(conv_out.reshape(-1, feats), ("blocks", col_count), block_bias)
        windows = grid_layout(section.reshape(row_count, col_count, feats))
        count = windows.shape[0]
        bias = key_major_bias(grid_table, plain // WIN, plain % WIN)
        out = run_grid(windows.transpose(1, 0, 2).reshape(-1, feats), ("strided", count), bias)
        out = out.reshape(WIN * WIN, count, feats).transpose(1, 0, 2)
        return spatial_layout(out, row_count, col_count)
    devices = row_devices * col_devices
    row_fold, col_fold = WIN // row_devices, WIN // col_devices
    row_rest, col_rest = row_count // row_fold, col_count // col_fold
    parts = row_rest // WIN
    count = WIN * col_rest // devices
    pieces = col_rest // count
    order = np.arange(WIN * WIN).reshape(row_devices, col_devices, row_fold, col_fold)
    at = np.indices(order.shape).reshape(4, -1)
    grid_bias = key_major_bias(grid_table, at[0] * row_fold + at[2], at[1] * col_fold + at[3])
    strips = conv_out.reshape(row_fold, parts, WIN, col_count, feats)
    results = []
    for part in range(parts):
        section = run_block(
            strips[:, part].reshape(-1, feats), ("blocks", col_count), block_bias
        )
        sent = (
            section.reshape(row_fold, WIN, col_fold, pieces, count, feats)
            .transpose(1, 3, 0, 2, 4, 5)
            .reshape(devices, row_fold * col_fold * count, feats)
        )
        got = lax.all_to_all(sent, ("row", "col"), split_axis=0, concat_axis=0, tiled=True)
        out = run_grid(got.reshape(-1, feats), ("strided", count), grid_bias)
        back = lax.all_to_all(
            out.reshape(devices, -1, feats), ("row", "col"), split_axis=0, concat_axis=0, tiled=True
        )
        results.append(
            back.reshape(WIN, pieces, row_fold, col_fold, count, feats)
            .transpose(2, 0, 3, 1, 4, 5)
            .reshape(row_fold, WIN, col_count, feats)
        )
    return jnp.stack(results, axis=1).reshape(row_count, col_count, feats)


def device_of(flat, columns):
    return {"row": lax.div(flat, columns), "col": lax.rem(flat, columns)}


def exchange_kernel(
    shape, head_size, x_ref, block_bias, grid_bias, gain_0, gain_1, gain_2, gain_3,
    w0, w1, w2, w3, w4, w5, w6, w7, o_ref,
    triple, heads, v0, v1, v2, v3, v4, v5, v6, v7,
    section, got, output, back, weight_sem, send_sem, recv_sem,
):
    parts, pieces, columns, devices = shape
    feats = x_ref.shape[1]
    slabs = feats // LANES
    per_slab = LANES // head_size
    tokens = WIN * WIN
    message = section.shape[1]
    chunk = 256
    batch = chunk // message
    halves = devices // batch
    part_rows = devices * message
    me = lax.axis_index("row") * columns + lax.axis_index("col")
    barrier = pltpu.get_barrier_semaphore()

    def greet(step, carry):
        pl.semaphore_signal(
            barrier, inc=1, device_id=device_of(lax.rem(me + step, devices), columns),
            device_id_type=pl.DeviceIdType.MESH,
        )
        return carry

    lax.fori_loop(1, devices, greet, 0)
    moves = [
        pltpu.make_async_copy(src, dst, weight_sem.at[k])
        for k, (src, dst) in enumerate(
            zip((w0, w1, w2, w3, w4, w5, w6, w7), (v0, v1, v2, v3, v4, v5, v6, v7))
        )
    ]
    for move in moves:
        move.start()
    for move in moves[:4]:
        move.wait()

    def project(values, rows, gain_ref, weight):
        normed = normed_rows(values.astype(jnp.float32), gain_ref[...])
        for part in range(3 * slabs // 2):
            product = jnp.dot(
                normed, weight[:, part * GROUP : (part + 1) * GROUP],
                preferred_element_type=jnp.float32,
            ).astype(jnp.bfloat16).astype(jnp.float32)
            triple[2 * part, rows, :] = product[:, :LANES]
            triple[2 * part + 1, rows, :] = product[:, LANES:]

    lane = lax.broadcasted_iota(jnp.int32, (tokens, GROUP), 1)
    head_of = (lane % LANES) // head_size
    scale = head_size ** (-0.5)

    def attend_window(spots, bias_ref):
        def fetch(slab):
            pieces = [triple[slab, spot, :] for spot in spots]
            return pieces[0] if len(pieces) == 1 else jnp.concatenate(pieces, axis=0)

        empty = jnp.zeros((tokens, LANES), jnp.bfloat16)
        for group in range(slabs // 2):
            first, second = 2 * group, 2 * group + 1
            query_0 = fetch(first).astype(jnp.bfloat16)
            query_1 = fetch(second).astype(jnp.bfloat16)
            keys = jnp.concatenate([fetch(slabs + first), fetch(slabs + second)], axis=1)
            vals = jnp.concatenate([fetch(2 * slabs + first), fetch(2 * slabs + second)], axis=1)
            block_q = jnp.concatenate(
                [
                    jnp.concatenate([query_0, empty], axis=1),
                    jnp.concatenate([empty, query_1], axis=1),
                ],
                axis=0,
            )
            block_k = jnp.concatenate(
                [jnp.where(head_of == j, keys, 0.0).astype(jnp.bfloat16) for j in range(per_slab)],
                axis=0,
            )
            block_v = jnp.concatenate(
                [jnp.where(head_of == j, vals, 0.0).astype(jnp.bfloat16) for j in range(per_slab)],
                axis=0,
            )
            scores = lax.dot_general(
                block_k, block_q, (((1,), (1,)), ((), ())), preferred_element_type=jnp.float32
            )
            scores = (scores * scale + bias_ref[group]).reshape(per_slab, tokens, 2 * tokens)
            weights = jnp.exp(scores - jnp.max(scores, axis=1, keepdims=True))
            shares = weights * (1.0 / jnp.sum(weights, axis=1, keepdims=True))
            shares = shares.reshape(per_slab * tokens, 2 * tokens).astype(jnp.bfloat16)
            mixed = lax.dot_general(
                shares, block_v, (((0,), (0,)), ((), ())), preferred_element_type=jnp.float32
            )
            for slab, part in (
                (first, mixed[:tokens, :LANES]), (second, mixed[tokens:, LANES:])
            ):
                if len(spots) == 1:
                    heads[slab, spots[0], :] = part
                else:
                    for r, spot in enumerate(spots):
                        heads[slab, spot, :] = part[r * WIN : (r + 1) * WIN]

    def feed(values, rows, gain_ref, out_w, up, down):
        mixed = jnp.concatenate([heads[s, rows, :] for s in range(slabs)], axis=1).astype(jnp.bfloat16)
        value = (
            values.astype(jnp.float32)
            + jnp.dot(mixed, out_w[...], preferred_element_type=jnp.float32)
        ).astype(jnp.bfloat16).astype(jnp.float32)
        normed = normed_rows(value, gain_ref[...])
        tile = 512
        for k in range(up.shape[1] // tile):
            part = slice(k * tile, (k + 1) * tile)
            hidden = jax.nn.gelu(
                jnp.dot(normed, up[:, part], preferred_element_type=jnp.float32),
                approximate=True,
            ).astype(jnp.bfloat16)
            value = value + jnp.dot(hidden, down[part, :], preferred_element_type=jnp.float32)
        return value.astype(jnp.bfloat16)

    def block_step(step, carry):
        base = pl.multiple_of(step * chunk, chunk)
        whole = pl.ds(0, chunk)
        project(x_ref[pl.ds(base, chunk), :], whole, gain_0, v0)

        def attend_pair(piece, inner):
            for fold in range(message // WIN):
                start = piece * (WIN * message) + fold * WIN
                attend_window(
                    [pl.ds(pl.multiple_of(start + r * message, WIN), WIN) for r in range(WIN)],
                    block_bias,
                )
            return inner

        lax.fori_loop(0, batch // WIN, attend_pair, 0)
        done = feed(x_ref[pl.ds(base, chunk), :], whole, gain_1, v1, v2, v3)
        section[pl.ds(step * batch, batch)] = done.reshape(batch, message, feats)

        @pl.when(step == 0)
        def _():
            pl.semaphore_wait(barrier, devices - 1)

        part, half = lax.div(step, halves), lax.rem(step, halves)

        def send(i, inner):
            at = lax.rem(i + me, batch)
            target = lax.rem(at, WIN) * pieces + half * (batch // WIN) + lax.div(at, WIN)
            src, dst = section.at[step * batch + at], got.at[part * devices + me]

            @pl.when(target != me)
            def _():
                pltpu.make_async_remote_copy(
                    src_ref=src, dst_ref=dst, send_sem=send_sem.at[0, part],
                    recv_sem=recv_sem.at[0, part], device_id=device_of(target, columns),
                    device_id_type=pl.DeviceIdType.MESH,
                ).start()

            @pl.when(target == me)
            def _():
                pltpu.make_async_copy(src, dst, recv_sem.at[0, part]).start()

            return inner

        lax.fori_loop(0, batch, send, 0)
        return carry

    lax.fori_loop(0, parts * halves, block_step, 0)
    for move in moves[4:]:
        move.wait()
    slot = lax.rem(me, pieces) * WIN + lax.div(me, pieces)

    def arrived(buffer, kind, part):
        block = buffer.at[pl.ds(part * devices, devices)]
        pltpu.make_async_copy(block, block, recv_sem.at[kind, part]).wait()

    def grid_step(part, carry):
        arrived(got, 0, part)

        def rows_of(half):
            return got[pl.ds(part * devices + half * batch, batch)].reshape(chunk, feats)

        for half in range(halves):
            project(rows_of(half), pl.ds(half * chunk, chunk), gain_2, v4)

        def attend_pair(pair, inner):
            for k in range(2):
                attend_window([pl.ds(2 * pair + k, tokens, stride=WIN)], grid_bias)
            return inner

        lax.fori_loop(0, part_rows // tokens // 2, attend_pair, 0)

        def feed_half(half, inner):
            rows = pl.ds(pl.multiple_of(half * chunk, chunk), chunk)
            done = feed(rows_of(half), rows, gain_3, v5, v6, v7)
            output[pl.ds(part * devices + half * batch, batch)] = done.reshape(batch, message, feats)

            def send(i, inner_2):
                target = half * batch + lax.rem(i + me, batch)
                src, dst = output.at[part * devices + target], back.at[part * devices + slot]

                @pl.when(target != me)
                def _():
                    pltpu.make_async_remote_copy(
                        src_ref=src, dst_ref=dst, send_sem=send_sem.at[1, part],
                        recv_sem=recv_sem.at[1, part], device_id=device_of(target, columns),
                        device_id_type=pl.DeviceIdType.MESH,
                    ).start()

                @pl.when(target == me)
                def _():
                    pltpu.make_async_copy(src, dst, recv_sem.at[1, part]).start()

                return inner_2

            lax.fori_loop(0, batch, send, 0)
            return inner

        lax.fori_loop(0, halves, feed_half, 0)
        return carry

    lax.fori_loop(0, parts, grid_step, 0)
    fold_rows = parts * WIN
    width = pieces * WIN

    def finish(part, carry):
        arrived(back, 1, part)

        def place(down, inner):
            tiles = [
                back[part * devices + piece * WIN + down].astype(jnp.float32)
                for piece in range(pieces)
            ]
            for fold in range(message // WIN):
                line = jnp.concatenate([t[fold * WIN : (fold + 1) * WIN] for t in tiles], axis=0)
                start = (fold * fold_rows + part * WIN + down) * width
                o_ref[pl.ds(pl.multiple_of(start, width), width), :] = line.astype(jnp.bfloat16)
            return inner

        return lax.fori_loop(0, WIN, place, carry)

    lax.fori_loop(0, parts, finish, 0)
    for kind, buffer in ((0, section), (1, output)):
        for part in range(parts):
            sent = buffer.at[pl.ds(part * devices, devices - 1)]
            pltpu.make_async_copy(sent, sent, send_sem.at[kind, part]).wait()


def exchange(x, shape, head_size, block_bias, grid_bias, gains, weights):
    parts, pieces, columns, devices = shape
    rows, feats = x.shape
    message = rows // (parts * devices)
    part_rows = rows // parts
    vmem = pl.BlockSpec(memory_space=pltpu.VMEM)
    hbm = pl.BlockSpec(memory_space=pltpu.HBM)
    mail = pltpu.VMEM((parts * devices, message, feats), jnp.bfloat16)
    return pl.pallas_call(
        functools.partial(exchange_kernel, shape, head_size),
        out_shape=jax.ShapeDtypeStruct((rows, feats), jnp.bfloat16),
        in_specs=[vmem] * 7 + [hbm] * 8,
        out_specs=vmem,
        scratch_shapes=[
            pltpu.VMEM((3 * feats // LANES, part_rows, LANES), jnp.float32),
            pltpu.VMEM((feats // LANES, part_rows, LANES), jnp.float32),
        ]
        + [pltpu.VMEM(w.shape, jnp.bfloat16) for w in weights]
        + [
            mail, mail, mail, mail,
            pltpu.SemaphoreType.DMA((8,)),
            pltpu.SemaphoreType.DMA((2, parts)),
            pltpu.SemaphoreType.DMA((2, parts)),
        ],
        compiler_params=pltpu.CompilerParams(
            collective_id=3, has_side_effects=True, vmem_limit_bytes=48 * 1024 * 1024
        ),
        name="exchange",
    )(x, block_bias, grid_bias, *[g[None] for g in gains], *weights)


def compact(row_count, col_count):
    row_devices, col_devices = lax.axis_size("row"), lax.axis_size("col")
    return (
        2 * row_devices == WIN and col_devices == WIN
        and row_count % (2 * WIN) == 0 and col_count == WIN * row_devices
    )


PAD = 8


def conv_kernel(
    row_count, col_count, flags, ext_ref, scale_ref, shift_ref, expand_ref, taps_ref,
    o_ref, sums_ref, conv_in, expanded,
):
    wide = col_count + PAD
    tall = row_count + 2
    width = expand_ref.shape[1]
    block = expanded.shape[-1]
    bounds = [8 * k for k in range(row_count // 8)] + [tall]
    for low, high in zip(bounds[:-1], bounds[1:]):
        rows = slice(low * wide, high * wide)
        conv_in[rows, :] = (
            ext_ref[rows, :].astype(jnp.float32) * scale_ref[...] + shift_ref[...]
        ).astype(jnp.bfloat16)
    spot = lax.broadcasted_iota(jnp.int32, (1, PAD, block), 1)
    side = jnp.where(spot == 0, flags[3], jnp.where(spot == PAD - 1, flags[2], 0.0))

    def channels(step, carry):
        lanes = pl.ds(pl.multiple_of(step * block, block), block)
        for low, high in zip(bounds[:-1], bounds[1:]):
            product = jnp.dot(
                conv_in[low * wide : high * wide, :], expand_ref[:, lanes],
                preferred_element_type=jnp.float32,
            )
            value = jax.nn.gelu(product, approximate=True).astype(jnp.bfloat16)
            expanded[low:high] = value.astype(jnp.float32).reshape(high - low, wide, block)
        expanded[0] = expanded[0] * flags[0]
        expanded[tall - 1] = expanded[tall - 1] * flags[1]
        expanded[:, col_count:, :] = expanded[:, col_count:, :] * side
        for half in range(block // LANES):
            inner = slice(half * LANES, (half + 1) * LANES)
            outer = pl.ds(pl.multiple_of(step * block + half * LANES, LANES), LANES)
            taps = [taps_ref[k : k + 1, outer] for k in range(9)]

            def rows_of(group, total):
                base = group * 4
                held = [expanded[base + k, :, inner] for k in range(6)]
                for k in range(4):
                    parts = [
                        held[k] * taps[side_step]
                        + held[k + 1] * taps[3 + side_step]
                        + held[k + 2] * taps[6 + side_step]
                        for side_step in range(3)
                    ]
                    summed = (
                        pltpu.roll(parts[0], 1, 0) + parts[1] + pltpu.roll(parts[2], wide - 1, 0)
                    )[:col_count]
                    deep = jax.nn.gelu(summed, approximate=True)
                    total = total + jnp.sum(deep.reshape(col_count // 8, 8, LANES), axis=0)
                    at = pl.ds(pl.multiple_of((base + k) * col_count, col_count), col_count)
                    o_ref[at, outer] = deep.astype(o_ref.dtype)
                return total

            total = lax.fori_loop(0, row_count // 4, rows_of, jnp.zeros((8, LANES), jnp.float32))
            sums_ref[:, outer] = jnp.sum(total, axis=0, keepdims=True)
        return carry

    lax.fori_loop(0, width // block, channels, 0)


def depthwise_stage(latent, conv_scale, conv_shift, expand_weight, depth_kernel):
    row_count, col_count, feats = latent.shape
    width = expand_weight.shape[1]
    row_at, col_at = lax.axis_index("row"), lax.axis_index("col")
    flags = jnp.stack(
        [row_at > 0, row_at < lax.axis_size("row") - 1, col_at > 0, col_at < lax.axis_size("col") - 1]
    ).astype(jnp.float32)
    tall = extended(latent, (("row", 0),), 1)
    count = lax.axis_size("col")
    ahead = [(i, i + 1) for i in range(count - 1)]
    left = lax.ppermute(tall[:, col_count - 1 :], "col", ahead)
    right = lax.ppermute(tall[:, :1], "col", [(b, a) for a, b in ahead])
    blank = jnp.zeros((row_count + 2, PAD - 2, feats), latent.dtype)
    ext = jnp.concatenate([tall, right, blank, left], axis=1).reshape(-1, feats)
    vmem = pl.BlockSpec(memory_space=pltpu.VMEM)
    block = 256
    return pl.pallas_call(
        functools.partial(conv_kernel, row_count, col_count),
        out_shape=(
            jax.ShapeDtypeStruct((row_count * col_count, width), jnp.bfloat16),
            jax.ShapeDtypeStruct((1, width), jnp.float32),
        ),
        in_specs=[pl.BlockSpec(memory_space=pltpu.SMEM)] + [vmem] * 5,
        out_specs=(vmem, vmem),
        scratch_shapes=[
            pltpu.VMEM(ext.shape, jnp.bfloat16),
            pltpu.VMEM((row_count + 2, col_count + PAD, block), jnp.float32),
        ],
        compiler_params=pltpu.CompilerParams(vmem_limit_bytes=20 * 1024 * 1024),
        name="conv_stage",
    )(flags, ext, conv_scale[None], conv_shift[None], expand_weight, depth_kernel)


def per_device(
    latent,
    conv_scale,
    conv_shift,
    expand_weight,
    depth_kernel,
    squeeze_down,
    squeeze_up,
    project_weight,
    block_gain,
    block_projection,
    block_output,
    block_table,
    first_gain,
    first_expand,
    first_reduce,
    grid_gain,
    grid_projection,
    grid_output,
    grid_table,
    second_gain,
    second_expand,
    second_reduce,
):
    row_devices = lax.axis_size("row")
    col_devices = lax.axis_size("col")
    row_count, col_count, channels = latent.shape
    depthwise, local_sums = depthwise_stage(
        latent, conv_scale, conv_shift, expand_weight, depth_kernel
    )
    local_sums = local_sums.reshape(-1, LANES)
    channel_sums = axis_sum(axis_sum(local_sums, "row", 1), "col", 2).reshape(-1)
    pooled = channel_sums / (row_count * row_devices * col_count * col_devices)
    excite = squeeze_gate(pooled, squeeze_down, squeeze_up)
    gated = (depthwise.astype(jnp.float32) * excite).astype(jnp.bfloat16)
    conv_out = (
        latent.reshape(-1, channels).astype(jnp.float32)
        + jnp.dot(gated, project_weight, preferred_element_type=jnp.float32)
    ).astype(jnp.bfloat16).reshape(row_count, col_count, channels)

    def run_block(cells, layout, bias):
        return mixer(
            cells, layout, block_gain, block_projection, block_output, bias, first_gain,
            first_expand, first_reduce, block_table.shape[0],
        )

    def run_grid(cells, layout, bias):
        return mixer(
            cells, layout, grid_gain, grid_projection, grid_output, bias, second_gain,
            second_expand, second_reduce, grid_table.shape[0],
        )

    if compact(row_count, col_count):
        parts, pieces = row_count // (2 * WIN), col_count // WIN
        plain = np.arange(WIN * WIN)
        block_bias = key_major_bias(block_table, plain // WIN, plain % WIN)
        grid_bias = key_major_bias(
            grid_table, 2 * (plain // (2 * col_devices)) + plain % 2, plain // 2 % col_devices
        )
        ordered = (
            conv_out.reshape(2, parts, WIN, pieces, WIN, channels)
            .transpose(1, 3, 2, 0, 4, 5)
            .reshape(-1, channels)
        )
        return exchange(
            ordered, (parts, pieces, col_devices, row_devices * col_devices),
            channels // block_table.shape[0], block_bias, grid_bias,
            (block_gain, first_gain, grid_gain, second_gain),
            (block_projection, block_output, first_expand, first_reduce,
             grid_projection, grid_output, second_expand, second_reduce),
        ).reshape(row_count, col_count, channels)
    return split_sublayers(conv_out, run_block, run_grid, block_table, grid_table)


def solution(mesh):
    placed = (
        P("row", "col", None),
        P(),
        P(),
        P(),
        P(),
        P(),
        P(),
        P(),
        P(),
        P(),
        P(),
        P(),
        P(),
        P(),
        P(),
        P(),
        P(),
        P(),
        P(),
        P(),
        P(),
        P(),
    )
    return jax.shard_map(
        per_device, mesh=mesh, in_specs=placed, out_specs=P("row", "col", None), check_vma=False
    )
```

```python
import functools

import jax
import jax.numpy as jnp
import numpy as np
from jax import lax
from jax.experimental import pallas as pl
from jax.experimental.pallas import tpu as pltpu
from jax.sharding import PartitionSpec as P

WIN = 8
PAD = 8


def extended(cells, sides, width):
    for axis, dim in sides:
        count = lax.axis_size(axis)
        ends = count - 1
        head = lax.slice_in_dim(cells, 0, width, axis=dim)
        tail = lax.slice_in_dim(cells, cells.shape[dim] - width, cells.shape[dim], axis=dim)
        cells = jnp.concatenate(
            [
                lax.ppermute(tail, axis, [(i, (i + 1) % count) for i in range(ends)]),
                cells,
                lax.ppermute(head, axis, [((i + 1) % count, i) for i in range(ends)]),
            ],
            axis=dim,
        )
    return cells


def layer_norm_apply(values, norm_gain):
    widened = values.astype(jnp.float32)
    center = widened - jnp.mean(widened, axis=-1, keepdims=True)
    spread = jnp.mean(center * center, axis=-1, keepdims=True)
    return (center * lax.rsqrt(spread + 1e-05) * norm_gain).astype(jnp.bfloat16)


def position_bias(offset_bias_lookup):
    spots = offset_bias_lookup.shape[1]
    position = jnp.arange(WIN * WIN)
    down_pos = position // WIN
    across = position % WIN
    relative = (down_pos[:, None] - down_pos[None, :] + WIN - 1) * (2 * WIN - 1) + (
        across[:, None] - across[None, :] + WIN - 1
    )
    indicator_matrix = (relative[:, :, None] == jnp.arange(spots)[None, None, :]).astype(
        jnp.float32
    )
    return jnp.einsum(
        "bp,rjp->brj", offset_bias_lookup, indicator_matrix, precision=lax.Precision.HIGHEST
    )


def attend(triple, pos_bias):
    window_count, tokens, three_width = triple.shape
    feature_width = three_width // 3
    head_count = pos_bias.shape[0]
    head_size = feature_width // head_count
    queries = triple[..., :feature_width].reshape(window_count, tokens, head_count, head_size)
    key_row_list = triple[..., feature_width : 2 * feature_width].reshape(
        window_count, tokens, head_count, head_size
    )
    values = triple[..., 2 * feature_width :].reshape(window_count, tokens, head_count, head_size)
    scores = (
        jnp.einsum("nqhd,nkhd->nhqk", queries, key_row_list, preferred_element_type=jnp.float32)
        * head_size ** (-0.5)
        + pos_bias[None]
    )
    row_max = jnp.max(scores, axis=-1, keepdims=True)
    weight_tensors = jnp.exp(scores - row_max)
    attention_weight_map = (
        weight_tensors / jnp.sum(weight_tensors, axis=-1, keepdims=True)
    ).astype(jnp.bfloat16)
    mixed = jnp.einsum(
        "nhqk,nkhd->nqhd", attention_weight_map, values, preferred_element_type=jnp.float32
    )
    return mixed.astype(jnp.bfloat16).reshape(window_count, tokens, feature_width)


def attention_sublayer(windows, norm_gain, in_weight, out_weight, pos_bias):
    normed = layer_norm_apply(windows, norm_gain)
    triple = jnp.dot(normed, in_weight, preferred_element_type=jnp.float32).astype(jnp.bfloat16)
    mixed = attend(triple, pos_bias)
    return (
        windows.astype(jnp.float32) + jnp.dot(mixed, out_weight, preferred_element_type=jnp.float32)
    ).astype(jnp.bfloat16)


def feed_forward(values, norm_gain, in_weight, out_weight):
    normed = layer_norm_apply(values, norm_gain)
    hidden = jax.nn.gelu(
        jnp.dot(normed, in_weight, preferred_element_type=jnp.float32), approximate=True
    ).astype(jnp.bfloat16)
    return (
        values.astype(jnp.float32) + jnp.dot(hidden, out_weight, preferred_element_type=jnp.float32)
    ).astype(jnp.bfloat16)


def to_blocks(field):
    row_count, col_count, feats = field.shape
    return (
        field.reshape(row_count // WIN, WIN, col_count // WIN, WIN, feats)
        .transpose(0, 2, 1, 3, 4)
        .reshape(-1, WIN * WIN, feats)
    )


def from_blocks(windows, row_count, col_count):
    feats = windows.shape[-1]
    return (
        windows.reshape(row_count // WIN, col_count // WIN, WIN, WIN, feats)
        .transpose(0, 2, 1, 3, 4)
        .reshape(row_count, col_count, feats)
    )


def axis_shape(length, devices):
    fold = max(1, WIN // devices)
    rest = length // max(devices, WIN)
    span = min(devices, WIN)
    return (fold, rest, span, devices // span)


def grid_layout(field):
    row_devices = lax.axis_size("row")
    col_devices = lax.axis_size("col")
    row_count, col_count, feats = field.shape
    row_fold, row_rest, row_span, row_hop = axis_shape(row_count, row_devices)
    col_fold, col_rest, col_span, col_hop = axis_shape(col_count, col_devices)
    ordered_layout = field.reshape(
        row_fold, row_devices, row_rest, col_fold, col_devices, col_rest, feats
    )
    flat = ordered_layout.transpose(1, 4, 0, 2, 3, 5, 6).reshape(
        row_devices * col_devices, row_fold, row_rest, col_fold, col_rest, feats
    )
    flat = lax.all_to_all(flat, ("row", "col"), split_axis=0, concat_axis=0, tiled=True)
    moved = flat.reshape(
        row_devices, col_devices, row_fold, row_rest, col_fold, col_rest, feats
    ).transpose(2, 0, 3, 4, 1, 5, 6)
    moved = moved.reshape(
        row_fold, row_span, row_hop, row_rest, col_fold, col_span, col_hop, col_rest, feats
    )
    return moved.transpose(2, 3, 6, 7, 1, 0, 5, 4, 8).reshape(-1, WIN * WIN, feats)


def spatial_layout(windows, row_count, col_count):
    row_devices = lax.axis_size("row")
    col_devices = lax.axis_size("col")
    feats = windows.shape[-1]
    row_fold, row_rest, row_span, row_hop = axis_shape(row_count, row_devices)
    col_fold, col_rest, col_span, col_hop = axis_shape(col_count, col_devices)
    gridded = windows.reshape(
        row_hop, row_rest, col_hop, col_rest, row_span, row_fold, col_span, col_fold, feats
    )
    ordered_layout = gridded.transpose(5, 4, 0, 1, 7, 6, 2, 3, 8).reshape(
        row_fold, row_devices, row_rest, col_fold, col_devices, col_rest, feats
    )
    flat = ordered_layout.transpose(1, 4, 0, 2, 3, 5, 6).reshape(
        row_devices * col_devices, row_fold, row_rest, col_fold, col_rest, feats
    )
    flat = lax.all_to_all(flat, ("row", "col"), split_axis=0, concat_axis=0, tiled=True)
    moved = flat.reshape(
        row_devices, col_devices, row_fold, row_rest, col_fold, col_rest, feats
    ).transpose(2, 0, 3, 4, 1, 5, 6)
    return moved.reshape(row_count, col_count, feats)


def squeeze_gate(pooled, squeeze_down, squeeze_up):
    reduced = jax.nn.silu(
        jnp.dot(pooled[None, :], squeeze_down.astype(jnp.float32), precision=lax.Precision.HIGHEST)
    )
    return jax.nn.sigmoid(
        jnp.dot(reduced, squeeze_up.astype(jnp.float32), precision=lax.Precision.HIGHEST)
    )[0]


def axis_sum_kernel(axis, count, x_ref, o_ref, slots, send_sem, recv_sem):
    me = lax.axis_index(axis)
    barrier = pltpu.get_barrier_semaphore()
    peers = [lax.rem(me + step, count) for step in range(1, count)]
    for peer in peers:
        pl.semaphore_signal(
            barrier, inc=1, device_id={axis: peer}, device_id_type=pl.DeviceIdType.MESH
        )
    pl.semaphore_wait(barrier, count - 1)
    copies = []
    for step, peer in enumerate(peers):
        copy = pltpu.make_async_remote_copy(
            src_ref=x_ref,
            dst_ref=slots.at[step],
            send_sem=send_sem.at[step],
            recv_sem=recv_sem.at[step],
            device_id={axis: peer},
            device_id_type=pl.DeviceIdType.MESH,
        )
        copy.start()
        copies.append(copy)
    for copy in copies:
        copy.wait()
    total = x_ref[...]
    for step in range(count - 1):
        total = total + slots[step]
    o_ref[...] = total


def axis_sum(values, axis, collective_id):
    count = lax.axis_size(axis)
    if count == 1:
        return values
    return pl.pallas_call(
        functools.partial(axis_sum_kernel, axis, count),
        out_shape=jax.ShapeDtypeStruct(values.shape, values.dtype),
        in_specs=[pl.BlockSpec(memory_space=pltpu.VMEM)],
        out_specs=pl.BlockSpec(memory_space=pltpu.VMEM),
        scratch_shapes=[
            pltpu.VMEM((count - 1,) + values.shape, values.dtype),
            pltpu.SemaphoreType.DMA((count - 1,)),
            pltpu.SemaphoreType.DMA((count - 1,)),
        ],
        compiler_params=pltpu.CompilerParams(
            collective_id=collective_id, has_side_effects=True, vmem_limit_bytes=4 * 1024 * 1024
        ),
        name="axis_sum_" + axis,
    )(values)


LANES = 128
GROUP = 256


def normed_rows(widened, gain):
    center = widened - jnp.mean(widened, axis=-1, keepdims=True)
    spread = jnp.mean(center * center, axis=-1, keepdims=True)
    return (center * lax.rsqrt(spread + 1e-05) * gain).astype(jnp.bfloat16)


def mixer_kernel(
    layout, head_size, x_ref, gain_ref, bias_ref, late_gain_ref, proj_hbm, out_hbm, up_hbm, down_hbm,
    o_ref, triple, heads, proj_ref, out_w_ref, up_ref, down_ref, sems,
):
    kind, across = layout
    rows_total, feats = x_ref.shape
    tokens = WIN * WIN
    window_count = rows_total // tokens
    slabs = feats // LANES
    per_slab = LANES // head_size
    moves = [
        pltpu.make_async_copy(src, dst, sems.at[k])
        for k, (src, dst) in enumerate(
            ((proj_hbm, proj_ref), (out_hbm, out_w_ref), (up_hbm, up_ref), (down_hbm, down_ref))
        )
    ]
    moves[0].start()
    moves[0].wait()
    for move in moves[1:]:
        move.start()
    chunk = 256

    def project(step, carry):
        rows = pl.ds(pl.multiple_of(step * chunk, chunk), chunk)
        normed = normed_rows(x_ref[rows, :].astype(jnp.float32), gain_ref[...])
        for part in range(3 * slabs // 2):
            product = jnp.dot(
                normed, proj_ref[:, part * GROUP : (part + 1) * GROUP],
                preferred_element_type=jnp.float32,
            ).astype(jnp.bfloat16).astype(jnp.float32)
            triple[2 * part, rows, :] = product[:, :LANES]
            triple[2 * part + 1, rows, :] = product[:, LANES:]
        return carry

    lax.fori_loop(0, rows_total // chunk, project, 0)

    def places(window):
        if kind == "strided":
            return [pl.ds(window, tokens, stride=across)]
        per_row = across // WIN
        base = (window // per_row) * (WIN * across) + (window % per_row) * WIN
        return [pl.ds(pl.multiple_of(base + r * across, WIN), WIN) for r in range(WIN)]

    lane = lax.broadcasted_iota(jnp.int32, (tokens, GROUP), 1)
    head_of = (lane % LANES) // head_size
    scale = head_size ** (-0.5)

    def one_window(window):
        spots = places(window)

        def fetch(slab):
            pieces = [triple[slab, spot, :] for spot in spots]
            whole = pieces[0] if len(pieces) == 1 else jnp.concatenate(pieces, axis=0)
            return whole

        empty = jnp.zeros((tokens, LANES), jnp.bfloat16)
        for group in range(slabs // 2):
            first, second = 2 * group, 2 * group + 1
            query_0 = fetch(first).astype(jnp.bfloat16)
            query_1 = fetch(second).astype(jnp.bfloat16)
            keys = jnp.concatenate([fetch(slabs + first), fetch(slabs + second)], axis=1)
            vals = jnp.concatenate([fetch(2 * slabs + first), fetch(2 * slabs + second)], axis=1)
            block_q = jnp.concatenate(
                [
                    jnp.concatenate([query_0, empty], axis=1),
                    jnp.concatenate([empty, query_1], axis=1),
                ],
                axis=0,
            )
            block_k = jnp.concatenate(
                [jnp.where(head_of == j, keys, 0.0).astype(jnp.bfloat16) for j in range(per_slab)],
                axis=0,
            )
            block_v = jnp.concatenate(
                [jnp.where(head_of == j, vals, 0.0).astype(jnp.bfloat16) for j in range(per_slab)],
                axis=0,
            )
            scores = lax.dot_general(
                block_k, block_q, (((1,), (1,)), ((), ())), preferred_element_type=jnp.float32
            )
            scores = (scores * scale + bias_ref[group]).reshape(per_slab, tokens, 2 * tokens)
            weights = jnp.exp(scores - jnp.max(scores, axis=1, keepdims=True))
            shares = weights * (1.0 / jnp.sum(weights, axis=1, keepdims=True))
            shares = shares.reshape(per_slab * tokens, 2 * tokens).astype(jnp.bfloat16)
            mixed = lax.dot_general(
                shares, block_v, (((0,), (0,)), ((), ())), preferred_element_type=jnp.float32
            )
            for slab, part in (
                (first, mixed[:tokens, :LANES]), (second, mixed[tokens:, LANES:])
            ):
                if len(spots) == 1:
                    heads[slab, spots[0], :] = part
                else:
                    for r, spot in enumerate(spots):
                        heads[slab, spot, :] = part[r * WIN : (r + 1) * WIN]

    def attend_pair(step, carry):
        one_window(2 * step)
        one_window(2 * step + 1)
        return carry

    lax.fori_loop(0, window_count // 2, attend_pair, 0)
    for move in moves[1:]:
        move.wait()
    hidden_width = up_ref.shape[1]
    tile = 512

    def feed(step, carry):
        rows = pl.ds(pl.multiple_of(step * chunk, chunk), chunk)
        mixed = jnp.concatenate([heads[s, rows, :] for s in range(slabs)], axis=1).astype(jnp.bfloat16)
        value = (
            x_ref[rows, :].astype(jnp.float32)
            + jnp.dot(mixed, out_w_ref[...], preferred_element_type=jnp.float32)
        ).astype(jnp.bfloat16).astype(jnp.float32)
        normed = normed_rows(value, late_gain_ref[...])
        for k in range(hidden_width // tile):
            part = slice(k * tile, (k + 1) * tile)
            hidden = jax.nn.gelu(
                jnp.dot(normed, up_ref[:, part], preferred_element_type=jnp.float32),
                approximate=True,
            ).astype(jnp.bfloat16)
            value = value + jnp.dot(hidden, down_ref[part, :], preferred_element_type=jnp.float32)
        o_ref[rows, :] = value.astype(jnp.bfloat16)
        return carry

    lax.fori_loop(0, rows_total // chunk, feed, 0)


def mixer(x, layout, gain, in_weight, out_weight, bias, late_gain, up, down, heads_count):
    rows, feats = x.shape
    vmem = pl.BlockSpec(memory_space=pltpu.VMEM)
    hbm = pl.BlockSpec(memory_space=pltpu.HBM)
    flops = 8 * rows * feats * (4 * feats + 2 * up.shape[1])
    return pl.pallas_call(
        functools.partial(mixer_kernel, layout, feats // heads_count),
        out_shape=jax.ShapeDtypeStruct((rows, feats), jnp.bfloat16),
        in_specs=[vmem] * 4 + [hbm] * 4,
        out_specs=vmem,
        scratch_shapes=[
            pltpu.VMEM((3 * feats // LANES, rows, LANES), jnp.float32),
            pltpu.VMEM((feats // LANES, rows, LANES), jnp.float32),
            pltpu.VMEM(in_weight.shape, jnp.bfloat16),
            pltpu.VMEM(out_weight.shape, jnp.bfloat16),
            pltpu.VMEM(up.shape, jnp.bfloat16),
            pltpu.VMEM(down.shape, jnp.bfloat16),
            pltpu.SemaphoreType.DMA((4,)),
        ],
        compiler_params=pltpu.CompilerParams(vmem_limit_bytes=60 * 1024 * 1024),
        cost_estimate=pl.CostEstimate(
            flops=flops, bytes_accessed=12 * 1024 * 1024, transcendentals=0
        ),
        name="mixer_" + layout[0],
    )(x, gain[None], bias, late_gain[None], in_weight, out_weight, up, down)


def key_major_bias(table, down, across):
    head_count, spots = table.shape
    relative = (down[None, :] - down[:, None] + WIN - 1) * (2 * WIN - 1) + (
        across[None, :] - across[:, None] + WIN - 1
    )
    tokens = WIN * WIN
    chosen = (jnp.arange(spots)[:, None] == jnp.asarray(relative.reshape(-1))[None, :]).astype(
        jnp.float32
    )
    spread = jnp.dot(table, chosen, precision=lax.Precision.HIGHEST)
    return (
        spread.reshape(head_count // 8, 2, 4, tokens, tokens)
        .transpose(0, 2, 3, 1, 4)
        .reshape(head_count // 8, 4 * tokens, 2 * tokens)
    )


def split_sublayers(conv_out, run_block, run_grid, block_table, grid_table):
    row_devices = lax.axis_size("row")
    col_devices = lax.axis_size("col")
    row_count, col_count, feats = conv_out.shape
    plain = np.arange(WIN * WIN)
    block_bias = key_major_bias(block_table, plain // WIN, plain % WIN)
    if row_devices > WIN or col_devices > WIN:
        section = run_block(conv_out.reshape(-1, feats), ("blocks", col_count), block_bias)
        windows = grid_layout(section.reshape(row_count, col_count, feats))
        count = windows.shape[0]
        bias = key_major_bias(grid_table, plain // WIN, plain % WIN)
        out = run_grid(windows.transpose(1, 0, 2).reshape(-1, feats), ("strided", count), bias)
        out = out.reshape(WIN * WIN, count, feats).transpose(1, 0, 2)
        return spatial_layout(out, row_count, col_count)
    devices = row_devices * col_devices
    row_fold, col_fold = WIN // row_devices, WIN // col_devices
    row_rest, col_rest = row_count // row_fold, col_count // col_fold
    parts = row_rest // WIN
    count = WIN * col_rest // devices
    pieces = col_rest // count
    order = np.arange(WIN * WIN).reshape(row_devices, col_devices, row_fold, col_fold)
    at = np.indices(order.shape).reshape(4, -1)
    grid_bias = key_major_bias(grid_table, at[0] * row_fold + at[2], at[1] * col_fold + at[3])
    strips = conv_out.reshape(row_fold, parts, WIN, col_count, feats)
    results = []
    for part in range(parts):
        section = run_block(
            strips[:, part].reshape(-1, feats), ("blocks", col_count), block_bias
        )
        sent = (
            section.reshape(row_fold, WIN, col_fold, pieces, count, feats)
            .transpose(1, 3, 0, 2, 4, 5)
            .reshape(devices, row_fold * col_fold * count, feats)
        )
        got = lax.all_to_all(sent, ("row", "col"), split_axis=0, concat_axis=0, tiled=True)
        out = run_grid(got.reshape(-1, feats), ("strided", count), grid_bias)
        back = lax.all_to_all(
            out.reshape(devices, -1, feats), ("row", "col"), split_axis=0, concat_axis=0, tiled=True
        )
        results.append(
            back.reshape(WIN, pieces, row_fold, col_fold, count, feats)
            .transpose(2, 0, 3, 1, 4, 5)
            .reshape(row_fold, WIN, col_count, feats)
        )
    return jnp.stack(results, axis=1).reshape(row_count, col_count, feats)


def device_of(flat, columns):
    return {"row": lax.div(flat, columns), "col": lax.rem(flat, columns)}


CORNERS = ((-1, -1), (-1, 1), (1, -1), (1, 1))


def split_parts(values):
    high = values.astype(jnp.bfloat16)
    rest = values - high.astype(jnp.float32)
    middle = rest.astype(jnp.bfloat16)
    low = (rest - middle.astype(jnp.float32)).astype(jnp.bfloat16)
    return high, middle, low


def exact_rows(values, weight):
    stacked = jnp.concatenate([p.astype(jnp.float32) for p in split_parts(values)], axis=0)
    product = jnp.dot(
        stacked.astype(jnp.bfloat16), weight[...], preferred_element_type=jnp.float32
    )
    return jnp.sum(product, axis=0, keepdims=True)


def block_kernel(
    shape, head_size, latent, scale_in, shift_in, taps_in, block_table, grid_table,
    gain_0, gain_1, gain_2, gain_3,
    h0, h1, h2, h3, w0, w1, w2, w3, w4, w5, w6, w7, o_ref,
    u0, u1, u2, u3, triple, heads, v0, v1, v2, v3, v4, v5, v6, v7,
    section, got, output, back, edges, halo, corner, conv_in, halo_in, expanded, deep_ref,
    sums, slots, excite_ref, padded, block_bias, grid_bias,
    weight_sem, send_sem, recv_sem, halo_send, halo_recv, sum_send, sum_recv,
):
    parts, pieces, rows_n, columns = shape
    devices = rows_n * columns
    row_count, col_count, feats = latent.shape
    width = u0.shape[1]
    slabs = feats // LANES
    per_slab = LANES // head_size
    tokens = WIN * WIN
    message = section.shape[1]
    folds = message // WIN
    chunk = 256
    batch = chunk // message
    halves = devices // batch
    part_rows = devices * message
    wide = col_count + PAD
    fold_rows = row_count // folds
    row_at, col_at = lax.axis_index("row"), lax.axis_index("col")
    me = row_at * columns + col_at
    mesh_ids = pl.DeviceIdType.MESH
    barrier = pltpu.get_barrier_semaphore()

    def greet(step, carry):
        pl.semaphore_signal(
            barrier, inc=1, device_id=device_of(lax.rem(me + step, devices), columns),
            device_id_type=mesh_ids,
        )
        return carry

    lax.fori_loop(1, devices, greet, 0)
    moves = [
        pltpu.make_async_copy(src, dst, weight_sem.at[k])
        for k, (src, dst) in enumerate(
            zip(
                (h0, h1, h2, h3, w0, w1, w2, w3, w4, w5, w6, w7),
                (u0, u1, u2, u3, v0, v1, v2, v3, v4, v5, v6, v7),
            )
        )
    ]
    for move in moves:
        move.start()

    near = {
        (down, side): jnp.logical_and(
            jnp.logical_and(row_at + down >= 0, row_at + down < rows_n),
            jnp.logical_and(col_at + side >= 0, col_at + side < columns),
        )
        for down in (-1, 0, 1)
        for side in (-1, 0, 1)
    }
    for side, block, inner in ((0, 0, 0), (1, col_count - message, message - 1)):
        for group in range(row_count // 8):
            cells = latent[8 * group : 8 * group + 8, block : block + message, :]
            edges[side, 8 * group : 8 * group + 8, :] = (
                cells.astype(jnp.float32)[:, inner, :].astype(jnp.bfloat16)
            )
    sides = ((-1, 0), (1, 0), (0, -1), (0, 1))
    for k, way in enumerate(sides):

        @pl.when(jnp.logical_not(near[way]))
        def _(k=k):
            halo[k] = jnp.zeros(halo.shape[1:], halo.dtype)

    for k, way in enumerate(CORNERS):

        @pl.when(jnp.logical_not(near[way]))
        def _(k=k):
            corner[k] = jnp.zeros(corner.shape[1:], corner.dtype)

    for group in range(row_count // 8):
        cells = latent[8 * group : 8 * group + 8].reshape(8 * col_count, feats)
        conv_in[8 * group * col_count : 8 * (group + 1) * col_count, :] = (
            cells.astype(jnp.float32) * scale_in[...] + shift_in[...]
        ).astype(jnp.bfloat16)
    pl.semaphore_wait(barrier, devices - 1)

    def outgoing(k):
        if k < 4:
            down, side = sides[k]
            src = (
                latent.at[0], latent.at[row_count - 1], edges.at[0], edges.at[1]
            )[k]
            dst = halo.at[k ^ 1]
        else:
            down, side = CORNERS[k - 4]
            line = 0 if down < 0 else row_count - 1
            start = 0 if side < 0 else col_count - message
            src = latent.at[line, pl.ds(start, message)]
            dst = corner.at[7 - k]
        return pltpu.make_async_remote_copy(
            src_ref=src, dst_ref=dst, send_sem=halo_send.at[k], recv_sem=halo_recv.at[k],
            device_id={"row": row_at + down, "col": col_at + side}, device_id_type=mesh_ids,
        )

    ways = sides + CORNERS
    for k, way in enumerate(ways):

        @pl.when(near[way])
        def _(k=k):
            outgoing(k).start()

    moves[0].wait()
    block = 256

    def expand(step, carry):
        lanes = pl.ds(pl.multiple_of(step * block, block), block)
        for group in range(row_count // 8):
            product = jnp.dot(
                conv_in[8 * group * col_count : 8 * (group + 1) * col_count, :], u0[:, lanes],
                preferred_element_type=jnp.float32,
            )
            value = jax.nn.gelu(product, approximate=True).astype(jnp.bfloat16).astype(jnp.float32)
            for r in range(8):
                start = (1 + 8 * group + r) * wide
                for half in range(block // LANES):
                    expanded[step * (block // LANES) + half, start : start + col_count, :] = value[
                        r * col_count : (r + 1) * col_count, half * LANES : (half + 1) * LANES
                    ]
        return carry

    lax.fori_loop(0, width // block, expand, 0)
    for k, way in enumerate(ways):
        opposite = (-way[0], -way[1])
        src_k = ways.index(opposite)

        @pl.when(near[way])
        def _(k=k, src_k=src_k):
            target = halo.at[k] if k < 4 else corner.at[k - 4]
            pltpu.make_async_copy(target, target, halo_recv.at[src_k]).wait()

    picked = [
        corner[k].astype(jnp.float32)[(message - 1 if side < 0 else 0) :][:1]
        for k, (_, side) in enumerate(CORNERS)
    ]
    picked = jnp.concatenate(picked + [jnp.zeros((message - 4, feats), jnp.float32)], axis=0)
    around = 2 * (row_count + col_count)
    for k, (start, size) in enumerate(
        (
            (0, col_count), (col_count, col_count), (2 * col_count, row_count),
            (2 * col_count + row_count, row_count),
        )
    ):
        halo_in[start : start + size, :] = (
            halo[k].astype(jnp.float32) * scale_in[...] + shift_in[...]
        ).astype(jnp.bfloat16)
    halo_in[around:, :] = (picked * scale_in[...] + shift_in[...]).astype(jnp.bfloat16)
    tall = row_count + 2

    def expand_halo(step, carry):
        lanes = pl.ds(pl.multiple_of(step * block, block), block)
        product = jnp.dot(halo_in[...], u0[:, lanes], preferred_element_type=jnp.float32)
        value = jax.nn.gelu(product, approximate=True).astype(jnp.bfloat16).astype(jnp.float32)
        up = jnp.where(near[(-1, 0)], value[:col_count], 0.0)
        low = jnp.where(near[(1, 0)], value[col_count : 2 * col_count], 0.0)
        left = jnp.where(near[(0, -1)], value[2 * col_count : 2 * col_count + row_count], 0.0)
        right = jnp.where(near[(0, 1)], value[2 * col_count + row_count : around], 0.0)
        for half in range(block // LANES):
            inner = slice(half * LANES, (half + 1) * LANES)
            outer = step * (block // LANES) + half
            last = (tall - 1) * wide
            expanded[outer, 0:col_count, :] = up[:, inner]
            expanded[outer, last : last + col_count, :] = low[:, inner]
            expanded[outer, pl.ds(wide + col_count, row_count, stride=wide), :] = right[:, inner]
            expanded[outer, pl.ds(2 * wide - 1, row_count, stride=wide), :] = left[:, inner]
            for k, way in enumerate(CORNERS):
                row = (0 if way[0] < 0 else last) + (wide - 1 if way[1] < 0 else col_count)
                expanded[outer, row : row + 1, :] = jnp.where(
                    near[way], value[around + k : around + k + 1, inner], 0.0
                )
        return carry

    lax.fori_loop(0, width // block, expand_halo, 0)

    def depth(step, carry):
        lanes = pl.ds(pl.multiple_of(step * LANES, LANES), LANES)
        taps = [taps_in[k : k + 1, lanes] for k in range(9)]

        def pair_of_rows(group, total):
            results = []
            for fold in range(folds):
                first = fold * fold_rows + 2 * group
                held = [
                    expanded[step, pl.ds(pl.multiple_of((first + k) * wide, 8), wide), :]
                    for k in range(4)
                ]
                for k in range(2):
                    sums_of = [
                        held[k] * taps[side]
                        + held[k + 1] * taps[3 + side]
                        + held[k + 2] * taps[6 + side]
                        for side in range(3)
                    ]
                    summed = (
                        pltpu.roll(sums_of[0], 1, 0) + sums_of[1] + pltpu.roll(sums_of[2], wide - 1, 0)
                    )[:col_count]
                    value = jax.nn.gelu(summed, approximate=True)
                    total = total + jnp.sum(value.reshape(col_count // 8, 8, LANES), axis=0)
                    results.append(value)
            part, down = lax.div(2 * group, WIN), lax.rem(2 * group, WIN)
            for k in range(2):
                for piece in range(pieces):
                    rows = slice(piece * WIN, (piece + 1) * WIN)
                    tile = jnp.concatenate(
                        [results[2 * fold + k][rows] for fold in range(folds)], axis=0
                    )
                    at = part * devices + piece * WIN + down + k
                    deep_ref[at, :, lanes] = tile.astype(jnp.bfloat16)
            return total

        sums[:, lanes] = lax.fori_loop(
            0, fold_rows // 2, pair_of_rows, jnp.zeros((8, LANES), jnp.float32)
        )
        return carry

    lax.fori_loop(0, width // LANES, depth, 0)
    for move in moves[1:4]:
        move.wait()
    slots[me] = exact_rows(sums[...], u1)

    def share(step, carry):
        pltpu.make_async_remote_copy(
            src_ref=slots.at[me], dst_ref=slots.at[me], send_sem=sum_send, recv_sem=sum_recv,
            device_id=device_of(lax.rem(me + step, devices), columns), device_id_type=mesh_ids,
        ).start()
        return carry

    lax.fori_loop(1, devices, share, 0)
    span = 2 * WIN
    spot = lax.broadcasted_iota(jnp.int32, (slabs * per_slab, span * span), 1)
    place = lax.broadcasted_iota(jnp.int32, (WIN, LANES), 1)
    for table, bias in ((block_table, block_bias), (grid_table, grid_bias)):
        padded[...] = jnp.zeros(padded.shape, jnp.float32)
        padded[:, : table.shape[1]] = table[...]
        flat = padded[...]
        spread = jnp.zeros(flat.shape, jnp.float32)
        for down in range(2 * WIN - 1):
            moved = flat if down == 0 else pltpu.roll(flat, down, 1)
            spread = jnp.where(spot // span == down, moved, spread)
        for head in range(slabs * per_slab // 2):
            group, j = head // per_slab, head % per_slab
            pair = [
                jnp.broadcast_to(spread[h : h + 1], (WIN, span * span))
                for h in (group * 2 * per_slab + j, group * 2 * per_slab + per_slab + j)
            ]
            for kr in range(WIN):
                shift = span * kr - (span * (WIN - 1) + WIN - 1)
                first, second = [
                    pltpu.roll(
                        pair[s], (shift + WIN * s) % (span * span), 1, stride=1, stride_axis=0
                    )[:, :LANES]
                    for s in range(2)
                ]
                start = j * tokens + kr * WIN
                bias[group, start : start + WIN, :] = jnp.where(place % span < WIN, first, second)
    arrivals = slots.at[pl.ds(0, devices - 1)]
    pltpu.make_async_copy(arrivals, arrivals, sum_recv).wait()
    pooled = jnp.sum(slots[...].reshape(devices, LANES), axis=0, keepdims=True) / (
        row_count * rows_n * col_count * columns
    )
    reduced = jax.nn.silu(pooled)
    spare = jnp.zeros((7, LANES), jnp.float32)
    excite_ref[...] = jax.nn.sigmoid(exact_rows(jnp.concatenate([reduced, spare], axis=0), u2))
    for move in moves[4:8]:
        move.wait()

    def project(values, rows, gain_ref, weight):
        normed = normed_rows(values.astype(jnp.float32), gain_ref[...])
        for part in range(3 * slabs // 2):
            product = jnp.dot(
                normed, weight[:, part * GROUP : (part + 1) * GROUP],
                preferred_element_type=jnp.float32,
            ).astype(jnp.bfloat16).astype(jnp.float32)
            triple[2 * part, rows, :] = product[:, :LANES]
            triple[2 * part + 1, rows, :] = product[:, LANES:]

    lane = lax.broadcasted_iota(jnp.int32, (tokens, GROUP), 1)
    head_of = (lane % LANES) // head_size
    scale = head_size ** (-0.5)

    def attend_window(spots, bias_ref):
        def fetch(slab):
            return [triple[slab, spot, :] for spot in spots]

        def whole(slab):
            return jnp.concatenate(fetch(slab), axis=0)

        empty = jnp.zeros((WIN, LANES), jnp.float32)
        for group in range(slabs // 2):
            first, second = 2 * group, 2 * group + 1
            block_q = jnp.concatenate(
                [
                    jnp.concatenate([p for q in fetch(first) for p in (q, empty)], axis=0),
                    jnp.concatenate([p for q in fetch(second) for p in (empty, q)], axis=0),
                ],
                axis=1,
            ).astype(jnp.bfloat16)
            keys = jnp.concatenate([whole(slabs + first), whole(slabs + second)], axis=1)
            vals = jnp.concatenate([whole(2 * slabs + first), whole(2 * slabs + second)], axis=1)
            block_k = jnp.concatenate(
                [jnp.where(head_of == j, keys, 0.0).astype(jnp.bfloat16) for j in range(per_slab)],
                axis=0,
            )
            block_v = jnp.concatenate(
                [jnp.where(head_of == j, vals, 0.0).astype(jnp.bfloat16) for j in range(per_slab)],
                axis=0,
            )
            scores = lax.dot_general(
                block_k, block_q, (((1,), (1,)), ((), ())), preferred_element_type=jnp.float32
            )
            scores = (scores * scale + bias_ref[group]).reshape(per_slab, tokens, 2 * tokens)
            weights = jnp.exp(scores - jnp.max(scores, axis=1, keepdims=True))
            shares = weights * (1.0 / jnp.sum(weights, axis=1, keepdims=True))
            shares = shares.reshape(per_slab * tokens, 2 * tokens).astype(jnp.bfloat16)
            mixed = lax.dot_general(
                shares, block_v, (((0,), (0,)), ((), ())), preferred_element_type=jnp.float32
            )
            for r, spot in enumerate(spots):
                start = 2 * r * WIN
                heads[first, spot, :] = mixed[start : start + WIN, :LANES]
                heads[second, spot, :] = mixed[start + WIN : start + 2 * WIN, LANES:]

    def feed(values, rows, gain_ref, out_w, up, down):
        mixed = jnp.concatenate([heads[s, rows, :] for s in range(slabs)], axis=1).astype(jnp.bfloat16)
        value = (
            values.astype(jnp.float32)
            + jnp.dot(mixed, out_w[...], preferred_element_type=jnp.float32)
        ).astype(jnp.bfloat16).astype(jnp.float32)
        normed = normed_rows(value, gain_ref[...])
        tile = 512
        for k in range(up.shape[1] // tile):
            part = slice(k * tile, (k + 1) * tile)
            hidden = jax.nn.gelu(
                jnp.dot(normed, up[:, part], preferred_element_type=jnp.float32),
                approximate=True,
            ).astype(jnp.bfloat16)
            value = value + jnp.dot(hidden, down[part, :], preferred_element_type=jnp.float32)
        return value.astype(jnp.bfloat16)

    def block_step(step, carry):
        part, half = lax.div(step, halves), lax.rem(step, halves)
        whole = pl.ds(0, chunk)
        across = batch // WIN
        own = {}
        for down in range(WIN):
            for fold in range(folds):
                line = latent[
                    fold * fold_rows + part * WIN + down,
                    pl.ds(pl.multiple_of(half * (across * WIN), across * WIN), across * WIN), :,
                ].astype(jnp.float32)
                for piece in range(across):
                    own[piece, down, fold] = line[piece * WIN : (piece + 1) * WIN]
        own = jnp.concatenate([own[key] for key in sorted(own)], axis=0)
        for k in range(width // block):
            lanes = slice(k * block, (k + 1) * block)
            gated = (
                deep_ref[pl.ds(step * batch, batch), :, lanes].reshape(chunk, block).astype(jnp.float32)
                * excite_ref[:, lanes]
            ).astype(jnp.bfloat16)
            own = own + jnp.dot(gated, u3[lanes, :], preferred_element_type=jnp.float32)
        value = own.astype(jnp.bfloat16)
        conv_in[0:chunk, :] = value
        project(value, whole, gain_0, v0)

        def attend_pair(piece, inner):
            for fold in range(folds):
                start = piece * (WIN * message) + fold * WIN
                attend_window(
                    [pl.ds(pl.multiple_of(start + r * message, WIN), WIN) for r in range(WIN)],
                    block_bias,
                )
            return inner

        lax.fori_loop(0, across, attend_pair, 0)
        done = feed(conv_in[0:chunk, :], whole, gain_1, v1, v2, v3)
        section[pl.ds(step * batch, batch)] = done.reshape(batch, message, feats)

        def send(i, inner):
            at = lax.rem(i + me, batch)
            target = lax.rem(at, WIN) * pieces + half * across + lax.div(at, WIN)
            src, dst = section.at[step * batch + at], got.at[part * devices + me]

            @pl.when(target != me)
            def _():
                pltpu.make_async_remote_copy(
                    src_ref=src, dst_ref=dst, send_sem=send_sem.at[0, part],
                    recv_sem=recv_sem.at[0, part], device_id=device_of(target, columns),
                    device_id_type=mesh_ids,
                ).start()

            @pl.when(target == me)
            def _():
                pltpu.make_async_copy(src, dst, recv_sem.at[0, part]).start()

            return inner

        lax.fori_loop(0, batch, send, 0)
        return carry

    lax.fori_loop(0, parts * halves, block_step, 0)
    for move in moves[8:]:
        move.wait()
    slot = lax.rem(me, pieces) * WIN + lax.div(me, pieces)

    def arrived(buffer, kind, part):
        mail = buffer.at[pl.ds(part * devices, devices)]
        pltpu.make_async_copy(mail, mail, recv_sem.at[kind, part]).wait()

    def grid_step(part, carry):
        arrived(got, 0, part)

        def rows_of(half):
            return got[pl.ds(part * devices + half * batch, batch)].reshape(chunk, feats)

        for half in range(halves):
            project(rows_of(half), pl.ds(half * chunk, chunk), gain_2, v4)

        def attend_pair(pair, inner):
            for k in range(2):
                attend_window(
                    [
                        pl.ds(r * columns * message + fold * WIN + 2 * pair + k, columns, stride=message)
                        for r in range(rows_n)
                        for fold in range(folds)
                    ],
                    grid_bias,
                )
            return inner

        lax.fori_loop(0, part_rows // tokens // 2, attend_pair, 0)

        def feed_half(half, inner):
            rows = pl.ds(pl.multiple_of(half * chunk, chunk), chunk)
            done = feed(rows_of(half), rows, gain_3, v5, v6, v7)
            output[pl.ds(part * devices + half * batch, batch)] = done.reshape(batch, message, feats)

            def send(i, inner_2):
                target = half * batch + lax.rem(i + me, batch)
                src, dst = output.at[part * devices + target], back.at[part * devices + slot]

                @pl.when(target != me)
                def _():
                    pltpu.make_async_remote_copy(
                        src_ref=src, dst_ref=dst, send_sem=send_sem.at[1, part],
                        recv_sem=recv_sem.at[1, part], device_id=device_of(target, columns),
                        device_id_type=mesh_ids,
                    ).start()

                @pl.when(target == me)
                def _():
                    pltpu.make_async_copy(src, dst, recv_sem.at[1, part]).start()

                return inner_2

            lax.fori_loop(0, batch, send, 0)
            return inner

        lax.fori_loop(0, halves, feed_half, 0)
        return carry

    lax.fori_loop(0, parts, grid_step, 0)

    def finish(part, carry):
        arrived(back, 1, part)

        def put(down, inner):
            tiles = [
                back[part * devices + piece * WIN + down].astype(jnp.float32)
                for piece in range(pieces)
            ]
            for fold in range(folds):
                line = jnp.concatenate([t[fold * WIN : (fold + 1) * WIN] for t in tiles], axis=0)
                o_ref[fold * fold_rows + part * WIN + down] = line.astype(jnp.bfloat16)
            return inner

        return lax.fori_loop(0, WIN, put, carry)

    lax.fori_loop(0, parts, finish, 0)
    for kind, buffer in ((0, section), (1, output)):
        for part in range(parts):
            sent = buffer.at[pl.ds(part * devices, devices - 1)]
            pltpu.make_async_copy(sent, sent, send_sem.at[kind, part]).wait()
    pltpu.make_async_copy(arrivals, arrivals, sum_send).wait()
    for k, way in enumerate(ways):

        @pl.when(near[way])
        def _(k=k):
            target = halo.at[k] if k < 4 else corner.at[k - 4]
            pltpu.make_async_copy(target, target, halo_send.at[k]).wait()


def whole_block(latent, scale, shift, taps, tables, gains, front, weights):
    row_count, col_count, feats = latent.shape
    rows_n, columns = lax.axis_size("row"), lax.axis_size("col")
    devices = rows_n * columns
    parts, pieces = row_count // (2 * WIN), col_count // WIN
    heads_n = tables[0].shape[0]
    rows = row_count * col_count
    width = front[0].shape[1]
    message = rows // (parts * devices)
    around = 2 * (row_count + col_count) + message
    vmem = pl.BlockSpec(memory_space=pltpu.VMEM)
    hbm = pl.BlockSpec(memory_space=pltpu.HBM)
    half_type = jnp.bfloat16
    mail = pltpu.VMEM((parts * devices, message, feats), half_type)
    bias = pltpu.VMEM((heads_n // 8, 4 * WIN * WIN, 2 * WIN * WIN), jnp.float32)
    dma = pltpu.SemaphoreType.DMA
    return pl.pallas_call(
        functools.partial(block_kernel, (parts, pieces, rows_n, columns), feats // heads_n),
        out_shape=jax.ShapeDtypeStruct(latent.shape, half_type),
        in_specs=[vmem] * 10 + [hbm] * 12,
        out_specs=vmem,
        scratch_shapes=[pltpu.VMEM(w.shape, half_type) for w in front]
        + [
            pltpu.VMEM((3 * feats // LANES, rows // parts, LANES), jnp.float32),
            pltpu.VMEM((feats // LANES, rows // parts, LANES), jnp.float32),
        ]
        + [pltpu.VMEM(w.shape, half_type) for w in weights]
        + [
            mail, mail, mail, mail,
            pltpu.VMEM((2, row_count, feats), half_type),
            pltpu.VMEM((4, row_count, feats), half_type),
            pltpu.VMEM((4, message, feats), half_type),
            pltpu.VMEM((rows, feats), half_type),
            pltpu.VMEM((around, feats), half_type),
            pltpu.VMEM(
                (width // LANES, (row_count + 2) * (col_count + PAD), LANES), jnp.float32
            ),
            pltpu.VMEM((parts * devices, message, width), half_type),
            pltpu.VMEM((8, width), jnp.float32),
            pltpu.VMEM((devices, 1, LANES), jnp.float32),
            pltpu.VMEM((1, width), jnp.float32),
            pltpu.VMEM((heads_n, 4 * WIN * WIN), jnp.float32),
            bias, bias,
            dma((12,)), dma((2, parts)), dma((2, parts)), dma((8,)), dma((8,)), dma, dma,
        ],
        compiler_params=pltpu.CompilerParams(
            collective_id=3, has_side_effects=True, vmem_limit_bytes=60 * 1024 * 1024
        ),
        name="whole_block",
    )(
        latent, scale[None], shift[None], taps, *tables, *[g[None] for g in gains], *front, *weights
    )


def compact(row_count, col_count):
    row_devices, col_devices = lax.axis_size("row"), lax.axis_size("col")
    return (
        2 * row_devices == WIN and col_devices == WIN
        and row_count % (2 * WIN) == 0 and col_count == WIN * row_devices
        and row_count == col_count
    )


def conv_kernel(
    row_count, col_count, flags, ext_ref, scale_ref, shift_ref, expand_ref, taps_ref,
    o_ref, sums_ref, conv_in, expanded,
):
    wide = col_count + PAD
    tall = row_count + 2
    width = expand_ref.shape[1]
    block = expanded.shape[-1]
    bounds = [8 * k for k in range(row_count // 8)] + [tall]
    for low, high in zip(bounds[:-1], bounds[1:]):
        rows = slice(low * wide, high * wide)
        conv_in[rows, :] = (
            ext_ref[rows, :].astype(jnp.float32) * scale_ref[...] + shift_ref[...]
        ).astype(jnp.bfloat16)
    spot = lax.broadcasted_iota(jnp.int32, (1, PAD, block), 1)
    side = jnp.where(spot == 0, flags[3], jnp.where(spot == PAD - 1, flags[2], 0.0))

    def channels(step, carry):
        lanes = pl.ds(pl.multiple_of(step * block, block), block)
        for low, high in zip(bounds[:-1], bounds[1:]):
            product = jnp.dot(
                conv_in[low * wide : high * wide, :], expand_ref[:, lanes],
                preferred_element_type=jnp.float32,
            )
            value = jax.nn.gelu(product, approximate=True).astype(jnp.bfloat16)
            expanded[low:high] = value.astype(jnp.float32).reshape(high - low, wide, block)
        expanded[0] = expanded[0] * flags[0]
        expanded[tall - 1] = expanded[tall - 1] * flags[1]
        expanded[:, col_count:, :] = expanded[:, col_count:, :] * side
        for half in range(block // LANES):
            inner = slice(half * LANES, (half + 1) * LANES)
            outer = pl.ds(pl.multiple_of(step * block + half * LANES, LANES), LANES)
            taps = [taps_ref[k : k + 1, outer] for k in range(9)]

            def rows_of(group, total):
                base = group * 4
                held = [expanded[base + k, :, inner] for k in range(6)]
                for k in range(4):
                    parts = [
                        held[k] * taps[side_step]
                        + held[k + 1] * taps[3 + side_step]
                        + held[k + 2] * taps[6 + side_step]
                        for side_step in range(3)
                    ]
                    summed = (
                        pltpu.roll(parts[0], 1, 0) + parts[1] + pltpu.roll(parts[2], wide - 1, 0)
                    )[:col_count]
                    deep = jax.nn.gelu(summed, approximate=True)
                    total = total + jnp.sum(deep.reshape(col_count // 8, 8, LANES), axis=0)
                    at = pl.ds(pl.multiple_of((base + k) * col_count, col_count), col_count)
                    o_ref[at, outer] = deep.astype(o_ref.dtype)
                return total

            total = lax.fori_loop(0, row_count // 4, rows_of, jnp.zeros((8, LANES), jnp.float32))
            sums_ref[:, outer] = jnp.sum(total, axis=0, keepdims=True)
        return carry

    lax.fori_loop(0, width // block, channels, 0)


def depthwise_stage(latent, conv_scale, conv_shift, expand_weight, depth_kernel):
    row_count, col_count, feats = latent.shape
    width = expand_weight.shape[1]
    row_at, col_at = lax.axis_index("row"), lax.axis_index("col")
    flags = jnp.stack(
        [row_at > 0, row_at < lax.axis_size("row") - 1, col_at > 0, col_at < lax.axis_size("col") - 1]
    ).astype(jnp.float32)
    tall = extended(latent, (("row", 0),), 1)
    count = lax.axis_size("col")
    ahead = [(i, i + 1) for i in range(count - 1)]
    left = lax.ppermute(tall[:, col_count - 1 :], "col", ahead)
    right = lax.ppermute(tall[:, :1], "col", [(b, a) for a, b in ahead])
    blank = jnp.zeros((row_count + 2, PAD - 2, feats), latent.dtype)
    ext = jnp.concatenate([tall, right, blank, left], axis=1).reshape(-1, feats)
    vmem = pl.BlockSpec(memory_space=pltpu.VMEM)
    block = 256
    return pl.pallas_call(
        functools.partial(conv_kernel, row_count, col_count),
        out_shape=(
            jax.ShapeDtypeStruct((row_count * col_count, width), jnp.bfloat16),
            jax.ShapeDtypeStruct((1, width), jnp.float32),
        ),
        in_specs=[pl.BlockSpec(memory_space=pltpu.SMEM)] + [vmem] * 5,
        out_specs=(vmem, vmem),
        scratch_shapes=[
            pltpu.VMEM(ext.shape, jnp.bfloat16),
            pltpu.VMEM((row_count + 2, col_count + PAD, block), jnp.float32),
        ],
        compiler_params=pltpu.CompilerParams(vmem_limit_bytes=20 * 1024 * 1024),
        name="conv_stage",
    )(flags, ext, conv_scale[None], conv_shift[None], expand_weight, depth_kernel)


def per_device(
    latent,
    conv_scale,
    conv_shift,
    expand_weight,
    depth_kernel,
    squeeze_down,
    squeeze_up,
    project_weight,
    block_gain,
    block_projection,
    block_output,
    block_table,
    first_gain,
    first_expand,
    first_reduce,
    grid_gain,
    grid_projection,
    grid_output,
    grid_table,
    second_gain,
    second_expand,
    second_reduce,
):
    row_devices = lax.axis_size("row")
    col_devices = lax.axis_size("col")
    row_count, col_count, channels = latent.shape
    if compact(row_count, col_count) and squeeze_up.shape[0] == LANES:
        return whole_block(
            latent, conv_scale, conv_shift, depth_kernel, (block_table, grid_table),
            (block_gain, first_gain, grid_gain, second_gain),
            (expand_weight, squeeze_down, squeeze_up, project_weight),
            (block_projection, block_output, first_expand, first_reduce,
             grid_projection, grid_output, second_expand, second_reduce),
        )
    depthwise, local_sums = depthwise_stage(
        latent, conv_scale, conv_shift, expand_weight, depth_kernel
    )
    local_sums = local_sums.reshape(-1, LANES)
    channel_sums = axis_sum(axis_sum(local_sums, "row", 1), "col", 2).reshape(-1)
    pooled = channel_sums / (row_count * row_devices * col_count * col_devices)
    excite = squeeze_gate(pooled, squeeze_down, squeeze_up)
    gated = (depthwise.astype(jnp.float32) * excite).astype(jnp.bfloat16)
    conv_out = (
        latent.reshape(-1, channels).astype(jnp.float32)
        + jnp.dot(gated, project_weight, preferred_element_type=jnp.float32)
    ).astype(jnp.bfloat16).reshape(row_count, col_count, channels)

    def run_block(cells, layout, bias):
        return mixer(
            cells, layout, block_gain, block_projection, block_output, bias, first_gain,
            first_expand, first_reduce, block_table.shape[0],
        )

    def run_grid(cells, layout, bias):
        return mixer(
            cells, layout, grid_gain, grid_projection, grid_output, bias, second_gain,
            second_expand, second_reduce, grid_table.shape[0],
        )

    return split_sublayers(conv_out, run_block, run_grid, block_table, grid_table)


def solution(mesh):
    placed = (
        P("row", "col", None),
        P(),
        P(),
        P(),
        P(),
        P(),
        P(),
        P(),
        P(),
        P(),
        P(),
        P(),
        P(),
        P(),
        P(),
        P(),
        P(),
        P(),
        P(),
        P(),
        P(),
        P(),
    )
    return jax.shard_map(
        per_device, mesh=mesh, in_specs=placed, out_specs=P("row", "col", None), check_vma=False
    )
```

```python
import functools

import jax
import jax.numpy as jnp
import numpy as np
from jax import lax
from jax.experimental import pallas as pl
from jax.experimental.pallas import tpu as pltpu
from jax.sharding import PartitionSpec as P

WIN = 8
PAD = 8
QUAD = 4
LOG2E = 1.4426950408889634


def extended(cells, sides, width):
    for axis, dim in sides:
        count = lax.axis_size(axis)
        ends = count - 1
        head = lax.slice_in_dim(cells, 0, width, axis=dim)
        tail = lax.slice_in_dim(cells, cells.shape[dim] - width, cells.shape[dim], axis=dim)
        cells = jnp.concatenate(
            [
                lax.ppermute(tail, axis, [(i, (i + 1) % count) for i in range(ends)]),
                cells,
                lax.ppermute(head, axis, [((i + 1) % count, i) for i in range(ends)]),
            ],
            axis=dim,
        )
    return cells


def layer_norm_apply(values, norm_gain):
    widened = values.astype(jnp.float32)
    center = widened - jnp.mean(widened, axis=-1, keepdims=True)
    spread = jnp.mean(center * center, axis=-1, keepdims=True)
    return (center * lax.rsqrt(spread + 1e-05) * norm_gain).astype(jnp.bfloat16)


def position_bias(offset_bias_lookup):
    spots = offset_bias_lookup.shape[1]
    position = jnp.arange(WIN * WIN)
    down_pos = position // WIN
    across = position % WIN
    relative = (down_pos[:, None] - down_pos[None, :] + WIN - 1) * (2 * WIN - 1) + (
        across[:, None] - across[None, :] + WIN - 1
    )
    indicator_matrix = (relative[:, :, None] == jnp.arange(spots)[None, None, :]).astype(
        jnp.float32
    )
    return jnp.einsum(
        "bp,rjp->brj", offset_bias_lookup, indicator_matrix, precision=lax.Precision.HIGHEST
    )


def attend(triple, pos_bias):
    window_count, tokens, three_width = triple.shape
    feature_width = three_width // 3
    head_count = pos_bias.shape[0]
    head_size = feature_width // head_count
    queries = triple[..., :feature_width].reshape(window_count, tokens, head_count, head_size)
    key_row_list = triple[..., feature_width : 2 * feature_width].reshape(
        window_count, tokens, head_count, head_size
    )
    values = triple[..., 2 * feature_width :].reshape(window_count, tokens, head_count, head_size)
    scores = (
        jnp.einsum("nqhd,nkhd->nhqk", queries, key_row_list, preferred_element_type=jnp.float32)
        * head_size ** (-0.5)
        + pos_bias[None]
    )
    row_max = jnp.max(scores, axis=-1, keepdims=True)
    weight_tensors = jnp.exp(scores - row_max)
    attention_weight_map = (
        weight_tensors / jnp.sum(weight_tensors, axis=-1, keepdims=True)
    ).astype(jnp.bfloat16)
    mixed = jnp.einsum(
        "nhqk,nkhd->nqhd", attention_weight_map, values, preferred_element_type=jnp.float32
    )
    return mixed.astype(jnp.bfloat16).reshape(window_count, tokens, feature_width)


def attention_sublayer(windows, norm_gain, in_weight, out_weight, pos_bias):
    normed = layer_norm_apply(windows, norm_gain)
    triple = jnp.dot(normed, in_weight, preferred_element_type=jnp.float32).astype(jnp.bfloat16)
    mixed = attend(triple, pos_bias)
    return (
        windows.astype(jnp.float32) + jnp.dot(mixed, out_weight, preferred_element_type=jnp.float32)
    ).astype(jnp.bfloat16)


def feed_forward(values, norm_gain, in_weight, out_weight):
    normed = layer_norm_apply(values, norm_gain)
    hidden = jax.nn.gelu(
        jnp.dot(normed, in_weight, preferred_element_type=jnp.float32), approximate=True
    ).astype(jnp.bfloat16)
    return (
        values.astype(jnp.float32) + jnp.dot(hidden, out_weight, preferred_element_type=jnp.float32)
    ).astype(jnp.bfloat16)


def to_blocks(field):
    row_count, col_count, feats = field.shape
    return (
        field.reshape(row_count // WIN, WIN, col_count // WIN, WIN, feats)
        .transpose(0, 2, 1, 3, 4)
        .reshape(-1, WIN * WIN, feats)
    )


def from_blocks(windows, row_count, col_count):
    feats = windows.shape[-1]
    return (
        windows.reshape(row_count // WIN, col_count // WIN, WIN, WIN, feats)
        .transpose(0, 2, 1, 3, 4)
        .reshape(row_count, col_count, feats)
    )


def axis_shape(length, devices):
    fold = max(1, WIN // devices)
    rest = length // max(devices, WIN)
    span = min(devices, WIN)
    return (fold, rest, span, devices // span)


def grid_layout(field):
    row_devices = lax.axis_size("row")
    col_devices = lax.axis_size("col")
    row_count, col_count, feats = field.shape
    row_fold, row_rest, row_span, row_hop = axis_shape(row_count, row_devices)
    col_fold, col_rest, col_span, col_hop = axis_shape(col_count, col_devices)
    ordered_layout = field.reshape(
        row_fold, row_devices, row_rest, col_fold, col_devices, col_rest, feats
    )
    flat = ordered_layout.transpose(1, 4, 0, 2, 3, 5, 6).reshape(
        row_devices * col_devices, row_fold, row_rest, col_fold, col_rest, feats
    )
    flat = lax.all_to_all(flat, ("row", "col"), split_axis=0, concat_axis=0, tiled=True)
    moved = flat.reshape(
        row_devices, col_devices, row_fold, row_rest, col_fold, col_rest, feats
    ).transpose(2, 0, 3, 4, 1, 5, 6)
    moved = moved.reshape(
        row_fold, row_span, row_hop, row_rest, col_fold, col_span, col_hop, col_rest, feats
    )
    return moved.transpose(2, 3, 6, 7, 1, 0, 5, 4, 8).reshape(-1, WIN * WIN, feats)


def spatial_layout(windows, row_count, col_count):
    row_devices = lax.axis_size("row")
    col_devices = lax.axis_size("col")
    feats = windows.shape[-1]
    row_fold, row_rest, row_span, row_hop = axis_shape(row_count, row_devices)
    col_fold, col_rest, col_span, col_hop = axis_shape(col_count, col_devices)
    gridded = windows.reshape(
        row_hop, row_rest, col_hop, col_rest, row_span, row_fold, col_span, col_fold, feats
    )
    ordered_layout = gridded.transpose(5, 4, 0, 1, 7, 6, 2, 3, 8).reshape(
        row_fold, row_devices, row_rest, col_fold, col_devices, col_rest, feats
    )
    flat = ordered_layout.transpose(1, 4, 0, 2, 3, 5, 6).reshape(
        row_devices * col_devices, row_fold, row_rest, col_fold, col_rest, feats
    )
    flat = lax.all_to_all(flat, ("row", "col"), split_axis=0, concat_axis=0, tiled=True)
    moved = flat.reshape(
        row_devices, col_devices, row_fold, row_rest, col_fold, col_rest, feats
    ).transpose(2, 0, 3, 4, 1, 5, 6)
    return moved.reshape(row_count, col_count, feats)


def squeeze_gate(pooled, squeeze_down, squeeze_up):
    reduced = jax.nn.silu(
        jnp.dot(pooled[None, :], squeeze_down.astype(jnp.float32), precision=lax.Precision.HIGHEST)
    )
    return jax.nn.sigmoid(
        jnp.dot(reduced, squeeze_up.astype(jnp.float32), precision=lax.Precision.HIGHEST)
    )[0]


def axis_sum_kernel(axis, count, x_ref, o_ref, slots, send_sem, recv_sem):
    me = lax.axis_index(axis)
    barrier = pltpu.get_barrier_semaphore()
    peers = [lax.rem(me + step, count) for step in range(1, count)]
    for peer in peers:
        pl.semaphore_signal(
            barrier, inc=1, device_id={axis: peer}, device_id_type=pl.DeviceIdType.MESH
        )
    pl.semaphore_wait(barrier, count - 1)
    copies = []
    for step, peer in enumerate(peers):
        copy = pltpu.make_async_remote_copy(
            src_ref=x_ref,
            dst_ref=slots.at[step],
            send_sem=send_sem.at[step],
            recv_sem=recv_sem.at[step],
            device_id={axis: peer},
            device_id_type=pl.DeviceIdType.MESH,
        )
        copy.start()
        copies.append(copy)
    for copy in copies:
        copy.wait()
    total = x_ref[...]
    for step in range(count - 1):
        total = total + slots[step]
    o_ref[...] = total


def axis_sum(values, axis, collective_id):
    count = lax.axis_size(axis)
    if count == 1:
        return values
    return pl.pallas_call(
        functools.partial(axis_sum_kernel, axis, count),
        out_shape=jax.ShapeDtypeStruct(values.shape, values.dtype),
        in_specs=[pl.BlockSpec(memory_space=pltpu.VMEM)],
        out_specs=pl.BlockSpec(memory_space=pltpu.VMEM),
        scratch_shapes=[
            pltpu.VMEM((count - 1,) + values.shape, values.dtype),
            pltpu.SemaphoreType.DMA((count - 1,)),
            pltpu.SemaphoreType.DMA((count - 1,)),
        ],
        compiler_params=pltpu.CompilerParams(
            collective_id=collective_id, has_side_effects=True, vmem_limit_bytes=4 * 1024 * 1024
        ),
        name="axis_sum_" + axis,
    )(values)


LANES = 128
GROUP = 256


def normed_rows(widened, gain):
    center = widened - jnp.mean(widened, axis=-1, keepdims=True)
    spread = jnp.mean(center * center, axis=-1, keepdims=True)
    return (center * lax.rsqrt(spread + 1e-05) * gain).astype(jnp.bfloat16)


def mixer_kernel(
    layout, head_size, x_ref, gain_ref, bias_ref, late_gain_ref, proj_hbm, out_hbm, up_hbm, down_hbm,
    o_ref, triple, heads, proj_ref, out_w_ref, up_ref, down_ref, sems,
):
    kind, across = layout
    rows_total, feats = x_ref.shape
    tokens = WIN * WIN
    window_count = rows_total // tokens
    slabs = feats // LANES
    per_slab = LANES // head_size
    moves = [
        pltpu.make_async_copy(src, dst, sems.at[k])
        for k, (src, dst) in enumerate(
            ((proj_hbm, proj_ref), (out_hbm, out_w_ref), (up_hbm, up_ref), (down_hbm, down_ref))
        )
    ]
    moves[0].start()
    moves[0].wait()
    for move in moves[1:]:
        move.start()
    chunk = 256

    def project(step, carry):
        rows = pl.ds(pl.multiple_of(step * chunk, chunk), chunk)
        normed = normed_rows(x_ref[rows, :].astype(jnp.float32), gain_ref[...])
        for part in range(3 * slabs // 2):
            product = jnp.dot(
                normed, proj_ref[:, part * GROUP : (part + 1) * GROUP],
                preferred_element_type=jnp.float32,
            ).astype(jnp.bfloat16).astype(jnp.float32)
            triple[2 * part, rows, :] = product[:, :LANES]
            triple[2 * part + 1, rows, :] = product[:, LANES:]
        return carry

    lax.fori_loop(0, rows_total // chunk, project, 0)

    def places(window):
        if kind == "strided":
            return [pl.ds(window, tokens, stride=across)]
        per_row = across // WIN
        base = (window // per_row) * (WIN * across) + (window % per_row) * WIN
        return [pl.ds(pl.multiple_of(base + r * across, WIN), WIN) for r in range(WIN)]

    lane = lax.broadcasted_iota(jnp.int32, (tokens, GROUP), 1)
    head_of = (lane % LANES) // head_size
    scale = head_size ** (-0.5)

    def one_window(window):
        spots = places(window)

        def fetch(slab):
            pieces = [triple[slab, spot, :] for spot in spots]
            whole = pieces[0] if len(pieces) == 1 else jnp.concatenate(pieces, axis=0)
            return whole

        empty = jnp.zeros((tokens, LANES), jnp.bfloat16)
        for group in range(slabs // 2):
            first, second = 2 * group, 2 * group + 1
            query_0 = fetch(first).astype(jnp.bfloat16)
            query_1 = fetch(second).astype(jnp.bfloat16)
            keys = jnp.concatenate([fetch(slabs + first), fetch(slabs + second)], axis=1)
            vals = jnp.concatenate([fetch(2 * slabs + first), fetch(2 * slabs + second)], axis=1)
            block_q = jnp.concatenate(
                [
                    jnp.concatenate([query_0, empty], axis=1),
                    jnp.concatenate([empty, query_1], axis=1),
                ],
                axis=0,
            )
            block_k = jnp.concatenate(
                [jnp.where(head_of == j, keys, 0.0).astype(jnp.bfloat16) for j in range(per_slab)],
                axis=0,
            )
            block_v = jnp.concatenate(
                [jnp.where(head_of == j, vals, 0.0).astype(jnp.bfloat16) for j in range(per_slab)],
                axis=0,
            )
            scores = lax.dot_general(
                block_k, block_q, (((1,), (1,)), ((), ())), preferred_element_type=jnp.float32
            )
            scores = (scores * scale + bias_ref[group]).reshape(per_slab, tokens, 2 * tokens)
            weights = jnp.exp(scores - jnp.max(scores, axis=1, keepdims=True))
            shares = weights * (1.0 / jnp.sum(weights, axis=1, keepdims=True))
            shares = shares.reshape(per_slab * tokens, 2 * tokens).astype(jnp.bfloat16)
            mixed = lax.dot_general(
                shares, block_v, (((0,), (0,)), ((), ())), preferred_element_type=jnp.float32
            )
            for slab, part in (
                (first, mixed[:tokens, :LANES]), (second, mixed[tokens:, LANES:])
            ):
                if len(spots) == 1:
                    heads[slab, spots[0], :] = part
                else:
                    for r, spot in enumerate(spots):
                        heads[slab, spot, :] = part[r * WIN : (r + 1) * WIN]

    def attend_pair(step, carry):
        one_window(2 * step)
        one_window(2 * step + 1)
        return carry

    lax.fori_loop(0, window_count // 2, attend_pair, 0)
    for move in moves[1:]:
        move.wait()
    hidden_width = up_ref.shape[1]
    tile = 512

    def feed(step, carry):
        rows = pl.ds(pl.multiple_of(step * chunk, chunk), chunk)
        mixed = jnp.concatenate([heads[s, rows, :] for s in range(slabs)], axis=1).astype(jnp.bfloat16)
        value = (
            x_ref[rows, :].astype(jnp.float32)
            + jnp.dot(mixed, out_w_ref[...], preferred_element_type=jnp.float32)
        ).astype(jnp.bfloat16).astype(jnp.float32)
        normed = normed_rows(value, late_gain_ref[...])
        for k in range(hidden_width // tile):
            part = slice(k * tile, (k + 1) * tile)
            hidden = jax.nn.gelu(
                jnp.dot(normed, up_ref[:, part], preferred_element_type=jnp.float32),
                approximate=True,
            ).astype(jnp.bfloat16)
            value = value + jnp.dot(hidden, down_ref[part, :], preferred_element_type=jnp.float32)
        o_ref[rows, :] = value.astype(jnp.bfloat16)
        return carry

    lax.fori_loop(0, rows_total // chunk, feed, 0)


def mixer(x, layout, gain, in_weight, out_weight, bias, late_gain, up, down, heads_count):
    rows, feats = x.shape
    vmem = pl.BlockSpec(memory_space=pltpu.VMEM)
    hbm = pl.BlockSpec(memory_space=pltpu.HBM)
    flops = 8 * rows * feats * (4 * feats + 2 * up.shape[1])
    return pl.pallas_call(
        functools.partial(mixer_kernel, layout, feats // heads_count),
        out_shape=jax.ShapeDtypeStruct((rows, feats), jnp.bfloat16),
        in_specs=[vmem] * 4 + [hbm] * 4,
        out_specs=vmem,
        scratch_shapes=[
            pltpu.VMEM((3 * feats // LANES, rows, LANES), jnp.float32),
            pltpu.VMEM((feats // LANES, rows, LANES), jnp.float32),
            pltpu.VMEM(in_weight.shape, jnp.bfloat16),
            pltpu.VMEM(out_weight.shape, jnp.bfloat16),
            pltpu.VMEM(up.shape, jnp.bfloat16),
            pltpu.VMEM(down.shape, jnp.bfloat16),
            pltpu.SemaphoreType.DMA((4,)),
        ],
        compiler_params=pltpu.CompilerParams(vmem_limit_bytes=60 * 1024 * 1024),
        cost_estimate=pl.CostEstimate(
            flops=flops, bytes_accessed=12 * 1024 * 1024, transcendentals=0
        ),
        name="mixer_" + layout[0],
    )(x, gain[None], bias, late_gain[None], in_weight, out_weight, up, down)


def key_major_bias(table, down, across):
    head_count, spots = table.shape
    relative = (down[None, :] - down[:, None] + WIN - 1) * (2 * WIN - 1) + (
        across[None, :] - across[:, None] + WIN - 1
    )
    tokens = WIN * WIN
    chosen = (jnp.arange(spots)[:, None] == jnp.asarray(relative.reshape(-1))[None, :]).astype(
        jnp.float32
    )
    spread = jnp.dot(table, chosen, precision=lax.Precision.HIGHEST)
    return (
        spread.reshape(head_count // 8, 2, 4, tokens, tokens)
        .transpose(0, 2, 3, 1, 4)
        .reshape(head_count // 8, 4 * tokens, 2 * tokens)
    )


def split_sublayers(conv_out, run_block, run_grid, block_table, grid_table):
    row_devices = lax.axis_size("row")
    col_devices = lax.axis_size("col")
    row_count, col_count, feats = conv_out.shape
    plain = np.arange(WIN * WIN)
    block_bias = key_major_bias(block_table, plain // WIN, plain % WIN)
    if row_devices > WIN or col_devices > WIN:
        section = run_block(conv_out.reshape(-1, feats), ("blocks", col_count), block_bias)
        windows = grid_layout(section.reshape(row_count, col_count, feats))
        count = windows.shape[0]
        bias = key_major_bias(grid_table, plain // WIN, plain % WIN)
        out = run_grid(windows.transpose(1, 0, 2).reshape(-1, feats), ("strided", count), bias)
        out = out.reshape(WIN * WIN, count, feats).transpose(1, 0, 2)
        return spatial_layout(out, row_count, col_count)
    devices = row_devices * col_devices
    row_fold, col_fold = WIN // row_devices, WIN // col_devices
    row_rest, col_rest = row_count // row_fold, col_count // col_fold
    parts = row_rest // WIN
    count = WIN * col_rest // devices
    pieces = col_rest // count
    order = np.arange(WIN * WIN).reshape(row_devices, col_devices, row_fold, col_fold)
    at = np.indices(order.shape).reshape(4, -1)
    grid_bias = key_major_bias(grid_table, at[0] * row_fold + at[2], at[1] * col_fold + at[3])
    strips = conv_out.reshape(row_fold, parts, WIN, col_count, feats)
    results = []
    for part in range(parts):
        section = run_block(
            strips[:, part].reshape(-1, feats), ("blocks", col_count), block_bias
        )
        sent = (
            section.reshape(row_fold, WIN, col_fold, pieces, count, feats)
            .transpose(1, 3, 0, 2, 4, 5)
            .reshape(devices, row_fold * col_fold * count, feats)
        )
        got = lax.all_to_all(sent, ("row", "col"), split_axis=0, concat_axis=0, tiled=True)
        out = run_grid(got.reshape(-1, feats), ("strided", count), grid_bias)
        back = lax.all_to_all(
            out.reshape(devices, -1, feats), ("row", "col"), split_axis=0, concat_axis=0, tiled=True
        )
        results.append(
            back.reshape(WIN, pieces, row_fold, col_fold, count, feats)
            .transpose(2, 0, 3, 1, 4, 5)
            .reshape(row_fold, WIN, col_count, feats)
        )
    return jnp.stack(results, axis=1).reshape(row_count, col_count, feats)


def device_of(flat, columns):
    return {"row": lax.div(flat, columns), "col": lax.rem(flat, columns)}


CORNERS = ((-1, -1), (-1, 1), (1, -1), (1, 1))


def split_parts(values):
    high = values.astype(jnp.bfloat16)
    rest = values - high.astype(jnp.float32)
    middle = rest.astype(jnp.bfloat16)
    low = (rest - middle.astype(jnp.float32)).astype(jnp.bfloat16)
    return high, middle, low


def exact_rows(values, weight):
    stacked = jnp.concatenate([p.astype(jnp.float32) for p in split_parts(values)], axis=0)
    product = jnp.dot(
        stacked.astype(jnp.bfloat16), weight[...], preferred_element_type=jnp.float32
    )
    return jnp.sum(product, axis=0, keepdims=True)


def twice_gelu(x):
    inner = x * (0.7978845608028654 + (0.7978845608028654 * 0.044715) * (x * x))
    return x + x * jnp.tanh(inner)


def block_kernel(
    shape, head_size, latent, scale_in, shift_in, taps_in, block_table, grid_table,
    gain_0, gain_1, gain_2, gain_3,
    h0, h1, h2, h3, w0, w1, w2, w3, w4, w5, w6, w7, o_ref,
    u0, u1, u2, u3, triple, heads, v0, v1, v2, v3, v4, v5, v6, v7,
    section, got, output, back, edges, halo, corner, conv_in, halo_in, expanded, deep_ref,
    sums, slots, excite_ref, padded, block_bias, grid_bias, score_ref, share_ref,
    weight_sem, send_sem, recv_sem, halo_send, halo_recv, sum_send, sum_recv,
):
    parts, pieces, rows_n, columns = shape
    devices = rows_n * columns
    row_count, col_count, feats = latent.shape
    width = u0.shape[1]
    slabs = feats // LANES
    per_slab = LANES // head_size
    tokens = WIN * WIN
    message = section.shape[1]
    folds = message // WIN
    chunk = 256
    batch = chunk // message
    halves = devices // batch
    part_rows = devices * message
    wide = col_count + PAD
    fold_rows = row_count // folds
    row_at, col_at = lax.axis_index("row"), lax.axis_index("col")
    me = row_at * columns + col_at
    mesh_ids = pl.DeviceIdType.MESH
    barrier = pltpu.get_barrier_semaphore()

    def greet(step, carry):
        pl.semaphore_signal(
            barrier, inc=1, device_id=device_of(lax.rem(me + step, devices), columns),
            device_id_type=mesh_ids,
        )
        return carry

    lax.fori_loop(1, devices, greet, 0)
    moves = [
        pltpu.make_async_copy(src, dst, weight_sem.at[k])
        for k, (src, dst) in enumerate(
            zip(
                (h0, h1, h2, h3, w0, w1, w2, w3, w4, w5, w6, w7),
                (u0, u1, u2, u3, v0, v1, v2, v3, v4, v5, v6, v7),
            )
        )
    ]
    for move in moves:
        move.start()

    near = {
        (down, side): jnp.logical_and(
            jnp.logical_and(row_at + down >= 0, row_at + down < rows_n),
            jnp.logical_and(col_at + side >= 0, col_at + side < columns),
        )
        for down in (-1, 0, 1)
        for side in (-1, 0, 1)
    }
    for side, block, inner in ((0, 0, 0), (1, col_count - message, message - 1)):
        for group in range(row_count // 8):
            cells = latent[8 * group : 8 * group + 8, block : block + message, :]
            edges[side, 8 * group : 8 * group + 8, :] = (
                cells.astype(jnp.float32)[:, inner, :].astype(jnp.bfloat16)
            )
    sides = ((-1, 0), (1, 0), (0, -1), (0, 1))
    for k, way in enumerate(sides):

        @pl.when(jnp.logical_not(near[way]))
        def _(k=k):
            halo[k] = jnp.zeros(halo.shape[1:], halo.dtype)

    for k, way in enumerate(CORNERS):

        @pl.when(jnp.logical_not(near[way]))
        def _(k=k):
            corner[k] = jnp.zeros(corner.shape[1:], corner.dtype)

    for group in range(row_count // 8):
        cells = latent[8 * group : 8 * group + 8].reshape(8 * col_count, feats)
        conv_in[8 * group * col_count : 8 * (group + 1) * col_count, :] = (
            cells.astype(jnp.float32) * scale_in[...] + shift_in[...]
        ).astype(jnp.bfloat16)
    pl.semaphore_wait(barrier, devices - 1)

    def outgoing(k):
        if k < 4:
            down, side = sides[k]
            src = (
                latent.at[0], latent.at[row_count - 1], edges.at[0], edges.at[1]
            )[k]
            dst = halo.at[k ^ 1]
        else:
            down, side = CORNERS[k - 4]
            line = 0 if down < 0 else row_count - 1
            start = 0 if side < 0 else col_count - message
            src = latent.at[line, pl.ds(start, message)]
            dst = corner.at[7 - k]
        return pltpu.make_async_remote_copy(
            src_ref=src, dst_ref=dst, send_sem=halo_send.at[k], recv_sem=halo_recv.at[k],
            device_id={"row": row_at + down, "col": col_at + side}, device_id_type=mesh_ids,
        )

    ways = sides + CORNERS
    for k, way in enumerate(ways):

        @pl.when(near[way])
        def _(k=k):
            outgoing(k).start()

    moves[0].wait()
    block = 256

    def expand(step, carry):
        lanes = pl.ds(pl.multiple_of(step * block, block), block)
        for group in range(row_count // 8):
            product = jnp.dot(
                conv_in[8 * group * col_count : 8 * (group + 1) * col_count, :], u0[:, lanes],
                preferred_element_type=jnp.float32,
            )
            value = twice_gelu(product).astype(jnp.bfloat16).astype(jnp.float32)
            for r in range(8):
                start = PAD + (1 + 8 * group + r) * wide
                for half in range(block // LANES):
                    expanded[step * (block // LANES) + half, start : start + col_count, :] = value[
                        r * col_count : (r + 1) * col_count, half * LANES : (half + 1) * LANES
                    ]
        return carry

    lax.fori_loop(0, width // block, expand, 0)
    for k, way in enumerate(ways):
        opposite = (-way[0], -way[1])
        src_k = ways.index(opposite)

        @pl.when(near[way])
        def _(k=k, src_k=src_k):
            target = halo.at[k] if k < 4 else corner.at[k - 4]
            pltpu.make_async_copy(target, target, halo_recv.at[src_k]).wait()

    picked = [
        corner[k].astype(jnp.float32)[(message - 1 if side < 0 else 0) :][:1]
        for k, (_, side) in enumerate(CORNERS)
    ]
    picked = jnp.concatenate(picked + [jnp.zeros((message - 4, feats), jnp.float32)], axis=0)
    around = 2 * (row_count + col_count)
    for k, (start, size) in enumerate(
        (
            (0, col_count), (col_count, col_count), (2 * col_count, row_count),
            (2 * col_count + row_count, row_count),
        )
    ):
        halo_in[start : start + size, :] = (
            halo[k].astype(jnp.float32) * scale_in[...] + shift_in[...]
        ).astype(jnp.bfloat16)
    halo_in[around:, :] = (picked * scale_in[...] + shift_in[...]).astype(jnp.bfloat16)
    tall = row_count + 2

    def expand_halo(step, carry):
        lanes = pl.ds(pl.multiple_of(step * block, block), block)
        product = jnp.dot(halo_in[...], u0[:, lanes], preferred_element_type=jnp.float32)
        value = twice_gelu(product).astype(jnp.bfloat16).astype(jnp.float32)
        up = jnp.where(near[(-1, 0)], value[:col_count], 0.0)
        low = jnp.where(near[(1, 0)], value[col_count : 2 * col_count], 0.0)
        left = jnp.where(near[(0, -1)], value[2 * col_count : 2 * col_count + row_count], 0.0)
        right = jnp.where(near[(0, 1)], value[2 * col_count + row_count : around], 0.0)
        for half in range(block // LANES):
            inner = slice(half * LANES, (half + 1) * LANES)
            outer = step * (block // LANES) + half
            last = PAD + (tall - 1) * wide
            expanded[outer, PAD : PAD + col_count, :] = up[:, inner]
            expanded[outer, last : last + col_count, :] = low[:, inner]
            expanded[outer, pl.ds(PAD + wide + col_count, row_count, stride=wide), :] = right[:, inner]
            expanded[outer, pl.ds(PAD + wide - 1, row_count, stride=wide), :] = left[:, inner]
            for k, way in enumerate(CORNERS):
                row = (PAD if way[0] < 0 else last) + (-1 if way[1] < 0 else col_count)
                expanded[outer, row : row + 1, :] = jnp.where(
                    near[way], value[around + k : around + k + 1, inner], 0.0
                )
        return carry

    lax.fori_loop(0, width // block, expand_halo, 0)

    def depth(step, carry):
        lanes = pl.ds(pl.multiple_of(step * LANES, LANES), LANES)
        taps = [0.5 * taps_in[k : k + 1, lanes] for k in range(9)]

        def pair_of_rows(group, total):
            results = []
            for fold in range(folds):
                first = fold * fold_rows + 2 * group
                base = pl.multiple_of(first * wide, 8)
                held = [
                    [
                        expanded[step, pl.ds(base + (PAD + k * wide + side), col_count), :]
                        for side in (-1, 0, 1)
                    ]
                    for k in range(4)
                ]
                for k in range(2):
                    summed = sum(
                        held[k + down][side] * taps[3 * down + side]
                        for down in range(3)
                        for side in range(3)
                    )
                    value = twice_gelu(summed)
                    total = total + jnp.sum(value.reshape(col_count // 8, 8, LANES), axis=0)
                    results.append(value)
            part, down = lax.div(2 * group, WIN), lax.rem(2 * group, WIN)
            for k in range(2):
                for piece in range(pieces):
                    rows = slice(piece * WIN, (piece + 1) * WIN)
                    tile = jnp.concatenate(
                        [results[2 * fold + k][rows] for fold in range(folds)], axis=0
                    )
                    at = part * devices + piece * WIN + down + k
                    deep_ref[at, :, lanes] = tile.astype(jnp.bfloat16)
            return total

        sums[:, lanes] = lax.fori_loop(
            0, fold_rows // 2, pair_of_rows, jnp.zeros((8, LANES), jnp.float32)
        )
        return carry

    lax.fori_loop(0, width // LANES, depth, 0)
    for move in moves[1:4]:
        move.wait()
    slots[me] = exact_rows(0.5 * sums[...], u1)

    def share(step, carry):
        pltpu.make_async_remote_copy(
            src_ref=slots.at[me], dst_ref=slots.at[me], send_sem=sum_send, recv_sem=sum_recv,
            device_id=device_of(lax.rem(me + step, devices), columns), device_id_type=mesh_ids,
        ).start()
        return carry

    lax.fori_loop(1, devices, share, 0)
    span = 2 * WIN
    spot = lax.broadcasted_iota(jnp.int32, (slabs * per_slab, span * span), 1)
    place = lax.broadcasted_iota(jnp.int32, (WIN, LANES), 1)
    for table, bias in ((block_table, block_bias), (grid_table, grid_bias)):
        padded[...] = jnp.zeros(padded.shape, jnp.float32)
        padded[:, : table.shape[1]] = table[...] * LOG2E
        flat = padded[...]
        spread = jnp.zeros(flat.shape, jnp.float32)
        for down in range(2 * WIN - 1):
            moved = flat if down == 0 else pltpu.roll(flat, down, 1)
            spread = jnp.where(spot // span == down, moved, spread)
        for head in range(slabs * per_slab // 2):
            group, j = head // per_slab, head % per_slab
            pair = [
                jnp.broadcast_to(spread[h : h + 1], (WIN, span * span))
                for h in (group * 2 * per_slab + j, group * 2 * per_slab + per_slab + j)
            ]
            for kr in range(WIN):
                shift = span * kr - (span * (WIN - 1) + WIN - 1)
                first, second = [
                    pltpu.roll(
                        pair[s], (shift + WIN * s) % (span * span), 1, stride=1, stride_axis=0
                    )[:, :LANES]
                    for s in range(2)
                ]
                start = j * tokens + kr * WIN
                bias[group, start : start + WIN, :] = jnp.where(place % span < WIN, first, second)
    arrivals = slots.at[pl.ds(0, devices - 1)]
    pltpu.make_async_copy(arrivals, arrivals, sum_recv).wait()
    pooled = jnp.sum(slots[...].reshape(devices, LANES), axis=0, keepdims=True) / (
        row_count * rows_n * col_count * columns
    )
    reduced = jax.nn.silu(pooled)
    spare = jnp.zeros((7, LANES), jnp.float32)
    excite_ref[...] = 0.5 * jax.nn.sigmoid(exact_rows(jnp.concatenate([reduced, spare], axis=0), u2))
    for move in moves[4:8]:
        move.wait()

    def project(values, rows, gain_ref, weight):
        normed = normed_rows(values.astype(jnp.float32), gain_ref[...])
        for part in range(3 * slabs // 2):
            product = jnp.dot(
                normed, weight[:, part * GROUP : (part + 1) * GROUP],
                preferred_element_type=jnp.float32,
            ).astype(jnp.bfloat16).astype(jnp.float32)
            triple[2 * part, rows, :] = product[:, :LANES]
            triple[2 * part + 1, rows, :] = product[:, LANES:]

    lane = lax.broadcasted_iota(jnp.int32, (tokens, GROUP), 1)
    masks = [
        jnp.where((lane % LANES) // head_size == j, 1.0, 0.0).astype(jnp.bfloat16)
        for j in range(per_slab)
    ]
    scale = head_size ** (-0.5) * LOG2E

    def attend_windows(windows, bias_ref):
        def spread(spots, slab, group):
            joined = jnp.concatenate(
                [
                    jnp.concatenate([triple[slab + 2 * group + k, spot, :] for spot in spots], axis=0)
                    for k in range(2)
                ],
                axis=1,
            ).astype(jnp.bfloat16)
            return jnp.concatenate([joined * mask for mask in masks], axis=0)

        empty = jnp.zeros((WIN, LANES), jnp.float32)
        chains = [(n, g) for n in range(len(windows)) for g in range(slabs // 2)]
        for at, (n, group) in enumerate(chains):
            spots = windows[n]
            left, right = [
                [triple[2 * group + k, spot, :] for spot in spots] for k in range(2)
            ]
            block_q = jnp.concatenate(
                [
                    jnp.concatenate([p for q in left for p in (q, empty)], axis=0),
                    jnp.concatenate([p for q in right for p in (empty, q)], axis=0),
                ],
                axis=1,
            ).astype(jnp.bfloat16)
            score_ref[at] = lax.dot_general(
                spread(spots, slabs, group), block_q, (((1,), (1,)), ((), ())),
                preferred_element_type=jnp.float32,
            )
        for at, (n, group) in enumerate(chains):
            scores = (score_ref[at] * scale + bias_ref[group]).reshape(
                per_slab, tokens, 2 * tokens
            )
            weights = jnp.exp2(scores - jnp.max(scores, axis=1, keepdims=True))
            shares = weights * (1.0 / jnp.sum(weights, axis=1, keepdims=True))
            share_ref[at] = shares.reshape(per_slab * tokens, 2 * tokens).astype(jnp.bfloat16)
        for at, (n, group) in enumerate(chains):
            mixed = lax.dot_general(
                share_ref[at], spread(windows[n], 2 * slabs, group), (((0,), (0,)), ((), ())),
                preferred_element_type=jnp.float32,
            )
            for r, spot in enumerate(windows[n]):
                start = 2 * r * WIN
                heads[2 * group, spot, :] = mixed[start : start + WIN, :LANES]
                heads[2 * group + 1, spot, :] = mixed[start + WIN : start + 2 * WIN, LANES:]

    def feed(values, rows, gain_ref, out_w, up, down):
        mixed = jnp.concatenate([heads[s, rows, :] for s in range(slabs)], axis=1).astype(jnp.bfloat16)
        value = (
            values.astype(jnp.float32)
            + jnp.dot(mixed, out_w[...], preferred_element_type=jnp.float32)
        ).astype(jnp.bfloat16).astype(jnp.float32)
        normed = normed_rows(value, gain_ref[...])
        tile = 512
        total = None
        for k in range(up.shape[1] // tile):
            part = slice(k * tile, (k + 1) * tile)
            hidden = twice_gelu(
                jnp.dot(normed, up[:, part], preferred_element_type=jnp.float32)
            ).astype(jnp.bfloat16)
            product = jnp.dot(hidden, down[part, :], preferred_element_type=jnp.float32)
            total = product if total is None else total + product
        value = value + 0.5 * total
        return value.astype(jnp.bfloat16)

    def block_step(step, carry):
        part, half = lax.div(step, halves), lax.rem(step, halves)
        whole = pl.ds(0, chunk)
        across = batch // WIN
        own = {}
        for down in range(WIN):
            for fold in range(folds):
                line = latent[
                    fold * fold_rows + part * WIN + down,
                    pl.ds(pl.multiple_of(half * (across * WIN), across * WIN), across * WIN), :,
                ].astype(jnp.float32)
                for piece in range(across):
                    own[piece, down, fold] = line[piece * WIN : (piece + 1) * WIN]
        own = jnp.concatenate([own[key] for key in sorted(own)], axis=0)
        for k in range(width // block):
            lanes = slice(k * block, (k + 1) * block)
            gated = (
                deep_ref[pl.ds(step * batch, batch), :, lanes].reshape(chunk, block).astype(jnp.float32)
                * excite_ref[:, lanes]
            ).astype(jnp.bfloat16)
            own = own + jnp.dot(gated, u3[lanes, :], preferred_element_type=jnp.float32)
        value = own.astype(jnp.bfloat16)
        conv_in[0:chunk, :] = value
        project(value, whole, gain_0, v0)

        attend_windows(
            [
                [pl.ds(piece * (WIN * message) + fold * WIN + r * message, WIN) for r in range(WIN)]
                for piece in range(across)
                for fold in range(folds)
            ],
            block_bias,
        )
        done = feed(conv_in[0:chunk, :], whole, gain_1, v1, v2, v3)
        section[pl.ds(step * batch, batch)] = done.reshape(batch, message, feats)

        def send(i, inner):
            at = lax.rem(i + me, batch)
            target = lax.rem(at, WIN) * pieces + half * across + lax.div(at, WIN)
            src, dst = section.at[step * batch + at], got.at[part * devices + me]

            @pl.when(target != me)
            def _():
                pltpu.make_async_remote_copy(
                    src_ref=src, dst_ref=dst, send_sem=send_sem.at[0, part],
                    recv_sem=recv_sem.at[0, part], device_id=device_of(target, columns),
                    device_id_type=mesh_ids,
                ).start()

            @pl.when(target == me)
            def _():
                pltpu.make_async_copy(src, dst, recv_sem.at[0, part]).start()

            return inner

        lax.fori_loop(0, batch, send, 0)
        return carry

    lax.fori_loop(0, parts * halves, block_step, 0)
    for move in moves[8:]:
        move.wait()
    slot = lax.rem(me, pieces) * WIN + lax.div(me, pieces)

    def arrived(buffer, kind, part):
        mail = buffer.at[pl.ds(part * devices, devices)]
        pltpu.make_async_copy(mail, mail, recv_sem.at[kind, part]).wait()

    def grid_step(part, carry):
        arrived(got, 0, part)

        def rows_of(half):
            return got[pl.ds(part * devices + half * batch, batch)].reshape(chunk, feats)

        for half in range(halves):
            project(rows_of(half), pl.ds(half * chunk, chunk), gain_2, v4)

        def attend_some(step, inner):
            attend_windows(
                [
                    [
                        pl.ds(r * columns * message + fold * WIN + QUAD * step + k, columns, stride=message)
                        for r in range(rows_n)
                        for fold in range(folds)
                    ]
                    for k in range(QUAD)
                ],
                grid_bias,
            )
            return inner

        lax.fori_loop(0, part_rows // tokens // QUAD, attend_some, 0)

        def feed_half(half, inner):
            rows = pl.ds(pl.multiple_of(half * chunk, chunk), chunk)
            done = feed(rows_of(half), rows, gain_3, v5, v6, v7)
            output[pl.ds(part * devices + half * batch, batch)] = done.reshape(batch, message, feats)

            def send(i, inner_2):
                target = half * batch + lax.rem(i + me, batch)
                src, dst = output.at[part * devices + target], back.at[part * devices + slot]

                @pl.when(target != me)
                def _():
                    pltpu.make_async_remote_copy(
                        src_ref=src, dst_ref=dst, send_sem=send_sem.at[1, part],
                        recv_sem=recv_sem.at[1, part], device_id=device_of(target, columns),
                        device_id_type=mesh_ids,
                    ).start()

                @pl.when(target == me)
                def _():
                    pltpu.make_async_copy(src, dst, recv_sem.at[1, part]).start()

                return inner_2

            lax.fori_loop(0, batch, send, 0)
            return inner

        lax.fori_loop(0, halves, feed_half, 0)
        return carry

    lax.fori_loop(0, parts, grid_step, 0)

    def finish(part, carry):
        arrived(back, 1, part)

        def put(down, inner):
            tiles = [
                back[part * devices + piece * WIN + down].astype(jnp.float32)
                for piece in range(pieces)
            ]
            for fold in range(folds):
                line = jnp.concatenate([t[fold * WIN : (fold + 1) * WIN] for t in tiles], axis=0)
                start = (fold * fold_rows + part * WIN + down) * col_count
                o_ref[pl.ds(pl.multiple_of(start, col_count), col_count), :] = line.astype(jnp.bfloat16)
            return inner

        return lax.fori_loop(0, WIN, put, carry)

    lax.fori_loop(0, parts, finish, 0)
    for kind, buffer in ((0, section), (1, output)):
        for part in range(parts):
            sent = buffer.at[pl.ds(part * devices, devices - 1)]
            pltpu.make_async_copy(sent, sent, send_sem.at[kind, part]).wait()
    pltpu.make_async_copy(arrivals, arrivals, sum_send).wait()
    for k, way in enumerate(ways):

        @pl.when(near[way])
        def _(k=k):
            target = halo.at[k] if k < 4 else corner.at[k - 4]
            pltpu.make_async_copy(target, target, halo_send.at[k]).wait()


def whole_block(latent, scale, shift, taps, tables, gains, front, weights):
    row_count, col_count, feats = latent.shape
    rows_n, columns = lax.axis_size("row"), lax.axis_size("col")
    devices = rows_n * columns
    parts, pieces = row_count // (2 * WIN), col_count // WIN
    heads_n = tables[0].shape[0]
    rows = row_count * col_count
    width = front[0].shape[1]
    message = rows // (parts * devices)
    around = 2 * (row_count + col_count) + message
    vmem = pl.BlockSpec(memory_space=pltpu.VMEM)
    hbm = pl.BlockSpec(memory_space=pltpu.HBM)
    half_type = jnp.bfloat16
    mail = pltpu.VMEM((parts * devices, message, feats), half_type)
    bias = pltpu.VMEM((heads_n // 8, 4 * WIN * WIN, 2 * WIN * WIN), jnp.float32)
    dma = pltpu.SemaphoreType.DMA
    return pl.pallas_call(
        functools.partial(block_kernel, (parts, pieces, rows_n, columns), feats // heads_n),
        out_shape=jax.ShapeDtypeStruct((rows, feats), half_type),
        in_specs=[vmem] * 10 + [hbm] * 12,
        out_specs=vmem,
        scratch_shapes=[pltpu.VMEM(w.shape, half_type) for w in front]
        + [
            pltpu.VMEM((3 * feats // LANES, rows // parts, LANES), jnp.float32),
            pltpu.VMEM((feats // LANES, rows // parts, LANES), jnp.float32),
        ]
        + [pltpu.VMEM(w.shape, half_type) for w in weights]
        + [
            mail, mail, mail, mail,
            pltpu.VMEM((2, row_count, feats), half_type),
            pltpu.VMEM((4, row_count, feats), half_type),
            pltpu.VMEM((4, message, feats), half_type),
            pltpu.VMEM((rows, feats), half_type),
            pltpu.VMEM((around, feats), half_type),
            pltpu.VMEM(
                (width // LANES, PAD + (row_count + 2) * (col_count + PAD), LANES), jnp.float32
            ),
            pltpu.VMEM((parts * devices, message, width), half_type),
            pltpu.VMEM((8, width), jnp.float32),
            pltpu.VMEM((devices, 1, LANES), jnp.float32),
            pltpu.VMEM((1, width), jnp.float32),
            pltpu.VMEM((heads_n, 4 * WIN * WIN), jnp.float32),
            bias, bias,
            pltpu.VMEM((QUAD * heads_n // 8, 4 * WIN * WIN, 2 * WIN * WIN), jnp.float32),
            pltpu.VMEM((QUAD * heads_n // 8, 4 * WIN * WIN, 2 * WIN * WIN), half_type),
            dma((12,)), dma((2, parts)), dma((2, parts)), dma((8,)), dma((8,)), dma, dma,
        ],
        compiler_params=pltpu.CompilerParams(
            collective_id=3, has_side_effects=True, vmem_limit_bytes=60 * 1024 * 1024
        ),
        name="whole_block",
    )(
        latent, scale[None], shift[None], taps, *tables, *[g[None] for g in gains], *front, *weights
    ).reshape(latent.shape)


def compact(row_count, col_count):
    row_devices, col_devices = lax.axis_size("row"), lax.axis_size("col")
    return (
        2 * row_devices == WIN and col_devices == WIN
        and row_count % (2 * WIN) == 0 and col_count == WIN * row_devices
        and row_count == col_count
    )


def conv_kernel(
    row_count, col_count, flags, ext_ref, scale_ref, shift_ref, expand_ref, taps_ref,
    o_ref, sums_ref, conv_in, expanded,
):
    wide = col_count + PAD
    tall = row_count + 2
    width = expand_ref.shape[1]
    block = expanded.shape[-1]
    bounds = [8 * k for k in range(row_count // 8)] + [tall]
    for low, high in zip(bounds[:-1], bounds[1:]):
        rows = slice(low * wide, high * wide)
        conv_in[rows, :] = (
            ext_ref[rows, :].astype(jnp.float32) * scale_ref[...] + shift_ref[...]
        ).astype(jnp.bfloat16)
    spot = lax.broadcasted_iota(jnp.int32, (1, PAD, block), 1)
    side = jnp.where(spot == 0, flags[3], jnp.where(spot == PAD - 1, flags[2], 0.0))

    def channels(step, carry):
        lanes = pl.ds(pl.multiple_of(step * block, block), block)
        for low, high in zip(bounds[:-1], bounds[1:]):
            product = jnp.dot(
                conv_in[low * wide : high * wide, :], expand_ref[:, lanes],
                preferred_element_type=jnp.float32,
            )
            value = jax.nn.gelu(product, approximate=True).astype(jnp.bfloat16)
            expanded[low:high] = value.astype(jnp.float32).reshape(high - low, wide, block)
        expanded[0] = expanded[0] * flags[0]
        expanded[tall - 1] = expanded[tall - 1] * flags[1]
        expanded[:, col_count:, :] = expanded[:, col_count:, :] * side
        for half in range(block // LANES):
            inner = slice(half * LANES, (half + 1) * LANES)
            outer = pl.ds(pl.multiple_of(step * block + half * LANES, LANES), LANES)
            taps = [taps_ref[k : k + 1, outer] for k in range(9)]

            def rows_of(group, total):
                base = group * 4
                held = [expanded[base + k, :, inner] for k in range(6)]
                for k in range(4):
                    parts = [
                        held[k] * taps[side_step]
                        + held[k + 1] * taps[3 + side_step]
                        + held[k + 2] * taps[6 + side_step]
                        for side_step in range(3)
                    ]
                    summed = (
                        pltpu.roll(parts[0], 1, 0) + parts[1] + pltpu.roll(parts[2], wide - 1, 0)
                    )[:col_count]
                    deep = jax.nn.gelu(summed, approximate=True)
                    total = total + jnp.sum(deep.reshape(col_count // 8, 8, LANES), axis=0)
                    at = pl.ds(pl.multiple_of((base + k) * col_count, col_count), col_count)
                    o_ref[at, outer] = deep.astype(o_ref.dtype)
                return total

            total = lax.fori_loop(0, row_count // 4, rows_of, jnp.zeros((8, LANES), jnp.float32))
            sums_ref[:, outer] = jnp.sum(total, axis=0, keepdims=True)
        return carry

    lax.fori_loop(0, width // block, channels, 0)


def depthwise_stage(latent, conv_scale, conv_shift, expand_weight, depth_kernel):
    row_count, col_count, feats = latent.shape
    width = expand_weight.shape[1]
    row_at, col_at = lax.axis_index("row"), lax.axis_index("col")
    flags = jnp.stack(
        [row_at > 0, row_at < lax.axis_size("row") - 1, col_at > 0, col_at < lax.axis_size("col") - 1]
    ).astype(jnp.float32)
    tall = extended(latent, (("row", 0),), 1)
    count = lax.axis_size("col")
    ahead = [(i, i + 1) for i in range(count - 1)]
    left = lax.ppermute(tall[:, col_count - 1 :], "col", ahead)
    right = lax.ppermute(tall[:, :1], "col", [(b, a) for a, b in ahead])
    blank = jnp.zeros((row_count + 2, PAD - 2, feats), latent.dtype)
    ext = jnp.concatenate([tall, right, blank, left], axis=1).reshape(-1, feats)
    vmem = pl.BlockSpec(memory_space=pltpu.VMEM)
    block = 256
    return pl.pallas_call(
        functools.partial(conv_kernel, row_count, col_count),
        out_shape=(
            jax.ShapeDtypeStruct((row_count * col_count, width), jnp.bfloat16),
            jax.ShapeDtypeStruct((1, width), jnp.float32),
        ),
        in_specs=[pl.BlockSpec(memory_space=pltpu.SMEM)] + [vmem] * 5,
        out_specs=(vmem, vmem),
        scratch_shapes=[
            pltpu.VMEM(ext.shape, jnp.bfloat16),
            pltpu.VMEM((row_count + 2, col_count + PAD, block), jnp.float32),
        ],
        compiler_params=pltpu.CompilerParams(vmem_limit_bytes=20 * 1024 * 1024),
        name="conv_stage",
    )(flags, ext, conv_scale[None], conv_shift[None], expand_weight, depth_kernel)


def per_device(
    latent,
    conv_scale,
    conv_shift,
    expand_weight,
    depth_kernel,
    squeeze_down,
    squeeze_up,
    project_weight,
    block_gain,
    block_projection,
    block_output,
    block_table,
    first_gain,
    first_expand,
    first_reduce,
    grid_gain,
    grid_projection,
    grid_output,
    grid_table,
    second_gain,
    second_expand,
    second_reduce,
):
    row_devices = lax.axis_size("row")
    col_devices = lax.axis_size("col")
    row_count, col_count, channels = latent.shape
    if compact(row_count, col_count) and squeeze_up.shape[0] == LANES:
        return whole_block(
            latent, conv_scale, conv_shift, depth_kernel, (block_table, grid_table),
            (block_gain, first_gain, grid_gain, second_gain),
            (expand_weight, squeeze_down, squeeze_up, project_weight),
            (block_projection, block_output, first_expand, first_reduce,
             grid_projection, grid_output, second_expand, second_reduce),
        )
    depthwise, local_sums = depthwise_stage(
        latent, conv_scale, conv_shift, expand_weight, depth_kernel
    )
    local_sums = local_sums.reshape(-1, LANES)
    channel_sums = axis_sum(axis_sum(local_sums, "row", 1), "col", 2).reshape(-1)
    pooled = channel_sums / (row_count * row_devices * col_count * col_devices)
    excite = squeeze_gate(pooled, squeeze_down, squeeze_up)
    gated = (depthwise.astype(jnp.float32) * excite).astype(jnp.bfloat16)
    conv_out = (
        latent.reshape(-1, channels).astype(jnp.float32)
        + jnp.dot(gated, project_weight, preferred_element_type=jnp.float32)
    ).astype(jnp.bfloat16).reshape(row_count, col_count, channels)

    def run_block(cells, layout, bias):
        return mixer(
            cells, layout, block_gain, block_projection, block_output, bias, first_gain,
            first_expand, first_reduce, block_table.shape[0],
        )

    def run_grid(cells, layout, bias):
        return mixer(
            cells, layout, grid_gain, grid_projection, grid_output, bias, second_gain,
            second_expand, second_reduce, grid_table.shape[0],
        )

    return split_sublayers(conv_out, run_block, run_grid, block_table, grid_table)


def solution(mesh):
    placed = (
        P("row", "col", None),
        P(),
        P(),
        P(),
        P(),
        P(),
        P(),
        P(),
        P(),
        P(),
        P(),
        P(),
        P(),
        P(),
        P(),
        P(),
        P(),
        P(),
        P(),
        P(),
        P(),
        P(),
    )
    return jax.shard_map(
        per_device, mesh=mesh, in_specs=placed, out_specs=P("row", "col", None), check_vma=False
    )
```

```python
import functools

import jax
import jax.numpy as jnp
import numpy as np
from jax import lax
from jax.experimental import pallas as pl
from jax.experimental.pallas import tpu as pltpu
from jax.sharding import PartitionSpec as P

WIN = 8
PAD = 8
QUAD = 4
LOG2E = 1.4426950408889634


def extended(cells, sides, width):
    for axis, dim in sides:
        count = lax.axis_size(axis)
        ends = count - 1
        head = lax.slice_in_dim(cells, 0, width, axis=dim)
        tail = lax.slice_in_dim(cells, cells.shape[dim] - width, cells.shape[dim], axis=dim)
        cells = jnp.concatenate(
            [
                lax.ppermute(tail, axis, [(i, (i + 1) % count) for i in range(ends)]),
                cells,
                lax.ppermute(head, axis, [((i + 1) % count, i) for i in range(ends)]),
            ],
            axis=dim,
        )
    return cells


def layer_norm_apply(values, norm_gain):
    widened = values.astype(jnp.float32)
    center = widened - jnp.mean(widened, axis=-1, keepdims=True)
    spread = jnp.mean(center * center, axis=-1, keepdims=True)
    return (center * lax.rsqrt(spread + 1e-05) * norm_gain).astype(jnp.bfloat16)


def position_bias(offset_bias_lookup):
    spots = offset_bias_lookup.shape[1]
    position = jnp.arange(WIN * WIN)
    down_pos = position // WIN
    across = position % WIN
    relative = (down_pos[:, None] - down_pos[None, :] + WIN - 1) * (2 * WIN - 1) + (
        across[:, None] - across[None, :] + WIN - 1
    )
    indicator_matrix = (relative[:, :, None] == jnp.arange(spots)[None, None, :]).astype(
        jnp.float32
    )
    return jnp.einsum(
        "bp,rjp->brj", offset_bias_lookup, indicator_matrix, precision=lax.Precision.HIGHEST
    )


def attend(triple, pos_bias):
    window_count, tokens, three_width = triple.shape
    feature_width = three_width // 3
    head_count = pos_bias.shape[0]
    head_size = feature_width // head_count
    queries = triple[..., :feature_width].reshape(window_count, tokens, head_count, head_size)
    key_row_list = triple[..., feature_width : 2 * feature_width].reshape(
        window_count, tokens, head_count, head_size
    )
    values = triple[..., 2 * feature_width :].reshape(window_count, tokens, head_count, head_size)
    scores = (
        jnp.einsum("nqhd,nkhd->nhqk", queries, key_row_list, preferred_element_type=jnp.float32)
        * head_size ** (-0.5)
        + pos_bias[None]
    )
    row_max = jnp.max(scores, axis=-1, keepdims=True)
    weight_tensors = jnp.exp(scores - row_max)
    attention_weight_map = (
        weight_tensors / jnp.sum(weight_tensors, axis=-1, keepdims=True)
    ).astype(jnp.bfloat16)
    mixed = jnp.einsum(
        "nhqk,nkhd->nqhd", attention_weight_map, values, preferred_element_type=jnp.float32
    )
    return mixed.astype(jnp.bfloat16).reshape(window_count, tokens, feature_width)


def attention_sublayer(windows, norm_gain, in_weight, out_weight, pos_bias):
    normed = layer_norm_apply(windows, norm_gain)
    triple = jnp.dot(normed, in_weight, preferred_element_type=jnp.float32).astype(jnp.bfloat16)
    mixed = attend(triple, pos_bias)
    return (
        windows.astype(jnp.float32) + jnp.dot(mixed, out_weight, preferred_element_type=jnp.float32)
    ).astype(jnp.bfloat16)


def feed_forward(values, norm_gain, in_weight, out_weight):
    normed = layer_norm_apply(values, norm_gain)
    hidden = jax.nn.gelu(
        jnp.dot(normed, in_weight, preferred_element_type=jnp.float32), approximate=True
    ).astype(jnp.bfloat16)
    return (
        values.astype(jnp.float32) + jnp.dot(hidden, out_weight, preferred_element_type=jnp.float32)
    ).astype(jnp.bfloat16)


def to_blocks(field):
    row_count, col_count, feats = field.shape
    return (
        field.reshape(row_count // WIN, WIN, col_count // WIN, WIN, feats)
        .transpose(0, 2, 1, 3, 4)
        .reshape(-1, WIN * WIN, feats)
    )


def from_blocks(windows, row_count, col_count):
    feats = windows.shape[-1]
    return (
        windows.reshape(row_count // WIN, col_count // WIN, WIN, WIN, feats)
        .transpose(0, 2, 1, 3, 4)
        .reshape(row_count, col_count, feats)
    )


def axis_shape(length, devices):
    fold = max(1, WIN // devices)
    rest = length // max(devices, WIN)
    span = min(devices, WIN)
    return (fold, rest, span, devices // span)


def grid_layout(field):
    row_devices = lax.axis_size("row")
    col_devices = lax.axis_size("col")
    row_count, col_count, feats = field.shape
    row_fold, row_rest, row_span, row_hop = axis_shape(row_count, row_devices)
    col_fold, col_rest, col_span, col_hop = axis_shape(col_count, col_devices)
    ordered_layout = field.reshape(
        row_fold, row_devices, row_rest, col_fold, col_devices, col_rest, feats
    )
    flat = ordered_layout.transpose(1, 4, 0, 2, 3, 5, 6).reshape(
        row_devices * col_devices, row_fold, row_rest, col_fold, col_rest, feats
    )
    flat = lax.all_to_all(flat, ("row", "col"), split_axis=0, concat_axis=0, tiled=True)
    moved = flat.reshape(
        row_devices, col_devices, row_fold, row_rest, col_fold, col_rest, feats
    ).transpose(2, 0, 3, 4, 1, 5, 6)
    moved = moved.reshape(
        row_fold, row_span, row_hop, row_rest, col_fold, col_span, col_hop, col_rest, feats
    )
    return moved.transpose(2, 3, 6, 7, 1, 0, 5, 4, 8).reshape(-1, WIN * WIN, feats)


def spatial_layout(windows, row_count, col_count):
    row_devices = lax.axis_size("row")
    col_devices = lax.axis_size("col")
    feats = windows.shape[-1]
    row_fold, row_rest, row_span, row_hop = axis_shape(row_count, row_devices)
    col_fold, col_rest, col_span, col_hop = axis_shape(col_count, col_devices)
    gridded = windows.reshape(
        row_hop, row_rest, col_hop, col_rest, row_span, row_fold, col_span, col_fold, feats
    )
    ordered_layout = gridded.transpose(5, 4, 0, 1, 7, 6, 2, 3, 8).reshape(
        row_fold, row_devices, row_rest, col_fold, col_devices, col_rest, feats
    )
    flat = ordered_layout.transpose(1, 4, 0, 2, 3, 5, 6).reshape(
        row_devices * col_devices, row_fold, row_rest, col_fold, col_rest, feats
    )
    flat = lax.all_to_all(flat, ("row", "col"), split_axis=0, concat_axis=0, tiled=True)
    moved = flat.reshape(
        row_devices, col_devices, row_fold, row_rest, col_fold, col_rest, feats
    ).transpose(2, 0, 3, 4, 1, 5, 6)
    return moved.reshape(row_count, col_count, feats)


def squeeze_gate(pooled, squeeze_down, squeeze_up):
    reduced = jax.nn.silu(
        jnp.dot(pooled[None, :], squeeze_down.astype(jnp.float32), precision=lax.Precision.HIGHEST)
    )
    return jax.nn.sigmoid(
        jnp.dot(reduced, squeeze_up.astype(jnp.float32), precision=lax.Precision.HIGHEST)
    )[0]


def axis_sum_kernel(axis, count, x_ref, o_ref, slots, send_sem, recv_sem):
    me = lax.axis_index(axis)
    barrier = pltpu.get_barrier_semaphore()
    peers = [lax.rem(me + step, count) for step in range(1, count)]
    for peer in peers:
        pl.semaphore_signal(
            barrier, inc=1, device_id={axis: peer}, device_id_type=pl.DeviceIdType.MESH
        )
    pl.semaphore_wait(barrier, count - 1)
    copies = []
    for step, peer in enumerate(peers):
        copy = pltpu.make_async_remote_copy(
            src_ref=x_ref,
            dst_ref=slots.at[step],
            send_sem=send_sem.at[step],
            recv_sem=recv_sem.at[step],
            device_id={axis: peer},
            device_id_type=pl.DeviceIdType.MESH,
        )
        copy.start()
        copies.append(copy)
    for copy in copies:
        copy.wait()
    total = x_ref[...]
    for step in range(count - 1):
        total = total + slots[step]
    o_ref[...] = total


def axis_sum(values, axis, collective_id):
    count = lax.axis_size(axis)
    if count == 1:
        return values
    return pl.pallas_call(
        functools.partial(axis_sum_kernel, axis, count),
        out_shape=jax.ShapeDtypeStruct(values.shape, values.dtype),
        in_specs=[pl.BlockSpec(memory_space=pltpu.VMEM)],
        out_specs=pl.BlockSpec(memory_space=pltpu.VMEM),
        scratch_shapes=[
            pltpu.VMEM((count - 1,) + values.shape, values.dtype),
            pltpu.SemaphoreType.DMA((count - 1,)),
            pltpu.SemaphoreType.DMA((count - 1,)),
        ],
        compiler_params=pltpu.CompilerParams(
            collective_id=collective_id, has_side_effects=True, vmem_limit_bytes=4 * 1024 * 1024
        ),
        name="axis_sum_" + axis,
    )(values)


LANES = 128
GROUP = 256


def normed_rows(widened, gain):
    center = widened - jnp.mean(widened, axis=-1, keepdims=True)
    spread = jnp.mean(center * center, axis=-1, keepdims=True)
    return (center * lax.rsqrt(spread + 1e-05) * gain).astype(jnp.bfloat16)


def mixer_kernel(
    layout, head_size, x_ref, gain_ref, bias_ref, late_gain_ref, proj_hbm, out_hbm, up_hbm, down_hbm,
    o_ref, triple, heads, proj_ref, out_w_ref, up_ref, down_ref, sems,
):
    kind, across = layout
    rows_total, feats = x_ref.shape
    tokens = WIN * WIN
    window_count = rows_total // tokens
    slabs = feats // LANES
    per_slab = LANES // head_size
    moves = [
        pltpu.make_async_copy(src, dst, sems.at[k])
        for k, (src, dst) in enumerate(
            ((proj_hbm, proj_ref), (out_hbm, out_w_ref), (up_hbm, up_ref), (down_hbm, down_ref))
        )
    ]
    moves[0].start()
    moves[0].wait()
    for move in moves[1:]:
        move.start()
    chunk = 256

    def project(step, carry):
        rows = pl.ds(pl.multiple_of(step * chunk, chunk), chunk)
        normed = normed_rows(x_ref[rows, :].astype(jnp.float32), gain_ref[...])
        for part in range(3 * slabs // 2):
            product = jnp.dot(
                normed, proj_ref[:, part * GROUP : (part + 1) * GROUP],
                preferred_element_type=jnp.float32,
            ).astype(jnp.bfloat16).astype(jnp.float32)
            triple[2 * part, rows, :] = product[:, :LANES]
            triple[2 * part + 1, rows, :] = product[:, LANES:]
        return carry

    lax.fori_loop(0, rows_total // chunk, project, 0)

    def places(window):
        if kind == "strided":
            return [pl.ds(window, tokens, stride=across)]
        per_row = across // WIN
        base = (window // per_row) * (WIN * across) + (window % per_row) * WIN
        return [pl.ds(pl.multiple_of(base + r * across, WIN), WIN) for r in range(WIN)]

    lane = lax.broadcasted_iota(jnp.int32, (tokens, GROUP), 1)
    head_of = (lane % LANES) // head_size
    scale = head_size ** (-0.5)

    def one_window(window):
        spots = places(window)

        def fetch(slab):
            pieces = [triple[slab, spot, :] for spot in spots]
            whole = pieces[0] if len(pieces) == 1 else jnp.concatenate(pieces, axis=0)
            return whole

        empty = jnp.zeros((tokens, LANES), jnp.bfloat16)
        for group in range(slabs // 2):
            first, second = 2 * group, 2 * group + 1
            query_0 = fetch(first).astype(jnp.bfloat16)
            query_1 = fetch(second).astype(jnp.bfloat16)
            keys = jnp.concatenate([fetch(slabs + first), fetch(slabs + second)], axis=1)
            vals = jnp.concatenate([fetch(2 * slabs + first), fetch(2 * slabs + second)], axis=1)
            block_q = jnp.concatenate(
                [
                    jnp.concatenate([query_0, empty], axis=1),
                    jnp.concatenate([empty, query_1], axis=1),
                ],
                axis=0,
            )
            block_k = jnp.concatenate(
                [jnp.where(head_of == j, keys, 0.0).astype(jnp.bfloat16) for j in range(per_slab)],
                axis=0,
            )
            block_v = jnp.concatenate(
                [jnp.where(head_of == j, vals, 0.0).astype(jnp.bfloat16) for j in range(per_slab)],
                axis=0,
            )
            scores = lax.dot_general(
                block_k, block_q, (((1,), (1,)), ((), ())), preferred_element_type=jnp.float32
            )
            scores = (scores * scale + bias_ref[group]).reshape(per_slab, tokens, 2 * tokens)
            weights = jnp.exp(scores - jnp.max(scores, axis=1, keepdims=True))
            shares = weights * (1.0 / jnp.sum(weights, axis=1, keepdims=True))
            shares = shares.reshape(per_slab * tokens, 2 * tokens).astype(jnp.bfloat16)
            mixed = lax.dot_general(
                shares, block_v, (((0,), (0,)), ((), ())), preferred_element_type=jnp.float32
            )
            for slab, part in (
                (first, mixed[:tokens, :LANES]), (second, mixed[tokens:, LANES:])
            ):
                if len(spots) == 1:
                    heads[slab, spots[0], :] = part
                else:
                    for r, spot in enumerate(spots):
                        heads[slab, spot, :] = part[r * WIN : (r + 1) * WIN]

    def attend_pair(step, carry):
        one_window(2 * step)
        one_window(2 * step + 1)
        return carry

    lax.fori_loop(0, window_count // 2, attend_pair, 0)
    for move in moves[1:]:
        move.wait()
    hidden_width = up_ref.shape[1]
    tile = 512

    def feed(step, carry):
        rows = pl.ds(pl.multiple_of(step * chunk, chunk), chunk)
        mixed = jnp.concatenate([heads[s, rows, :] for s in range(slabs)], axis=1).astype(jnp.bfloat16)
        value = (
            x_ref[rows, :].astype(jnp.float32)
            + jnp.dot(mixed, out_w_ref[...], preferred_element_type=jnp.float32)
        ).astype(jnp.bfloat16).astype(jnp.float32)
        normed = normed_rows(value, late_gain_ref[...])
        for k in range(hidden_width // tile):
            part = slice(k * tile, (k + 1) * tile)
            hidden = jax.nn.gelu(
                jnp.dot(normed, up_ref[:, part], preferred_element_type=jnp.float32),
                approximate=True,
            ).astype(jnp.bfloat16)
            value = value + jnp.dot(hidden, down_ref[part, :], preferred_element_type=jnp.float32)
        o_ref[rows, :] = value.astype(jnp.bfloat16)
        return carry

    lax.fori_loop(0, rows_total // chunk, feed, 0)


def mixer(x, layout, gain, in_weight, out_weight, bias, late_gain, up, down, heads_count):
    rows, feats = x.shape
    vmem = pl.BlockSpec(memory_space=pltpu.VMEM)
    hbm = pl.BlockSpec(memory_space=pltpu.HBM)
    flops = 8 * rows * feats * (4 * feats + 2 * up.shape[1])
    return pl.pallas_call(
        functools.partial(mixer_kernel, layout, feats // heads_count),
        out_shape=jax.ShapeDtypeStruct((rows, feats), jnp.bfloat16),
        in_specs=[vmem] * 4 + [hbm] * 4,
        out_specs=vmem,
        scratch_shapes=[
            pltpu.VMEM((3 * feats // LANES, rows, LANES), jnp.float32),
            pltpu.VMEM((feats // LANES, rows, LANES), jnp.float32),
            pltpu.VMEM(in_weight.shape, jnp.bfloat16),
            pltpu.VMEM(out_weight.shape, jnp.bfloat16),
            pltpu.VMEM(up.shape, jnp.bfloat16),
            pltpu.VMEM(down.shape, jnp.bfloat16),
            pltpu.SemaphoreType.DMA((4,)),
        ],
        compiler_params=pltpu.CompilerParams(vmem_limit_bytes=60 * 1024 * 1024),
        cost_estimate=pl.CostEstimate(
            flops=flops, bytes_accessed=12 * 1024 * 1024, transcendentals=0
        ),
        name="mixer_" + layout[0],
    )(x, gain[None], bias, late_gain[None], in_weight, out_weight, up, down)


def key_major_bias(table, down, across):
    head_count, spots = table.shape
    relative = (down[None, :] - down[:, None] + WIN - 1) * (2 * WIN - 1) + (
        across[None, :] - across[:, None] + WIN - 1
    )
    tokens = WIN * WIN
    chosen = (jnp.arange(spots)[:, None] == jnp.asarray(relative.reshape(-1))[None, :]).astype(
        jnp.float32
    )
    spread = jnp.dot(table, chosen, precision=lax.Precision.HIGHEST)
    return (
        spread.reshape(head_count // 8, 2, 4, tokens, tokens)
        .transpose(0, 2, 3, 1, 4)
        .reshape(head_count // 8, 4 * tokens, 2 * tokens)
    )


def split_sublayers(conv_out, run_block, run_grid, block_table, grid_table):
    row_devices = lax.axis_size("row")
    col_devices = lax.axis_size("col")
    row_count, col_count, feats = conv_out.shape
    plain = np.arange(WIN * WIN)
    block_bias = key_major_bias(block_table, plain // WIN, plain % WIN)
    if row_devices > WIN or col_devices > WIN:
        section = run_block(conv_out.reshape(-1, feats), ("blocks", col_count), block_bias)
        windows = grid_layout(section.reshape(row_count, col_count, feats))
        count = windows.shape[0]
        bias = key_major_bias(grid_table, plain // WIN, plain % WIN)
        out = run_grid(windows.transpose(1, 0, 2).reshape(-1, feats), ("strided", count), bias)
        out = out.reshape(WIN * WIN, count, feats).transpose(1, 0, 2)
        return spatial_layout(out, row_count, col_count)
    devices = row_devices * col_devices
    row_fold, col_fold = WIN // row_devices, WIN // col_devices
    row_rest, col_rest = row_count // row_fold, col_count // col_fold
    parts = row_rest // WIN
    count = WIN * col_rest // devices
    pieces = col_rest // count
    order = np.arange(WIN * WIN).reshape(row_devices, col_devices, row_fold, col_fold)
    at = np.indices(order.shape).reshape(4, -1)
    grid_bias = key_major_bias(grid_table, at[0] * row_fold + at[2], at[1] * col_fold + at[3])
    strips = conv_out.reshape(row_fold, parts, WIN, col_count, feats)
    results = []
    for part in range(parts):
        section = run_block(
            strips[:, part].reshape(-1, feats), ("blocks", col_count), block_bias
        )
        sent = (
            section.reshape(row_fold, WIN, col_fold, pieces, count, feats)
            .transpose(1, 3, 0, 2, 4, 5)
            .reshape(devices, row_fold * col_fold * count, feats)
        )
        got = lax.all_to_all(sent, ("row", "col"), split_axis=0, concat_axis=0, tiled=True)
        out = run_grid(got.reshape(-1, feats), ("strided", count), grid_bias)
        back = lax.all_to_all(
            out.reshape(devices, -1, feats), ("row", "col"), split_axis=0, concat_axis=0, tiled=True
        )
        results.append(
            back.reshape(WIN, pieces, row_fold, col_fold, count, feats)
            .transpose(2, 0, 3, 1, 4, 5)
            .reshape(row_fold, WIN, col_count, feats)
        )
    return jnp.stack(results, axis=1).reshape(row_count, col_count, feats)


def device_of(flat, columns):
    return {"row": lax.div(flat, columns), "col": lax.rem(flat, columns)}


CORNERS = ((-1, -1), (-1, 1), (1, -1), (1, 1))


def split_parts(values):
    high = values.astype(jnp.bfloat16)
    rest = values - high.astype(jnp.float32)
    middle = rest.astype(jnp.bfloat16)
    low = (rest - middle.astype(jnp.float32)).astype(jnp.bfloat16)
    return high, middle, low


def exact_rows(values, weight):
    stacked = jnp.concatenate([p.astype(jnp.float32) for p in split_parts(values)], axis=0)
    product = jnp.dot(
        stacked.astype(jnp.bfloat16), weight[...], preferred_element_type=jnp.float32
    )
    return jnp.sum(product, axis=0, keepdims=True)


def twice_gelu(x):
    inner = x * (0.7978845608028654 + (0.7978845608028654 * 0.044715) * (x * x))
    return x + x * jnp.tanh(inner)


def block_kernel(
    shape, head_size, latent, scale_in, shift_in, taps_in, block_table, grid_table,
    gain_0, gain_1, gain_2, gain_3,
    h0, h1, h2, h3, w0, w1, w2, w3, w4, w5, w6, w7, o_ref,
    u0, u1, u2, u3, triple, heads, v0, v1, v2, v3, v4, v5, v6, v7,
    section, got, output, back, edges, halo, corner, conv_in, halo_in, expanded, deep_ref,
    sums, slots, excite_ref, padded, block_bias, grid_bias, score_ref, share_ref, half_taps,
    weight_sem, send_sem, recv_sem, halo_send, halo_recv, sum_send, sum_recv,
):
    parts, pieces, rows_n, columns = shape
    devices = rows_n * columns
    row_count, col_count, feats = latent.shape
    width = u0.shape[1]
    slabs = feats // LANES
    per_slab = LANES // head_size
    tokens = WIN * WIN
    message = section.shape[1]
    folds = message // WIN
    chunk = 256
    batch = chunk // message
    halves = devices // batch
    part_rows = devices * message
    wide = col_count + PAD
    fold_rows = row_count // folds
    row_at, col_at = lax.axis_index("row"), lax.axis_index("col")
    me = row_at * columns + col_at
    mesh_ids = pl.DeviceIdType.MESH
    barrier = pltpu.get_barrier_semaphore()

    def greet(step, carry):
        pl.semaphore_signal(
            barrier, inc=1, device_id=device_of(lax.rem(me + step, devices), columns),
            device_id_type=mesh_ids,
        )
        return carry

    lax.fori_loop(1, devices, greet, 0)
    moves = [
        pltpu.make_async_copy(src, dst, weight_sem.at[k])
        for k, (src, dst) in enumerate(
            zip(
                (h0, h1, h2, h3, w0, w1, w2, w3, w4, w5, w6, w7),
                (u0, u1, u2, u3, v0, v1, v2, v3, v4, v5, v6, v7),
            )
        )
    ]
    for move in moves:
        move.start()

    near = {
        (down, side): jnp.logical_and(
            jnp.logical_and(row_at + down >= 0, row_at + down < rows_n),
            jnp.logical_and(col_at + side >= 0, col_at + side < columns),
        )
        for down in (-1, 0, 1)
        for side in (-1, 0, 1)
    }
    for side, block, inner in ((0, 0, 0), (1, col_count - message, message - 1)):
        for group in range(row_count // 8):
            cells = latent[8 * group : 8 * group + 8, block : block + message, :]
            edges[side, 8 * group : 8 * group + 8, :] = (
                cells.astype(jnp.float32)[:, inner, :].astype(jnp.bfloat16)
            )
    sides = ((-1, 0), (1, 0), (0, -1), (0, 1))
    for k, way in enumerate(sides):

        @pl.when(jnp.logical_not(near[way]))
        def _(k=k):
            halo[k] = jnp.zeros(halo.shape[1:], halo.dtype)

    for k, way in enumerate(CORNERS):

        @pl.when(jnp.logical_not(near[way]))
        def _(k=k):
            corner[k] = jnp.zeros(corner.shape[1:], corner.dtype)

    for group in range(row_count // 8):
        cells = latent[8 * group : 8 * group + 8].reshape(8 * col_count, feats)
        conv_in[8 * group * col_count : 8 * (group + 1) * col_count, :] = (
            cells.astype(jnp.float32) * scale_in[...] + shift_in[...]
        ).astype(jnp.bfloat16)
    half_taps[...] = 0.5 * taps_in[...]

    def outgoing(k):
        if k < 4:
            down, side = sides[k]
            src = (
                latent.at[0], latent.at[row_count - 1], edges.at[0], edges.at[1]
            )[k]
            dst = halo.at[k ^ 1]
        else:
            down, side = CORNERS[k - 4]
            line = 0 if down < 0 else row_count - 1
            start = 0 if side < 0 else col_count - message
            src = latent.at[line, pl.ds(start, message)]
            dst = corner.at[7 - k]
        return pltpu.make_async_remote_copy(
            src_ref=src, dst_ref=dst, send_sem=halo_send.at[k], recv_sem=halo_recv.at[k],
            device_id={"row": row_at + down, "col": col_at + side}, device_id_type=mesh_ids,
        )

    moves[0].wait()
    block = 256

    def expand(step, carry):
        lanes = pl.ds(pl.multiple_of(step * block, block), block)
        for group in range(row_count // 8):
            product = jnp.dot(
                conv_in[8 * group * col_count : 8 * (group + 1) * col_count, :], u0[:, lanes],
                preferred_element_type=jnp.float32,
            )
            value = twice_gelu(product.astype(jnp.bfloat16)).astype(jnp.float32)
            for r in range(8):
                start = PAD + (1 + 8 * group + r) * wide
                for half in range(block // LANES):
                    expanded[step * (block // LANES) + half, start : start + col_count, :] = value[
                        r * col_count : (r + 1) * col_count, half * LANES : (half + 1) * LANES
                    ]
        return carry

    lax.fori_loop(0, width // block // 2, expand, 0)
    pl.semaphore_wait(barrier, devices - 1)
    ways = sides + CORNERS
    for k, way in enumerate(ways):

        @pl.when(near[way])
        def _(k=k):
            outgoing(k).start()

    lax.fori_loop(width // block // 2, width // block, expand, 0)
    for k, way in enumerate(ways):
        opposite = (-way[0], -way[1])
        src_k = ways.index(opposite)

        @pl.when(near[way])
        def _(k=k, src_k=src_k):
            target = halo.at[k] if k < 4 else corner.at[k - 4]
            pltpu.make_async_copy(target, target, halo_recv.at[src_k]).wait()

    picked = [
        corner[k].astype(jnp.float32)[(message - 1 if side < 0 else 0) :][:1]
        for k, (_, side) in enumerate(CORNERS)
    ]
    picked = jnp.concatenate(picked + [jnp.zeros((message - 4, feats), jnp.float32)], axis=0)
    around = 2 * (row_count + col_count)
    for k, (start, size) in enumerate(
        (
            (0, col_count), (col_count, col_count), (2 * col_count, row_count),
            (2 * col_count + row_count, row_count),
        )
    ):
        halo_in[start : start + size, :] = (
            halo[k].astype(jnp.float32) * scale_in[...] + shift_in[...]
        ).astype(jnp.bfloat16)
    halo_in[around:, :] = (picked * scale_in[...] + shift_in[...]).astype(jnp.bfloat16)
    tall = row_count + 2

    def expand_halo(step, carry):
        lanes = pl.ds(pl.multiple_of(step * block, block), block)
        product = jnp.dot(halo_in[...], u0[:, lanes], preferred_element_type=jnp.float32)
        value = twice_gelu(product.astype(jnp.bfloat16)).astype(jnp.float32)
        up = jnp.where(near[(-1, 0)], value[:col_count], 0.0)
        low = jnp.where(near[(1, 0)], value[col_count : 2 * col_count], 0.0)
        left = jnp.where(near[(0, -1)], value[2 * col_count : 2 * col_count + row_count], 0.0)
        right = jnp.where(near[(0, 1)], value[2 * col_count + row_count : around], 0.0)
        for half in range(block // LANES):
            inner = slice(half * LANES, (half + 1) * LANES)
            outer = step * (block // LANES) + half
            last = PAD + (tall - 1) * wide
            expanded[outer, PAD : PAD + col_count, :] = up[:, inner]
            expanded[outer, last : last + col_count, :] = low[:, inner]
            expanded[outer, pl.ds(PAD + wide + col_count, row_count, stride=wide), :] = right[:, inner]
            expanded[outer, pl.ds(PAD + wide - 1, row_count, stride=wide), :] = left[:, inner]
            for k, way in enumerate(CORNERS):
                row = (PAD if way[0] < 0 else last) + (-1 if way[1] < 0 else col_count)
                expanded[outer, row : row + 1, :] = jnp.where(
                    near[way], value[around + k : around + k + 1, inner], 0.0
                )
        return carry

    lax.fori_loop(0, width // block, expand_halo, 0)

    def depth(step, carry):
        lanes = pl.ds(pl.multiple_of(step * LANES, LANES), LANES)
        taps = [half_taps[k : k + 1, lanes] for k in range(9)]

        def pair_of_rows(group, total):
            results = []
            for fold in range(folds):
                first = fold * fold_rows + 2 * group
                base = pl.multiple_of(first * wide, 8)
                held = [
                    [
                        expanded[step, pl.ds(base + (PAD + k * wide + side), col_count), :]
                        for side in (-1, 0, 1)
                    ]
                    for k in range(4)
                ]
                for k in range(2):
                    summed = sum(
                        held[k + down][side] * taps[3 * down + side]
                        for down in range(3)
                        for side in range(3)
                    )
                    value = twice_gelu(summed)
                    total = total + jnp.sum(value.reshape(col_count // 8, 8, LANES), axis=0)
                    results.append(value)
            part, down = lax.div(2 * group, WIN), lax.rem(2 * group, WIN)
            for k in range(2):
                for piece in range(pieces):
                    rows = slice(piece * WIN, (piece + 1) * WIN)
                    tile = jnp.concatenate(
                        [results[2 * fold + k][rows] for fold in range(folds)], axis=0
                    )
                    at = part * devices + piece * WIN + down + k
                    deep_ref[at, :, lanes] = tile.astype(jnp.bfloat16)
            return total

        sums[:, lanes] = lax.fori_loop(
            0, fold_rows // 2, pair_of_rows, jnp.zeros((8, LANES), jnp.float32), unroll=2
        )
        return carry

    lax.fori_loop(0, width // LANES, depth, 0)
    for move in moves[1:4]:
        move.wait()
    slots[me] = exact_rows(0.5 * sums[...], u1)

    def share(step, carry):
        pltpu.make_async_remote_copy(
            src_ref=slots.at[me], dst_ref=slots.at[me], send_sem=sum_send, recv_sem=sum_recv,
            device_id=device_of(lax.rem(me + step, devices), columns), device_id_type=mesh_ids,
        ).start()
        return carry

    lax.fori_loop(1, devices, share, 0)
    span = 2 * WIN
    spot = lax.broadcasted_iota(jnp.int32, (slabs * per_slab, span * span), 1)
    place = lax.broadcasted_iota(jnp.int32, (WIN, LANES), 1)
    for table, bias in ((block_table, block_bias), (grid_table, grid_bias)):
        padded[...] = jnp.zeros(padded.shape, jnp.float32)
        padded[:, : table.shape[1]] = table[...] * LOG2E
        flat = padded[...]
        spread = jnp.zeros(flat.shape, jnp.float32)
        for down in range(2 * WIN - 1):
            moved = flat if down == 0 else pltpu.roll(flat, down, 1)
            spread = jnp.where(spot // span == down, moved, spread)
        for head in range(slabs * per_slab // 2):
            group, j = head // per_slab, head % per_slab
            pair = [
                jnp.broadcast_to(spread[h : h + 1], (WIN, span * span))
                for h in (group * 2 * per_slab + j, group * 2 * per_slab + per_slab + j)
            ]
            for kr in range(WIN):
                shift = span * kr - (span * (WIN - 1) + WIN - 1)
                first, second = [
                    pltpu.roll(
                        pair[s], (shift + WIN * s) % (span * span), 1, stride=1, stride_axis=0
                    )[:, :LANES]
                    for s in range(2)
                ]
                start = j * tokens + kr * WIN
                bias[group, start : start + WIN, :] = jnp.where(place % span < WIN, first, second)
    arrivals = slots.at[pl.ds(0, devices - 1)]
    pltpu.make_async_copy(arrivals, arrivals, sum_recv).wait()
    pooled = jnp.sum(slots[...].reshape(devices, LANES), axis=0, keepdims=True) / (
        row_count * rows_n * col_count * columns
    )
    reduced = jax.nn.silu(pooled)
    spare = jnp.zeros((7, LANES), jnp.float32)
    excite_ref[...] = 0.5 * jax.nn.sigmoid(exact_rows(jnp.concatenate([reduced, spare], axis=0), u2))
    for move in moves[4:8]:
        move.wait()

    def project(values, rows, gain_ref, weight):
        normed = normed_rows(values.astype(jnp.float32), gain_ref[...])
        for part in range(3 * slabs // 2):
            product = jnp.dot(
                normed, weight[:, part * GROUP : (part + 1) * GROUP],
                preferred_element_type=jnp.float32,
            ).astype(jnp.bfloat16).astype(jnp.float32)
            triple[2 * part, rows, :] = product[:, :LANES]
            triple[2 * part + 1, rows, :] = product[:, LANES:]

    lane = lax.broadcasted_iota(jnp.int32, (tokens, GROUP), 1)
    masks = [
        jnp.where((lane % LANES) // head_size == j, 1.0, 0.0).astype(jnp.bfloat16)
        for j in range(per_slab)
    ]
    scale = head_size ** (-0.5) * LOG2E

    def attend_windows(windows, bias_ref):
        def spread(spots, slab, group):
            joined = jnp.concatenate(
                [
                    jnp.concatenate([triple[slab + 2 * group + k, spot, :] for spot in spots], axis=0)
                    for k in range(2)
                ],
                axis=1,
            ).astype(jnp.bfloat16)
            return jnp.concatenate([joined * mask for mask in masks], axis=0)

        empty = jnp.zeros((WIN, LANES), jnp.float32)
        chains = [(n, g) for n in range(len(windows)) for g in range(slabs // 2)]
        for at, (n, group) in enumerate(chains):
            spots = windows[n]
            left, right = [
                [triple[2 * group + k, spot, :] for spot in spots] for k in range(2)
            ]
            block_q = jnp.concatenate(
                [
                    jnp.concatenate([p for q in left for p in (q, empty)], axis=0),
                    jnp.concatenate([p for q in right for p in (empty, q)], axis=0),
                ],
                axis=1,
            ).astype(jnp.bfloat16)
            score_ref[at] = lax.dot_general(
                spread(spots, slabs, group), block_q, (((1,), (1,)), ((), ())),
                preferred_element_type=jnp.float32,
            )
        for at, (n, group) in enumerate(chains):
            scores = (score_ref[at] * scale + bias_ref[group]).reshape(
                per_slab, tokens, 2 * tokens
            )
            weights = jnp.exp2(scores - jnp.max(scores, axis=1, keepdims=True))
            shares = weights * (1.0 / jnp.sum(weights, axis=1, keepdims=True))
            share_ref[at] = shares.reshape(per_slab * tokens, 2 * tokens).astype(jnp.bfloat16)
        for at, (n, group) in enumerate(chains):
            mixed = lax.dot_general(
                share_ref[at], spread(windows[n], 2 * slabs, group), (((0,), (0,)), ((), ())),
                preferred_element_type=jnp.float32,
            )
            for r, spot in enumerate(windows[n]):
                start = 2 * r * WIN
                heads[2 * group, spot, :] = mixed[start : start + WIN, :LANES]
                heads[2 * group + 1, spot, :] = mixed[start + WIN : start + 2 * WIN, LANES:]

    def feed(values, rows, gain_ref, out_w, up, down):
        mixed = jnp.concatenate([heads[s, rows, :] for s in range(slabs)], axis=1).astype(jnp.bfloat16)
        value = (
            values.astype(jnp.float32)
            + jnp.dot(mixed, out_w[...], preferred_element_type=jnp.float32)
        ).astype(jnp.bfloat16).astype(jnp.float32)
        normed = normed_rows(value, gain_ref[...])
        tile = 512
        total = None
        for k in range(up.shape[1] // tile):
            part = slice(k * tile, (k + 1) * tile)
            hidden = twice_gelu(
                jnp.dot(normed, up[:, part], preferred_element_type=jnp.float32).astype(jnp.bfloat16)
            )
            product = jnp.dot(hidden, down[part, :], preferred_element_type=jnp.float32)
            total = product if total is None else total + product
        value = value + 0.5 * total
        return value.astype(jnp.bfloat16)

    def block_step(step, carry):
        part, half = lax.div(step, halves), lax.rem(step, halves)
        whole = pl.ds(0, chunk)
        across = batch // WIN
        own = {}
        for down in range(WIN):
            for fold in range(folds):
                line = latent[
                    fold * fold_rows + part * WIN + down,
                    pl.ds(pl.multiple_of(half * (across * WIN), across * WIN), across * WIN), :,
                ].astype(jnp.float32)
                for piece in range(across):
                    own[piece, down, fold] = line[piece * WIN : (piece + 1) * WIN]
        own = jnp.concatenate([own[key] for key in sorted(own)], axis=0)
        for k in range(width // block):
            lanes = slice(k * block, (k + 1) * block)
            gated = (
                deep_ref[pl.ds(step * batch, batch), :, lanes].reshape(chunk, block).astype(jnp.float32)
                * excite_ref[:, lanes]
            ).astype(jnp.bfloat16)
            own = own + jnp.dot(gated, u3[lanes, :], preferred_element_type=jnp.float32)
        value = own.astype(jnp.bfloat16)
        conv_in[0:chunk, :] = value
        project(value, whole, gain_0, v0)

        attend_windows(
            [
                [pl.ds(piece * (WIN * message) + fold * WIN + r * message, WIN) for r in range(WIN)]
                for piece in range(across)
                for fold in range(folds)
            ],
            block_bias,
        )
        done = feed(conv_in[0:chunk, :], whole, gain_1, v1, v2, v3)
        section[pl.ds(step * batch, batch)] = done.reshape(batch, message, feats)

        def send(i, inner):
            at = lax.rem(i + me, batch)
            target = lax.rem(at, WIN) * pieces + half * across + lax.div(at, WIN)
            src, dst = section.at[step * batch + at], got.at[part * devices + me]

            @pl.when(target != me)
            def _():
                pltpu.make_async_remote_copy(
                    src_ref=src, dst_ref=dst, send_sem=send_sem.at[0, part],
                    recv_sem=recv_sem.at[0, part], device_id=device_of(target, columns),
                    device_id_type=mesh_ids,
                ).start()

            @pl.when(target == me)
            def _():
                pltpu.make_async_copy(src, dst, recv_sem.at[0, part]).start()

            return inner

        lax.fori_loop(0, batch, send, 0)
        return carry

    lax.fori_loop(0, parts * halves, block_step, 0)
    for move in moves[8:]:
        move.wait()
    slot = lax.rem(me, pieces) * WIN + lax.div(me, pieces)

    def arrived(buffer, kind, part):
        mail = buffer.at[pl.ds(part * devices, devices)]
        pltpu.make_async_copy(mail, mail, recv_sem.at[kind, part]).wait()

    def grid_step(part, carry):
        arrived(got, 0, part)

        def rows_of(half):
            return got[pl.ds(part * devices + half * batch, batch)].reshape(chunk, feats)

        for half in range(halves):
            project(rows_of(half), pl.ds(half * chunk, chunk), gain_2, v4)

        def attend_some(step, inner):
            attend_windows(
                [
                    [
                        pl.ds(r * columns * message + fold * WIN + QUAD * step + k, columns, stride=message)
                        for r in range(rows_n)
                        for fold in range(folds)
                    ]
                    for k in range(QUAD)
                ],
                grid_bias,
            )
            return inner

        lax.fori_loop(0, part_rows // tokens // QUAD, attend_some, 0)

        def feed_half(half, inner):
            rows = pl.ds(pl.multiple_of(half * chunk, chunk), chunk)
            done = feed(rows_of(half), rows, gain_3, v5, v6, v7)
            output[pl.ds(part * devices + half * batch, batch)] = done.reshape(batch, message, feats)

            def send(i, inner_2):
                target = half * batch + lax.rem(i + me, batch)
                src, dst = output.at[part * devices + target], back.at[part * devices + slot]

                @pl.when(target != me)
                def _():
                    pltpu.make_async_remote_copy(
                        src_ref=src, dst_ref=dst, send_sem=send_sem.at[1, part],
                        recv_sem=recv_sem.at[1, part], device_id=device_of(target, columns),
                        device_id_type=mesh_ids,
                    ).start()

                @pl.when(target == me)
                def _():
                    pltpu.make_async_copy(src, dst, recv_sem.at[1, part]).start()

                return inner_2

            lax.fori_loop(0, batch, send, 0)
            return inner

        lax.fori_loop(0, halves, feed_half, 0)
        return carry

    lax.fori_loop(0, parts, grid_step, 0)

    def finish(part, carry):
        arrived(back, 1, part)

        def put(down, inner):
            tiles = [
                back[part * devices + piece * WIN + down].astype(jnp.float32)
                for piece in range(pieces)
            ]
            for fold in range(folds):
                line = jnp.concatenate([t[fold * WIN : (fold + 1) * WIN] for t in tiles], axis=0)
                start = (fold * fold_rows + part * WIN + down) * col_count
                o_ref[pl.ds(pl.multiple_of(start, col_count), col_count), :] = line.astype(jnp.bfloat16)
            return inner

        return lax.fori_loop(0, WIN, put, carry)

    lax.fori_loop(0, parts, finish, 0)
    for kind, buffer in ((0, section), (1, output)):
        for part in range(parts):
            sent = buffer.at[pl.ds(part * devices, devices - 1)]
            pltpu.make_async_copy(sent, sent, send_sem.at[kind, part]).wait()
    pltpu.make_async_copy(arrivals, arrivals, sum_send).wait()
    for k, way in enumerate(ways):

        @pl.when(near[way])
        def _(k=k):
            target = halo.at[k] if k < 4 else corner.at[k - 4]
            pltpu.make_async_copy(target, target, halo_send.at[k]).wait()


def whole_block(latent, scale, shift, taps, tables, gains, front, weights):
    row_count, col_count, feats = latent.shape
    rows_n, columns = lax.axis_size("row"), lax.axis_size("col")
    devices = rows_n * columns
    parts, pieces = row_count // (2 * WIN), col_count // WIN
    heads_n = tables[0].shape[0]
    rows = row_count * col_count
    width = front[0].shape[1]
    message = rows // (parts * devices)
    around = 2 * (row_count + col_count) + message
    vmem = pl.BlockSpec(memory_space=pltpu.VMEM)
    hbm = pl.BlockSpec(memory_space=pltpu.HBM)
    half_type = jnp.bfloat16
    mail = pltpu.VMEM((parts * devices, message, feats), half_type)
    bias = pltpu.VMEM((heads_n // 8, 4 * WIN * WIN, 2 * WIN * WIN), jnp.float32)
    dma = pltpu.SemaphoreType.DMA
    return pl.pallas_call(
        functools.partial(block_kernel, (parts, pieces, rows_n, columns), feats // heads_n),
        out_shape=jax.ShapeDtypeStruct((rows, feats), half_type),
        in_specs=[vmem] * 10 + [hbm] * 12,
        out_specs=vmem,
        scratch_shapes=[pltpu.VMEM(w.shape, half_type) for w in front]
        + [
            pltpu.VMEM((3 * feats // LANES, rows // parts, LANES), jnp.float32),
            pltpu.VMEM((feats // LANES, rows // parts, LANES), jnp.float32),
        ]
        + [pltpu.VMEM(w.shape, half_type) for w in weights]
        + [
            mail, mail, mail, mail,
            pltpu.VMEM((2, row_count, feats), half_type),
            pltpu.VMEM((4, row_count, feats), half_type),
            pltpu.VMEM((4, message, feats), half_type),
            pltpu.VMEM((rows, feats), half_type),
            pltpu.VMEM((around, feats), half_type),
            pltpu.VMEM(
                (width // LANES, PAD + (row_count + 2) * (col_count + PAD), LANES), jnp.float32
            ),
            pltpu.VMEM((parts * devices, message, width), half_type),
            pltpu.VMEM((8, width), jnp.float32),
            pltpu.VMEM((devices, 1, LANES), jnp.float32),
            pltpu.VMEM((1, width), jnp.float32),
            pltpu.VMEM((heads_n, 4 * WIN * WIN), jnp.float32),
            bias, bias,
            pltpu.VMEM((QUAD * heads_n // 8, 4 * WIN * WIN, 2 * WIN * WIN), jnp.float32),
            pltpu.VMEM((QUAD * heads_n // 8, 4 * WIN * WIN, 2 * WIN * WIN), half_type),
            pltpu.VMEM(taps.shape, jnp.float32),
            dma((12,)), dma((2, parts)), dma((2, parts)), dma((8,)), dma((8,)), dma, dma,
        ],
        compiler_params=pltpu.CompilerParams(
            collective_id=3, has_side_effects=True, vmem_limit_bytes=50 * 1024 * 1024
        ),
        name="whole_block",
    )(
        latent, scale[None], shift[None], taps, *tables, *[g[None] for g in gains], *front, *weights
    ).reshape(latent.shape)


def compact(row_count, col_count):
    row_devices, col_devices = lax.axis_size("row"), lax.axis_size("col")
    return (
        2 * row_devices == WIN and col_devices == WIN
        and row_count % (2 * WIN) == 0 and col_count == WIN * row_devices
        and row_count == col_count
    )


def conv_kernel(
    row_count, col_count, flags, ext_ref, scale_ref, shift_ref, expand_ref, taps_ref,
    o_ref, sums_ref, conv_in, expanded,
):
    wide = col_count + PAD
    tall = row_count + 2
    width = expand_ref.shape[1]
    block = expanded.shape[-1]
    bounds = [8 * k for k in range(row_count // 8)] + [tall]
    for low, high in zip(bounds[:-1], bounds[1:]):
        rows = slice(low * wide, high * wide)
        conv_in[rows, :] = (
            ext_ref[rows, :].astype(jnp.float32) * scale_ref[...] + shift_ref[...]
        ).astype(jnp.bfloat16)
    spot = lax.broadcasted_iota(jnp.int32, (1, PAD, block), 1)
    side = jnp.where(spot == 0, flags[3], jnp.where(spot == PAD - 1, flags[2], 0.0))

    def channels(step, carry):
        lanes = pl.ds(pl.multiple_of(step * block, block), block)
        for low, high in zip(bounds[:-1], bounds[1:]):
            product = jnp.dot(
                conv_in[low * wide : high * wide, :], expand_ref[:, lanes],
                preferred_element_type=jnp.float32,
            )
            value = jax.nn.gelu(product, approximate=True).astype(jnp.bfloat16)
            expanded[low:high] = value.astype(jnp.float32).reshape(high - low, wide, block)
        expanded[0] = expanded[0] * flags[0]
        expanded[tall - 1] = expanded[tall - 1] * flags[1]
        expanded[:, col_count:, :] = expanded[:, col_count:, :] * side
        for half in range(block // LANES):
            inner = slice(half * LANES, (half + 1) * LANES)
            outer = pl.ds(pl.multiple_of(step * block + half * LANES, LANES), LANES)
            taps = [taps_ref[k : k + 1, outer] for k in range(9)]

            def rows_of(group, total):
                base = group * 4
                held = [expanded[base + k, :, inner] for k in range(6)]
                for k in range(4):
                    parts = [
                        held[k] * taps[side_step]
                        + held[k + 1] * taps[3 + side_step]
                        + held[k + 2] * taps[6 + side_step]
                        for side_step in range(3)
                    ]
                    summed = (
                        pltpu.roll(parts[0], 1, 0) + parts[1] + pltpu.roll(parts[2], wide - 1, 0)
                    )[:col_count]
                    deep = jax.nn.gelu(summed, approximate=True)
                    total = total + jnp.sum(deep.reshape(col_count // 8, 8, LANES), axis=0)
                    at = pl.ds(pl.multiple_of((base + k) * col_count, col_count), col_count)
                    o_ref[at, outer] = deep.astype(o_ref.dtype)
                return total

            total = lax.fori_loop(0, row_count // 4, rows_of, jnp.zeros((8, LANES), jnp.float32))
            sums_ref[:, outer] = jnp.sum(total, axis=0, keepdims=True)
        return carry

    lax.fori_loop(0, width // block, channels, 0)


def depthwise_stage(latent, conv_scale, conv_shift, expand_weight, depth_kernel):
    row_count, col_count, feats = latent.shape
    width = expand_weight.shape[1]
    row_at, col_at = lax.axis_index("row"), lax.axis_index("col")
    flags = jnp.stack(
        [row_at > 0, row_at < lax.axis_size("row") - 1, col_at > 0, col_at < lax.axis_size("col") - 1]
    ).astype(jnp.float32)
    tall = extended(latent, (("row", 0),), 1)
    count = lax.axis_size("col")
    ahead = [(i, i + 1) for i in range(count - 1)]
    left = lax.ppermute(tall[:, col_count - 1 :], "col", ahead)
    right = lax.ppermute(tall[:, :1], "col", [(b, a) for a, b in ahead])
    blank = jnp.zeros((row_count + 2, PAD - 2, feats), latent.dtype)
    ext = jnp.concatenate([tall, right, blank, left], axis=1).reshape(-1, feats)
    vmem = pl.BlockSpec(memory_space=pltpu.VMEM)
    block = 256
    return pl.pallas_call(
        functools.partial(conv_kernel, row_count, col_count),
        out_shape=(
            jax.ShapeDtypeStruct((row_count * col_count, width), jnp.bfloat16),
            jax.ShapeDtypeStruct((1, width), jnp.float32),
        ),
        in_specs=[pl.BlockSpec(memory_space=pltpu.SMEM)] + [vmem] * 5,
        out_specs=(vmem, vmem),
        scratch_shapes=[
            pltpu.VMEM(ext.shape, jnp.bfloat16),
            pltpu.VMEM((row_count + 2, col_count + PAD, block), jnp.float32),
        ],
        compiler_params=pltpu.CompilerParams(vmem_limit_bytes=20 * 1024 * 1024),
        name="conv_stage",
    )(flags, ext, conv_scale[None], conv_shift[None], expand_weight, depth_kernel)


def per_device(
    latent,
    conv_scale,
    conv_shift,
    expand_weight,
    depth_kernel,
    squeeze_down,
    squeeze_up,
    project_weight,
    block_gain,
    block_projection,
    block_output,
    block_table,
    first_gain,
    first_expand,
    first_reduce,
    grid_gain,
    grid_projection,
    grid_output,
    grid_table,
    second_gain,
    second_expand,
    second_reduce,
):
    row_devices = lax.axis_size("row")
    col_devices = lax.axis_size("col")
    row_count, col_count, channels = latent.shape
    if compact(row_count, col_count) and squeeze_up.shape[0] == LANES:
        return whole_block(
            latent, conv_scale, conv_shift, depth_kernel, (block_table, grid_table),
            (block_gain, first_gain, grid_gain, second_gain),
            (expand_weight, squeeze_down, squeeze_up, project_weight),
            (block_projection, block_output, first_expand, first_reduce,
             grid_projection, grid_output, second_expand, second_reduce),
        )
    depthwise, local_sums = depthwise_stage(
        latent, conv_scale, conv_shift, expand_weight, depth_kernel
    )
    local_sums = local_sums.reshape(-1, LANES)
    channel_sums = axis_sum(axis_sum(local_sums, "row", 1), "col", 2).reshape(-1)
    pooled = channel_sums / (row_count * row_devices * col_count * col_devices)
    excite = squeeze_gate(pooled, squeeze_down, squeeze_up)
    gated = (depthwise.astype(jnp.float32) * excite).astype(jnp.bfloat16)
    conv_out = (
        latent.reshape(-1, channels).astype(jnp.float32)
        + jnp.dot(gated, project_weight, preferred_element_type=jnp.float32)
    ).astype(jnp.bfloat16).reshape(row_count, col_count, channels)

    def run_block(cells, layout, bias):
        return mixer(
            cells, layout, block_gain, block_projection, block_output, bias, first_gain,
            first_expand, first_reduce, block_table.shape[0],
        )

    def run_grid(cells, layout, bias):
        return mixer(
            cells, layout, grid_gain, grid_projection, grid_output, bias, second_gain,
            second_expand, second_reduce, grid_table.shape[0],
        )

    return split_sublayers(conv_out, run_block, run_grid, block_table, grid_table)


def solution(mesh):
    placed = (
        P("row", "col", None),
        P(),
        P(),
        P(),
        P(),
        P(),
        P(),
        P(),
        P(),
        P(),
        P(),
        P(),
        P(),
        P(),
        P(),
        P(),
        P(),
        P(),
        P(),
        P(),
        P(),
        P(),
    )
    return jax.shard_map(
        per_device, mesh=mesh, in_specs=placed, out_specs=P("row", "col", None), check_vma=False
    )
```

```python
import functools

import jax
import jax.numpy as jnp
import numpy as np
from jax import lax
from jax.experimental import pallas as pl
from jax.experimental.pallas import tpu as pltpu
from jax.sharding import PartitionSpec as P

WIN = 8
PAD = 8
QUAD = 4
LOG2E = 1.4426950408889634


def extended(cells, sides, width):
    for axis, dim in sides:
        count = lax.axis_size(axis)
        ends = count - 1
        head = lax.slice_in_dim(cells, 0, width, axis=dim)
        tail = lax.slice_in_dim(cells, cells.shape[dim] - width, cells.shape[dim], axis=dim)
        cells = jnp.concatenate(
            [
                lax.ppermute(tail, axis, [(i, (i + 1) % count) for i in range(ends)]),
                cells,
                lax.ppermute(head, axis, [((i + 1) % count, i) for i in range(ends)]),
            ],
            axis=dim,
        )
    return cells


def layer_norm_apply(values, norm_gain):
    widened = values.astype(jnp.float32)
    center = widened - jnp.mean(widened, axis=-1, keepdims=True)
    spread = jnp.mean(center * center, axis=-1, keepdims=True)
    return (center * lax.rsqrt(spread + 1e-05) * norm_gain).astype(jnp.bfloat16)


def position_bias(offset_bias_lookup):
    spots = offset_bias_lookup.shape[1]
    position = jnp.arange(WIN * WIN)
    down_pos = position // WIN
    across = position % WIN
    relative = (down_pos[:, None] - down_pos[None, :] + WIN - 1) * (2 * WIN - 1) + (
        across[:, None] - across[None, :] + WIN - 1
    )
    indicator_matrix = (relative[:, :, None] == jnp.arange(spots)[None, None, :]).astype(
        jnp.float32
    )
    return jnp.einsum(
        "bp,rjp->brj", offset_bias_lookup, indicator_matrix, precision=lax.Precision.HIGHEST
    )


def attend(triple, pos_bias):
    window_count, tokens, three_width = triple.shape
    feature_width = three_width // 3
    head_count = pos_bias.shape[0]
    head_size = feature_width // head_count
    queries = triple[..., :feature_width].reshape(window_count, tokens, head_count, head_size)
    key_row_list = triple[..., feature_width : 2 * feature_width].reshape(
        window_count, tokens, head_count, head_size
    )
    values = triple[..., 2 * feature_width :].reshape(window_count, tokens, head_count, head_size)
    scores = (
        jnp.einsum("nqhd,nkhd->nhqk", queries, key_row_list, preferred_element_type=jnp.float32)
        * head_size ** (-0.5)
        + pos_bias[None]
    )
    row_max = jnp.max(scores, axis=-1, keepdims=True)
    weight_tensors = jnp.exp(scores - row_max)
    attention_weight_map = (
        weight_tensors / jnp.sum(weight_tensors, axis=-1, keepdims=True)
    ).astype(jnp.bfloat16)
    mixed = jnp.einsum(
        "nhqk,nkhd->nqhd", attention_weight_map, values, preferred_element_type=jnp.float32
    )
    return mixed.astype(jnp.bfloat16).reshape(window_count, tokens, feature_width)


def attention_sublayer(windows, norm_gain, in_weight, out_weight, pos_bias):
    normed = layer_norm_apply(windows, norm_gain)
    triple = jnp.dot(normed, in_weight, preferred_element_type=jnp.float32).astype(jnp.bfloat16)
    mixed = attend(triple, pos_bias)
    return (
        windows.astype(jnp.float32) + jnp.dot(mixed, out_weight, preferred_element_type=jnp.float32)
    ).astype(jnp.bfloat16)


def feed_forward(values, norm_gain, in_weight, out_weight):
    normed = layer_norm_apply(values, norm_gain)
    hidden = jax.nn.gelu(
        jnp.dot(normed, in_weight, preferred_element_type=jnp.float32), approximate=True
    ).astype(jnp.bfloat16)
    return (
        values.astype(jnp.float32) + jnp.dot(hidden, out_weight, preferred_element_type=jnp.float32)
    ).astype(jnp.bfloat16)


def to_blocks(field):
    row_count, col_count, feats = field.shape
    return (
        field.reshape(row_count // WIN, WIN, col_count // WIN, WIN, feats)
        .transpose(0, 2, 1, 3, 4)
        .reshape(-1, WIN * WIN, feats)
    )


def from_blocks(windows, row_count, col_count):
    feats = windows.shape[-1]
    return (
        windows.reshape(row_count // WIN, col_count // WIN, WIN, WIN, feats)
        .transpose(0, 2, 1, 3, 4)
        .reshape(row_count, col_count, feats)
    )


def axis_shape(length, devices):
    fold = max(1, WIN // devices)
    rest = length // max(devices, WIN)
    span = min(devices, WIN)
    return (fold, rest, span, devices // span)


def grid_layout(field):
    row_devices = lax.axis_size("row")
    col_devices = lax.axis_size("col")
    row_count, col_count, feats = field.shape
    row_fold, row_rest, row_span, row_hop = axis_shape(row_count, row_devices)
    col_fold, col_rest, col_span, col_hop = axis_shape(col_count, col_devices)
    ordered_layout = field.reshape(
        row_fold, row_devices, row_rest, col_fold, col_devices, col_rest, feats
    )
    flat = ordered_layout.transpose(1, 4, 0, 2, 3, 5, 6).reshape(
        row_devices * col_devices, row_fold, row_rest, col_fold, col_rest, feats
    )
    flat = lax.all_to_all(flat, ("row", "col"), split_axis=0, concat_axis=0, tiled=True)
    moved = flat.reshape(
        row_devices, col_devices, row_fold, row_rest, col_fold, col_rest, feats
    ).transpose(2, 0, 3, 4, 1, 5, 6)
    moved = moved.reshape(
        row_fold, row_span, row_hop, row_rest, col_fold, col_span, col_hop, col_rest, feats
    )
    return moved.transpose(2, 3, 6, 7, 1, 0, 5, 4, 8).reshape(-1, WIN * WIN, feats)


def spatial_layout(windows, row_count, col_count):
    row_devices = lax.axis_size("row")
    col_devices = lax.axis_size("col")
    feats = windows.shape[-1]
    row_fold, row_rest, row_span, row_hop = axis_shape(row_count, row_devices)
    col_fold, col_rest, col_span, col_hop = axis_shape(col_count, col_devices)
    gridded = windows.reshape(
        row_hop, row_rest, col_hop, col_rest, row_span, row_fold, col_span, col_fold, feats
    )
    ordered_layout = gridded.transpose(5, 4, 0, 1, 7, 6, 2, 3, 8).reshape(
        row_fold, row_devices, row_rest, col_fold, col_devices, col_rest, feats
    )
    flat = ordered_layout.transpose(1, 4, 0, 2, 3, 5, 6).reshape(
        row_devices * col_devices, row_fold, row_rest, col_fold, col_rest, feats
    )
    flat = lax.all_to_all(flat, ("row", "col"), split_axis=0, concat_axis=0, tiled=True)
    moved = flat.reshape(
        row_devices, col_devices, row_fold, row_rest, col_fold, col_rest, feats
    ).transpose(2, 0, 3, 4, 1, 5, 6)
    return moved.reshape(row_count, col_count, feats)


def squeeze_gate(pooled, squeeze_down, squeeze_up):
    reduced = jax.nn.silu(
        jnp.dot(pooled[None, :], squeeze_down.astype(jnp.float32), precision=lax.Precision.HIGHEST)
    )
    return jax.nn.sigmoid(
        jnp.dot(reduced, squeeze_up.astype(jnp.float32), precision=lax.Precision.HIGHEST)
    )[0]


def axis_sum_kernel(axis, count, x_ref, o_ref, slots, send_sem, recv_sem):
    me = lax.axis_index(axis)
    barrier = pltpu.get_barrier_semaphore()
    peers = [lax.rem(me + step, count) for step in range(1, count)]
    for peer in peers:
        pl.semaphore_signal(
            barrier, inc=1, device_id={axis: peer}, device_id_type=pl.DeviceIdType.MESH
        )
    pl.semaphore_wait(barrier, count - 1)
    copies = []
    for step, peer in enumerate(peers):
        copy = pltpu.make_async_remote_copy(
            src_ref=x_ref,
            dst_ref=slots.at[step],
            send_sem=send_sem.at[step],
            recv_sem=recv_sem.at[step],
            device_id={axis: peer},
            device_id_type=pl.DeviceIdType.MESH,
        )
        copy.start()
        copies.append(copy)
    for copy in copies:
        copy.wait()
    total = x_ref[...]
    for step in range(count - 1):
        total = total + slots[step]
    o_ref[...] = total


def axis_sum(values, axis, collective_id):
    count = lax.axis_size(axis)
    if count == 1:
        return values
    return pl.pallas_call(
        functools.partial(axis_sum_kernel, axis, count),
        out_shape=jax.ShapeDtypeStruct(values.shape, values.dtype),
        in_specs=[pl.BlockSpec(memory_space=pltpu.VMEM)],
        out_specs=pl.BlockSpec(memory_space=pltpu.VMEM),
        scratch_shapes=[
            pltpu.VMEM((count - 1,) + values.shape, values.dtype),
            pltpu.SemaphoreType.DMA((count - 1,)),
            pltpu.SemaphoreType.DMA((count - 1,)),
        ],
        compiler_params=pltpu.CompilerParams(
            collective_id=collective_id, has_side_effects=True, vmem_limit_bytes=4 * 1024 * 1024
        ),
        name="axis_sum_" + axis,
    )(values)


LANES = 128
GROUP = 256


def normed_rows(widened, gain):
    center = widened - jnp.mean(widened, axis=-1, keepdims=True)
    spread = jnp.mean(center * center, axis=-1, keepdims=True)
    return (center * lax.rsqrt(spread + 1e-05) * gain).astype(jnp.bfloat16)


def mixer_kernel(
    layout, head_size, x_ref, gain_ref, bias_ref, late_gain_ref, proj_hbm, out_hbm, up_hbm, down_hbm,
    o_ref, triple, heads, proj_ref, out_w_ref, up_ref, down_ref, sems,
):
    kind, across = layout
    rows_total, feats = x_ref.shape
    tokens = WIN * WIN
    window_count = rows_total // tokens
    slabs = feats // LANES
    per_slab = LANES // head_size
    moves = [
        pltpu.make_async_copy(src, dst, sems.at[k])
        for k, (src, dst) in enumerate(
            ((proj_hbm, proj_ref), (out_hbm, out_w_ref), (up_hbm, up_ref), (down_hbm, down_ref))
        )
    ]
    moves[0].start()
    moves[0].wait()
    for move in moves[1:]:
        move.start()
    chunk = 256

    def project(step, carry):
        rows = pl.ds(pl.multiple_of(step * chunk, chunk), chunk)
        normed = normed_rows(x_ref[rows, :].astype(jnp.float32), gain_ref[...])
        for part in range(3 * slabs // 2):
            product = jnp.dot(
                normed, proj_ref[:, part * GROUP : (part + 1) * GROUP],
                preferred_element_type=jnp.float32,
            ).astype(jnp.bfloat16).astype(jnp.float32)
            triple[2 * part, rows, :] = product[:, :LANES]
            triple[2 * part + 1, rows, :] = product[:, LANES:]
        return carry

    lax.fori_loop(0, rows_total // chunk, project, 0)

    def places(window):
        if kind == "strided":
            return [pl.ds(window, tokens, stride=across)]
        per_row = across // WIN
        base = (window // per_row) * (WIN * across) + (window % per_row) * WIN
        return [pl.ds(pl.multiple_of(base + r * across, WIN), WIN) for r in range(WIN)]

    lane = lax.broadcasted_iota(jnp.int32, (tokens, GROUP), 1)
    head_of = (lane % LANES) // head_size
    scale = head_size ** (-0.5)

    def one_window(window):
        spots = places(window)

        def fetch(slab):
            pieces = [triple[slab, spot, :] for spot in spots]
            whole = pieces[0] if len(pieces) == 1 else jnp.concatenate(pieces, axis=0)
            return whole

        empty = jnp.zeros((tokens, LANES), jnp.bfloat16)
        for group in range(slabs // 2):
            first, second = 2 * group, 2 * group + 1
            query_0 = fetch(first).astype(jnp.bfloat16)
            query_1 = fetch(second).astype(jnp.bfloat16)
            keys = jnp.concatenate([fetch(slabs + first), fetch(slabs + second)], axis=1)
            vals = jnp.concatenate([fetch(2 * slabs + first), fetch(2 * slabs + second)], axis=1)
            block_q = jnp.concatenate(
                [
                    jnp.concatenate([query_0, empty], axis=1),
                    jnp.concatenate([empty, query_1], axis=1),
                ],
                axis=0,
            )
            block_k = jnp.concatenate(
                [jnp.where(head_of == j, keys, 0.0).astype(jnp.bfloat16) for j in range(per_slab)],
                axis=0,
            )
            block_v = jnp.concatenate(
                [jnp.where(head_of == j, vals, 0.0).astype(jnp.bfloat16) for j in range(per_slab)],
                axis=0,
            )
            scores = lax.dot_general(
                block_k, block_q, (((1,), (1,)), ((), ())), preferred_element_type=jnp.float32
            )
            scores = (scores * scale + bias_ref[group]).reshape(per_slab, tokens, 2 * tokens)
            weights = jnp.exp(scores - jnp.max(scores, axis=1, keepdims=True))
            shares = weights * (1.0 / jnp.sum(weights, axis=1, keepdims=True))
            shares = shares.reshape(per_slab * tokens, 2 * tokens).astype(jnp.bfloat16)
            mixed = lax.dot_general(
                shares, block_v, (((0,), (0,)), ((), ())), preferred_element_type=jnp.float32
            )
            for slab, part in (
                (first, mixed[:tokens, :LANES]), (second, mixed[tokens:, LANES:])
            ):
                if len(spots) == 1:
                    heads[slab, spots[0], :] = part
                else:
                    for r, spot in enumerate(spots):
                        heads[slab, spot, :] = part[r * WIN : (r + 1) * WIN]

    def attend_pair(step, carry):
        one_window(2 * step)
        one_window(2 * step + 1)
        return carry

    lax.fori_loop(0, window_count // 2, attend_pair, 0)
    for move in moves[1:]:
        move.wait()
    hidden_width = up_ref.shape[1]
    tile = 512

    def feed(step, carry):
        rows = pl.ds(pl.multiple_of(step * chunk, chunk), chunk)
        mixed = jnp.concatenate([heads[s, rows, :] for s in range(slabs)], axis=1).astype(jnp.bfloat16)
        value = (
            x_ref[rows, :].astype(jnp.float32)
            + jnp.dot(mixed, out_w_ref[...], preferred_element_type=jnp.float32)
        ).astype(jnp.bfloat16).astype(jnp.float32)
        normed = normed_rows(value, late_gain_ref[...])
        for k in range(hidden_width // tile):
            part = slice(k * tile, (k + 1) * tile)
            hidden = jax.nn.gelu(
                jnp.dot(normed, up_ref[:, part], preferred_element_type=jnp.float32),
                approximate=True,
            ).astype(jnp.bfloat16)
            value = value + jnp.dot(hidden, down_ref[part, :], preferred_element_type=jnp.float32)
        o_ref[rows, :] = value.astype(jnp.bfloat16)
        return carry

    lax.fori_loop(0, rows_total // chunk, feed, 0)


def mixer(x, layout, gain, in_weight, out_weight, bias, late_gain, up, down, heads_count):
    rows, feats = x.shape
    vmem = pl.BlockSpec(memory_space=pltpu.VMEM)
    hbm = pl.BlockSpec(memory_space=pltpu.HBM)
    flops = 8 * rows * feats * (4 * feats + 2 * up.shape[1])
    return pl.pallas_call(
        functools.partial(mixer_kernel, layout, feats // heads_count),
        out_shape=jax.ShapeDtypeStruct((rows, feats), jnp.bfloat16),
        in_specs=[vmem] * 4 + [hbm] * 4,
        out_specs=vmem,
        scratch_shapes=[
            pltpu.VMEM((3 * feats // LANES, rows, LANES), jnp.float32),
            pltpu.VMEM((feats // LANES, rows, LANES), jnp.float32),
            pltpu.VMEM(in_weight.shape, jnp.bfloat16),
            pltpu.VMEM(out_weight.shape, jnp.bfloat16),
            pltpu.VMEM(up.shape, jnp.bfloat16),
            pltpu.VMEM(down.shape, jnp.bfloat16),
            pltpu.SemaphoreType.DMA((4,)),
        ],
        compiler_params=pltpu.CompilerParams(vmem_limit_bytes=60 * 1024 * 1024),
        cost_estimate=pl.CostEstimate(
            flops=flops, bytes_accessed=12 * 1024 * 1024, transcendentals=0
        ),
        name="mixer_" + layout[0],
    )(x, gain[None], bias, late_gain[None], in_weight, out_weight, up, down)


def key_major_bias(table, down, across):
    head_count, spots = table.shape
    relative = (down[None, :] - down[:, None] + WIN - 1) * (2 * WIN - 1) + (
        across[None, :] - across[:, None] + WIN - 1
    )
    tokens = WIN * WIN
    chosen = (jnp.arange(spots)[:, None] == jnp.asarray(relative.reshape(-1))[None, :]).astype(
        jnp.float32
    )
    spread = jnp.dot(table, chosen, precision=lax.Precision.HIGHEST)
    return (
        spread.reshape(head_count // 8, 2, 4, tokens, tokens)
        .transpose(0, 2, 3, 1, 4)
        .reshape(head_count // 8, 4 * tokens, 2 * tokens)
    )


def split_sublayers(conv_out, run_block, run_grid, block_table, grid_table):
    row_devices = lax.axis_size("row")
    col_devices = lax.axis_size("col")
    row_count, col_count, feats = conv_out.shape
    plain = np.arange(WIN * WIN)
    block_bias = key_major_bias(block_table, plain // WIN, plain % WIN)
    if row_devices > WIN or col_devices > WIN:
        section = run_block(conv_out.reshape(-1, feats), ("blocks", col_count), block_bias)
        windows = grid_layout(section.reshape(row_count, col_count, feats))
        count = windows.shape[0]
        bias = key_major_bias(grid_table, plain // WIN, plain % WIN)
        out = run_grid(windows.transpose(1, 0, 2).reshape(-1, feats), ("strided", count), bias)
        out = out.reshape(WIN * WIN, count, feats).transpose(1, 0, 2)
        return spatial_layout(out, row_count, col_count)
    devices = row_devices * col_devices
    row_fold, col_fold = WIN // row_devices, WIN // col_devices
    row_rest, col_rest = row_count // row_fold, col_count // col_fold
    parts = row_rest // WIN
    count = WIN * col_rest // devices
    pieces = col_rest // count
    order = np.arange(WIN * WIN).reshape(row_devices, col_devices, row_fold, col_fold)
    at = np.indices(order.shape).reshape(4, -1)
    grid_bias = key_major_bias(grid_table, at[0] * row_fold + at[2], at[1] * col_fold + at[3])
    strips = conv_out.reshape(row_fold, parts, WIN, col_count, feats)
    results = []
    for part in range(parts):
        section = run_block(
            strips[:, part].reshape(-1, feats), ("blocks", col_count), block_bias
        )
        sent = (
            section.reshape(row_fold, WIN, col_fold, pieces, count, feats)
            .transpose(1, 3, 0, 2, 4, 5)
            .reshape(devices, row_fold * col_fold * count, feats)
        )
        got = lax.all_to_all(sent, ("row", "col"), split_axis=0, concat_axis=0, tiled=True)
        out = run_grid(got.reshape(-1, feats), ("strided", count), grid_bias)
        back = lax.all_to_all(
            out.reshape(devices, -1, feats), ("row", "col"), split_axis=0, concat_axis=0, tiled=True
        )
        results.append(
            back.reshape(WIN, pieces, row_fold, col_fold, count, feats)
            .transpose(2, 0, 3, 1, 4, 5)
            .reshape(row_fold, WIN, col_count, feats)
        )
    return jnp.stack(results, axis=1).reshape(row_count, col_count, feats)


def device_of(flat, columns):
    return {"row": lax.div(flat, columns), "col": lax.rem(flat, columns)}


CORNERS = ((-1, -1), (-1, 1), (1, -1), (1, 1))


def split_parts(values):
    high = values.astype(jnp.bfloat16)
    rest = values - high.astype(jnp.float32)
    middle = rest.astype(jnp.bfloat16)
    low = (rest - middle.astype(jnp.float32)).astype(jnp.bfloat16)
    return high, middle, low


def exact_rows(values, weight):
    stacked = jnp.concatenate([p.astype(jnp.float32) for p in split_parts(values)], axis=0)
    product = jnp.dot(
        stacked.astype(jnp.bfloat16), weight[...], preferred_element_type=jnp.float32
    )
    return jnp.sum(product, axis=0, keepdims=True)


def twice_gelu(x):
    inner = x * (0.7978845608028654 + (0.7978845608028654 * 0.044715) * (x * x))
    return x + x * jnp.tanh(inner)


def block_kernel(
    shape, head_size, ready, latent, scale_in, shift_in, taps_in, block_table, grid_table,
    gain_0, gain_1, gain_2, gain_3,
    h0, h1, h2, h3, w0, w1, w2, w3, w4, w5, w6, w7, o_ref,
    u0, u1, u2, u3, triple, heads, v0, v1, v2, v3, v4, v5, v6, v7,
    section, got, output, back, edges, halo, corner, conv_in, halo_in, expanded, deep_ref,
    sums, slots, excite_ref, padded, block_bias, grid_bias, score_ref, share_ref, half_taps,
    weight_sem, send_sem, recv_sem, halo_send, halo_recv, sum_send, sum_recv,
):
    parts, pieces, rows_n, columns = shape
    devices = rows_n * columns
    row_count, col_count, feats = latent.shape
    width = u0.shape[1]
    slabs = feats // LANES
    per_slab = LANES // head_size
    tokens = WIN * WIN
    message = section.shape[1]
    folds = message // WIN
    chunk = 256
    batch = chunk // message
    halves = devices // batch
    part_rows = devices * message
    wide = col_count + PAD
    fold_rows = row_count // folds
    row_at, col_at = lax.axis_index("row"), lax.axis_index("col")
    me = row_at * columns + col_at
    mesh_ids = pl.DeviceIdType.MESH
    barrier = pltpu.get_barrier_semaphore()

    def greet(step, carry):
        pl.semaphore_signal(
            barrier, inc=1, device_id=device_of(lax.rem(me + step, devices), columns),
            device_id_type=mesh_ids,
        )
        return carry

    lax.fori_loop(1, devices, greet, 0)
    moves = [
        pltpu.make_async_copy(src, dst, weight_sem.at[k])
        for k, (src, dst) in enumerate(
            zip(
                (h0, h1, h2, h3, w0, w1, w2, w3, w4, w5, w6, w7),
                (u0, u1, u2, u3, v0, v1, v2, v3, v4, v5, v6, v7),
            )
        )
    ]
    for move in moves:
        move.start()
    ready()

    near = {
        (down, side): jnp.logical_and(
            jnp.logical_and(row_at + down >= 0, row_at + down < rows_n),
            jnp.logical_and(col_at + side >= 0, col_at + side < columns),
        )
        for down in (-1, 0, 1)
        for side in (-1, 0, 1)
    }
    for side, block, inner in ((0, 0, 0), (1, col_count - message, message - 1)):
        for group in range(row_count // 8):
            cells = latent[8 * group : 8 * group + 8, block : block + message, :]
            edges[side, 8 * group : 8 * group + 8, :] = (
                cells.astype(jnp.float32)[:, inner, :].astype(jnp.bfloat16)
            )
    sides = ((-1, 0), (1, 0), (0, -1), (0, 1))
    for k, way in enumerate(sides):

        @pl.when(jnp.logical_not(near[way]))
        def _(k=k):
            halo[k] = jnp.zeros(halo.shape[1:], halo.dtype)

    for k, way in enumerate(CORNERS):

        @pl.when(jnp.logical_not(near[way]))
        def _(k=k):
            corner[k] = jnp.zeros(corner.shape[1:], corner.dtype)

    for group in range(row_count // 8):
        cells = latent[8 * group : 8 * group + 8].reshape(8 * col_count, feats)
        conv_in[8 * group * col_count : 8 * (group + 1) * col_count, :] = (
            cells.astype(jnp.float32) * scale_in[...] + shift_in[...]
        ).astype(jnp.bfloat16)
    half_taps[...] = 0.5 * taps_in[...]

    def outgoing(k):
        if k < 4:
            down, side = sides[k]
            src = (
                latent.at[0], latent.at[row_count - 1], edges.at[0], edges.at[1]
            )[k]
            dst = halo.at[k ^ 1]
        else:
            down, side = CORNERS[k - 4]
            line = 0 if down < 0 else row_count - 1
            start = 0 if side < 0 else col_count - message
            src = latent.at[line, pl.ds(start, message)]
            dst = corner.at[7 - k]
        return pltpu.make_async_remote_copy(
            src_ref=src, dst_ref=dst, send_sem=halo_send.at[k], recv_sem=halo_recv.at[k],
            device_id={"row": row_at + down, "col": col_at + side}, device_id_type=mesh_ids,
        )

    moves[0].wait()
    block = 256

    def expand(step, carry):
        lanes = pl.ds(pl.multiple_of(step * block, block), block)
        for group in range(row_count // 8):
            product = jnp.dot(
                conv_in[8 * group * col_count : 8 * (group + 1) * col_count, :], u0[:, lanes],
                preferred_element_type=jnp.float32,
            )
            value = twice_gelu(product.astype(jnp.bfloat16)).astype(jnp.float32)
            for r in range(8):
                start = PAD + (1 + 8 * group + r) * wide
                for half in range(block // LANES):
                    expanded[step * (block // LANES) + half, start : start + col_count, :] = value[
                        r * col_count : (r + 1) * col_count, half * LANES : (half + 1) * LANES
                    ]
        return carry

    lax.fori_loop(0, width // block // 2, expand, 0)
    pl.semaphore_wait(barrier, devices - 1)
    ways = sides + CORNERS
    for k, way in enumerate(ways):

        @pl.when(near[way])
        def _(k=k):
            outgoing(k).start()

    lax.fori_loop(width // block // 2, width // block, expand, 0)
    for k, way in enumerate(ways):
        opposite = (-way[0], -way[1])
        src_k = ways.index(opposite)

        @pl.when(near[way])
        def _(k=k, src_k=src_k):
            target = halo.at[k] if k < 4 else corner.at[k - 4]
            pltpu.make_async_copy(target, target, halo_recv.at[src_k]).wait()

    picked = [
        corner[k].astype(jnp.float32)[(message - 1 if side < 0 else 0) :][:1]
        for k, (_, side) in enumerate(CORNERS)
    ]
    picked = jnp.concatenate(picked + [jnp.zeros((message - 4, feats), jnp.float32)], axis=0)
    around = 2 * (row_count + col_count)
    for k, (start, size) in enumerate(
        (
            (0, col_count), (col_count, col_count), (2 * col_count, row_count),
            (2 * col_count + row_count, row_count),
        )
    ):
        halo_in[start : start + size, :] = (
            halo[k].astype(jnp.float32) * scale_in[...] + shift_in[...]
        ).astype(jnp.bfloat16)
    halo_in[around:, :] = (picked * scale_in[...] + shift_in[...]).astype(jnp.bfloat16)
    tall = row_count + 2

    def expand_halo(step, carry):
        lanes = pl.ds(pl.multiple_of(step * block, block), block)
        product = jnp.dot(halo_in[...], u0[:, lanes], preferred_element_type=jnp.float32)
        value = twice_gelu(product.astype(jnp.bfloat16)).astype(jnp.float32)
        up = jnp.where(near[(-1, 0)], value[:col_count], 0.0)
        low = jnp.where(near[(1, 0)], value[col_count : 2 * col_count], 0.0)
        left = jnp.where(near[(0, -1)], value[2 * col_count : 2 * col_count + row_count], 0.0)
        right = jnp.where(near[(0, 1)], value[2 * col_count + row_count : around], 0.0)
        for half in range(block // LANES):
            inner = slice(half * LANES, (half + 1) * LANES)
            outer = step * (block // LANES) + half
            last = PAD + (tall - 1) * wide
            expanded[outer, PAD : PAD + col_count, :] = up[:, inner]
            expanded[outer, last : last + col_count, :] = low[:, inner]
            expanded[outer, pl.ds(PAD + wide + col_count, row_count, stride=wide), :] = right[:, inner]
            expanded[outer, pl.ds(PAD + wide - 1, row_count, stride=wide), :] = left[:, inner]
            for k, way in enumerate(CORNERS):
                row = (PAD if way[0] < 0 else last) + (-1 if way[1] < 0 else col_count)
                expanded[outer, row : row + 1, :] = jnp.where(
                    near[way], value[around + k : around + k + 1, inner], 0.0
                )
        return carry

    lax.fori_loop(0, width // block, expand_halo, 0)

    def depth(step, carry):
        lanes = pl.ds(pl.multiple_of(step * LANES, LANES), LANES)
        taps = [half_taps[k : k + 1, lanes].astype(jnp.bfloat16) for k in range(9)]

        def pair_of_rows(group, total):
            def cells(k, side):
                lines = []
                for fold in range(folds):
                    base = pl.multiple_of((fold * fold_rows + 2 * group) * wide, 8)
                    lines.append(expanded[step, pl.ds(base + (PAD + k * wide + side), col_count), :])
                return jnp.concatenate(
                    [
                        line[piece * WIN : (piece + 1) * WIN]
                        for piece in range(pieces)
                        for line in lines
                    ],
                    axis=0,
                ).astype(jnp.bfloat16)

            held = [[cells(k, side) for side in (-1, 0, 1)] for k in range(4)]
            part, down = lax.div(2 * group, WIN), lax.rem(2 * group, WIN)
            for k in range(2):
                columns_of = [
                    held[k][side] * taps[side]
                    + held[k + 1][side] * taps[3 + side]
                    + held[k + 2][side] * taps[6 + side]
                    for side in range(3)
                ]
                value = twice_gelu(columns_of[0] + columns_of[2] + columns_of[1])
                total = total + jnp.sum(
                    value.astype(jnp.float32).reshape(-1, 8, LANES), axis=0
                )
                for piece in range(pieces):
                    at = part * devices + piece * WIN + down + k
                    deep_ref[at, :, lanes] = value[piece * message : (piece + 1) * message]
            return total

        sums[:, lanes] = lax.fori_loop(
            0, fold_rows // 2, pair_of_rows, jnp.zeros((8, LANES), jnp.float32), unroll=2
        )
        return carry

    lax.fori_loop(0, width // LANES, depth, 0)
    for move in moves[1:4]:
        move.wait()
    slots[me] = exact_rows(0.5 * sums[...], u1)

    def share(step, carry):
        pltpu.make_async_remote_copy(
            src_ref=slots.at[me], dst_ref=slots.at[me], send_sem=sum_send, recv_sem=sum_recv,
            device_id=device_of(lax.rem(me + step, devices), columns), device_id_type=mesh_ids,
        ).start()
        return carry

    lax.fori_loop(1, devices, share, 0)
    span = 2 * WIN
    spot = lax.broadcasted_iota(jnp.int32, (slabs * per_slab, span * span), 1)
    place = lax.broadcasted_iota(jnp.int32, (WIN, LANES), 1)
    for table, bias in ((block_table, block_bias), (grid_table, grid_bias)):
        padded[...] = jnp.zeros(padded.shape, jnp.float32)
        padded[:, : table.shape[1]] = table[...] * LOG2E
        flat = padded[...]
        spread = jnp.zeros(flat.shape, jnp.float32)
        for down in range(2 * WIN - 1):
            moved = flat if down == 0 else pltpu.roll(flat, down, 1)
            spread = jnp.where(spot // span == down, moved, spread)
        for head in range(slabs * per_slab // 2):
            group, j = head // per_slab, head % per_slab
            pair = [
                jnp.broadcast_to(spread[h : h + 1], (WIN, span * span))
                for h in (group * 2 * per_slab + j, group * 2 * per_slab + per_slab + j)
            ]
            for kr in range(WIN):
                shift = span * kr - (span * (WIN - 1) + WIN - 1)
                first, second = [
                    pltpu.roll(
                        pair[s], (shift + WIN * s) % (span * span), 1, stride=1, stride_axis=0
                    )[:, :LANES]
                    for s in range(2)
                ]
                start = j * tokens + kr * WIN
                bias[group, start : start + WIN, :] = jnp.where(place % span < WIN, first, second)
    arrivals = slots.at[pl.ds(0, devices - 1)]
    pltpu.make_async_copy(arrivals, arrivals, sum_recv).wait()
    pooled = jnp.sum(slots[...].reshape(devices, LANES), axis=0, keepdims=True) / (
        row_count * rows_n * col_count * columns
    )
    reduced = jax.nn.silu(pooled)
    spare = jnp.zeros((7, LANES), jnp.float32)
    excite_ref[...] = 0.5 * jax.nn.sigmoid(exact_rows(jnp.concatenate([reduced, spare], axis=0), u2))
    for move in moves[4:8]:
        move.wait()

    def project(values, rows, gain_ref, weight):
        normed = normed_rows(values.astype(jnp.float32), gain_ref[...])
        for part in range(3 * slabs // 2):
            product = jnp.dot(
                normed, weight[:, part * GROUP : (part + 1) * GROUP],
                preferred_element_type=jnp.float32,
            ).astype(jnp.bfloat16).astype(jnp.float32)
            triple[2 * part, rows, :] = product[:, :LANES]
            triple[2 * part + 1, rows, :] = product[:, LANES:]

    lane = lax.broadcasted_iota(jnp.int32, (tokens, GROUP), 1)
    masks = [
        jnp.where((lane % LANES) // head_size == j, 1.0, 0.0).astype(jnp.bfloat16)
        for j in range(per_slab)
    ]
    scale = head_size ** (-0.5) * LOG2E

    def attend_windows(windows, bias_ref):
        def spread(spots, slab, group):
            joined = jnp.concatenate(
                [
                    jnp.concatenate([triple[slab + 2 * group + k, spot, :] for spot in spots], axis=0)
                    for k in range(2)
                ],
                axis=1,
            ).astype(jnp.bfloat16)
            return jnp.concatenate([joined * mask for mask in masks], axis=0)

        empty = jnp.zeros((WIN, LANES), jnp.float32)
        chains = [(n, g) for n in range(len(windows)) for g in range(slabs // 2)]
        for at, (n, group) in enumerate(chains):
            spots = windows[n]
            left, right = [
                [triple[2 * group + k, spot, :] for spot in spots] for k in range(2)
            ]
            block_q = jnp.concatenate(
                [
                    jnp.concatenate([p for q in left for p in (q, empty)], axis=0),
                    jnp.concatenate([p for q in right for p in (empty, q)], axis=0),
                ],
                axis=1,
            ).astype(jnp.bfloat16)
            score_ref[at] = lax.dot_general(
                spread(spots, slabs, group), block_q, (((1,), (1,)), ((), ())),
                preferred_element_type=jnp.float32,
            )
        for at, (n, group) in enumerate(chains):
            scores = (score_ref[at] * scale + bias_ref[group]).reshape(
                per_slab, tokens, 2 * tokens
            )
            weights = jnp.exp2(scores - jnp.max(scores, axis=1, keepdims=True))
            shares = weights * (1.0 / jnp.sum(weights, axis=1, keepdims=True))
            share_ref[at] = shares.reshape(per_slab * tokens, 2 * tokens).astype(jnp.bfloat16)
        for at, (n, group) in enumerate(chains):
            mixed = lax.dot_general(
                share_ref[at], spread(windows[n], 2 * slabs, group), (((0,), (0,)), ((), ())),
                preferred_element_type=jnp.float32,
            )
            for r, spot in enumerate(windows[n]):
                start = 2 * r * WIN
                heads[2 * group, spot, :] = mixed[start : start + WIN, :LANES]
                heads[2 * group + 1, spot, :] = mixed[start + WIN : start + 2 * WIN, LANES:]

    def feed(values, rows, gain_ref, out_w, up, down):
        mixed = jnp.concatenate([heads[s, rows, :] for s in range(slabs)], axis=1).astype(jnp.bfloat16)
        value = (
            values.astype(jnp.float32)
            + jnp.dot(mixed, out_w[...], preferred_element_type=jnp.float32)
        ).astype(jnp.bfloat16).astype(jnp.float32)
        normed = normed_rows(value, gain_ref[...])
        tile = 512
        total = None
        for k in range(up.shape[1] // tile):
            part = slice(k * tile, (k + 1) * tile)
            hidden = twice_gelu(
                jnp.dot(normed, up[:, part], preferred_element_type=jnp.float32).astype(jnp.bfloat16)
            )
            product = jnp.dot(hidden, down[part, :], preferred_element_type=jnp.float32)
            total = product if total is None else total + product
        value = value + 0.5 * total
        return value.astype(jnp.bfloat16)

    def block_step(step, carry):
        part, half = lax.div(step, halves), lax.rem(step, halves)
        whole = pl.ds(0, chunk)
        across = batch // WIN
        own = {}
        for down in range(WIN):
            for fold in range(folds):
                line = latent[
                    fold * fold_rows + part * WIN + down,
                    pl.ds(pl.multiple_of(half * (across * WIN), across * WIN), across * WIN), :,
                ].astype(jnp.float32)
                for piece in range(across):
                    own[piece, down, fold] = line[piece * WIN : (piece + 1) * WIN]
        own = jnp.concatenate([own[key] for key in sorted(own)], axis=0)
        for k in range(width // block):
            lanes = slice(k * block, (k + 1) * block)
            gated = (
                deep_ref[pl.ds(step * batch, batch), :, lanes].reshape(chunk, block).astype(jnp.float32)
                * excite_ref[:, lanes]
            ).astype(jnp.bfloat16)
            own = own + jnp.dot(gated, u3[lanes, :], preferred_element_type=jnp.float32)
        value = own.astype(jnp.bfloat16)
        conv_in[0:chunk, :] = value
        project(value, whole, gain_0, v0)

        attend_windows(
            [
                [pl.ds(piece * (WIN * message) + fold * WIN + r * message, WIN) for r in range(WIN)]
                for piece in range(across)
                for fold in range(folds)
            ],
            block_bias,
        )
        done = feed(conv_in[0:chunk, :], whole, gain_1, v1, v2, v3)
        section[pl.ds(step * batch, batch)] = done.reshape(batch, message, feats)

        def send(i, inner):
            at = lax.rem(i + me, batch)
            target = lax.rem(at, WIN) * pieces + half * across + lax.div(at, WIN)
            src, dst = section.at[step * batch + at], got.at[part * devices + me]

            @pl.when(target != me)
            def _():
                pltpu.make_async_remote_copy(
                    src_ref=src, dst_ref=dst, send_sem=send_sem.at[0, part],
                    recv_sem=recv_sem.at[0, part], device_id=device_of(target, columns),
                    device_id_type=mesh_ids,
                ).start()

            @pl.when(target == me)
            def _():
                pltpu.make_async_copy(src, dst, recv_sem.at[0, part]).start()

            return inner

        lax.fori_loop(0, batch, send, 0)
        return carry

    lax.fori_loop(0, parts * halves, block_step, 0)
    for move in moves[8:]:
        move.wait()
    slot = lax.rem(me, pieces) * WIN + lax.div(me, pieces)

    def arrived(buffer, kind, part):
        mail = buffer.at[pl.ds(part * devices, devices)]
        pltpu.make_async_copy(mail, mail, recv_sem.at[kind, part]).wait()

    def grid_step(part, carry):
        arrived(got, 0, part)

        def rows_of(half):
            return got[pl.ds(part * devices + half * batch, batch)].reshape(chunk, feats)

        for half in range(halves):
            project(rows_of(half), pl.ds(half * chunk, chunk), gain_2, v4)

        def attend_some(step, inner):
            attend_windows(
                [
                    [
                        pl.ds(r * columns * message + fold * WIN + QUAD * step + k, columns, stride=message)
                        for r in range(rows_n)
                        for fold in range(folds)
                    ]
                    for k in range(QUAD)
                ],
                grid_bias,
            )
            return inner

        lax.fori_loop(0, part_rows // tokens // QUAD, attend_some, 0)

        def feed_half(half, inner):
            rows = pl.ds(pl.multiple_of(half * chunk, chunk), chunk)
            done = feed(rows_of(half), rows, gain_3, v5, v6, v7)
            output[pl.ds(part * devices + half * batch, batch)] = done.reshape(batch, message, feats)

            def send(i, inner_2):
                target = half * batch + lax.rem(i + me, batch)
                src, dst = output.at[part * devices + target], back.at[part * devices + slot]

                @pl.when(target != me)
                def _():
                    pltpu.make_async_remote_copy(
                        src_ref=src, dst_ref=dst, send_sem=send_sem.at[1, part],
                        recv_sem=recv_sem.at[1, part], device_id=device_of(target, columns),
                        device_id_type=mesh_ids,
                    ).start()

                @pl.when(target == me)
                def _():
                    pltpu.make_async_copy(src, dst, recv_sem.at[1, part]).start()

                return inner_2

            lax.fori_loop(0, batch, send, 0)
            return inner

        lax.fori_loop(0, halves, feed_half, 0)
        return carry

    lax.fori_loop(0, parts, grid_step, 0)

    def finish(part, carry):
        arrived(back, 1, part)

        def put(down, inner):
            tiles = [
                back[part * devices + piece * WIN + down].astype(jnp.float32)
                for piece in range(pieces)
            ]
            for fold in range(folds):
                line = jnp.concatenate([t[fold * WIN : (fold + 1) * WIN] for t in tiles], axis=0)
                start = (fold * fold_rows + part * WIN + down) * col_count
                o_ref[pl.ds(pl.multiple_of(start, col_count), col_count), :] = line.astype(jnp.bfloat16)
            return inner

        return lax.fori_loop(0, WIN, put, carry)

    lax.fori_loop(0, parts, finish, 0)
    for kind, buffer in ((0, section), (1, output)):
        for part in range(parts):
            sent = buffer.at[pl.ds(part * devices, devices - 1)]
            pltpu.make_async_copy(sent, sent, send_sem.at[kind, part]).wait()
    pltpu.make_async_copy(arrivals, arrivals, sum_send).wait()
    for k, way in enumerate(ways):

        @pl.when(near[way])
        def _(k=k):
            target = halo.at[k] if k < 4 else corner.at[k - 4]
            pltpu.make_async_copy(target, target, halo_send.at[k]).wait()


def fetch_and_run(shape, head_size, count, latent, *refs):
    smalls, refs, held, sem = refs[:count], refs[count : -count - 1], refs[-count - 1 : -1], refs[-1]
    copies = [
        pltpu.make_async_copy(src, dst, sem.at[k]) for k, (src, dst) in enumerate(zip(smalls, held))
    ]
    for copy in copies:
        copy.start()

    def ready():
        for copy in copies:
            copy.wait()

    block_kernel(shape, head_size, ready, latent, *held, *refs)


def whole_block(latent, scale, shift, taps, tables, gains, front, weights):
    row_count, col_count, feats = latent.shape
    rows_n, columns = lax.axis_size("row"), lax.axis_size("col")
    devices = rows_n * columns
    parts, pieces = row_count // (2 * WIN), col_count // WIN
    heads_n = tables[0].shape[0]
    rows = row_count * col_count
    width = front[0].shape[1]
    message = rows // (parts * devices)
    around = 2 * (row_count + col_count) + message
    vmem = pl.BlockSpec(memory_space=pltpu.VMEM)
    hbm = pl.BlockSpec(memory_space=pltpu.HBM)
    half_type = jnp.bfloat16
    mail = pltpu.VMEM((parts * devices, message, feats), half_type)
    bias = pltpu.VMEM((heads_n // 8, 4 * WIN * WIN, 2 * WIN * WIN), jnp.float32)
    dma = pltpu.SemaphoreType.DMA
    smalls = (scale[None], shift[None], taps, *tables, *[g[None] for g in gains])
    return pl.pallas_call(
        functools.partial(
            fetch_and_run, (parts, pieces, rows_n, columns), feats // heads_n, len(smalls)
        ),
        out_shape=jax.ShapeDtypeStruct((rows, feats), half_type),
        in_specs=[vmem] + [hbm] * (len(smalls) + 12),
        out_specs=vmem,
        scratch_shapes=[pltpu.VMEM(w.shape, half_type) for w in front]
        + [
            pltpu.VMEM((3 * feats // LANES, rows // parts, LANES), jnp.float32),
            pltpu.VMEM((feats // LANES, rows // parts, LANES), jnp.float32),
        ]
        + [pltpu.VMEM(w.shape, half_type) for w in weights]
        + [
            mail, mail, mail, mail,
            pltpu.VMEM((2, row_count, feats), half_type),
            pltpu.VMEM((4, row_count, feats), half_type),
            pltpu.VMEM((4, message, feats), half_type),
            pltpu.VMEM((rows, feats), half_type),
            pltpu.VMEM((around, feats), half_type),
            pltpu.VMEM(
                (width // LANES, PAD + (row_count + 2) * (col_count + PAD), LANES), jnp.float32
            ),
            pltpu.VMEM((parts * devices, message, width), half_type),
            pltpu.VMEM((8, width), jnp.float32),
            pltpu.VMEM((devices, 1, LANES), jnp.float32),
            pltpu.VMEM((1, width), jnp.float32),
            pltpu.VMEM((heads_n, 4 * WIN * WIN), jnp.float32),
            bias, bias,
            pltpu.VMEM((QUAD * heads_n // 8, 4 * WIN * WIN, 2 * WIN * WIN), jnp.float32),
            pltpu.VMEM((QUAD * heads_n // 8, 4 * WIN * WIN, 2 * WIN * WIN), half_type),
            pltpu.VMEM(taps.shape, jnp.float32),
            dma((12,)), dma((2, parts)), dma((2, parts)), dma((8,)), dma((8,)), dma, dma,
        ]
        + [pltpu.VMEM(small.shape, jnp.float32) for small in smalls]
        + [dma((len(smalls),))],
        compiler_params=pltpu.CompilerParams(
            collective_id=3, has_side_effects=True, vmem_limit_bytes=54 * 1024 * 1024
        ),
        name="whole_block",
    )(
        latent, *smalls, *front, *weights
    ).reshape(latent.shape)


def compact(row_count, col_count):
    row_devices, col_devices = lax.axis_size("row"), lax.axis_size("col")
    return (
        2 * row_devices == WIN and col_devices == WIN
        and row_count % (2 * WIN) == 0 and col_count == WIN * row_devices
        and row_count == col_count
    )


def conv_kernel(
    row_count, col_count, flags, ext_ref, scale_ref, shift_ref, expand_ref, taps_ref,
    o_ref, sums_ref, conv_in, expanded,
):
    wide = col_count + PAD
    tall = row_count + 2
    width = expand_ref.shape[1]
    block = expanded.shape[-1]
    bounds = [8 * k for k in range(row_count // 8)] + [tall]
    for low, high in zip(bounds[:-1], bounds[1:]):
        rows = slice(low * wide, high * wide)
        conv_in[rows, :] = (
            ext_ref[rows, :].astype(jnp.float32) * scale_ref[...] + shift_ref[...]
        ).astype(jnp.bfloat16)
    spot = lax.broadcasted_iota(jnp.int32, (1, PAD, block), 1)
    side = jnp.where(spot == 0, flags[3], jnp.where(spot == PAD - 1, flags[2], 0.0))

    def channels(step, carry):
        lanes = pl.ds(pl.multiple_of(step * block, block), block)
        for low, high in zip(bounds[:-1], bounds[1:]):
            product = jnp.dot(
                conv_in[low * wide : high * wide, :], expand_ref[:, lanes],
                preferred_element_type=jnp.float32,
            )
            value = jax.nn.gelu(product, approximate=True).astype(jnp.bfloat16)
            expanded[low:high] = value.astype(jnp.float32).reshape(high - low, wide, block)
        expanded[0] = expanded[0] * flags[0]
        expanded[tall - 1] = expanded[tall - 1] * flags[1]
        expanded[:, col_count:, :] = expanded[:, col_count:, :] * side
        for half in range(block // LANES):
            inner = slice(half * LANES, (half + 1) * LANES)
            outer = pl.ds(pl.multiple_of(step * block + half * LANES, LANES), LANES)
            taps = [taps_ref[k : k + 1, outer] for k in range(9)]

            def rows_of(group, total):
                base = group * 4
                held = [expanded[base + k, :, inner] for k in range(6)]
                for k in range(4):
                    parts = [
                        held[k] * taps[side_step]
                        + held[k + 1] * taps[3 + side_step]
                        + held[k + 2] * taps[6 + side_step]
                        for side_step in range(3)
                    ]
                    summed = (
                        pltpu.roll(parts[0], 1, 0) + parts[1] + pltpu.roll(parts[2], wide - 1, 0)
                    )[:col_count]
                    deep = jax.nn.gelu(summed, approximate=True)
                    total = total + jnp.sum(deep.reshape(col_count // 8, 8, LANES), axis=0)
                    at = pl.ds(pl.multiple_of((base + k) * col_count, col_count), col_count)
                    o_ref[at, outer] = deep.astype(o_ref.dtype)
                return total

            total = lax.fori_loop(0, row_count // 4, rows_of, jnp.zeros((8, LANES), jnp.float32))
            sums_ref[:, outer] = jnp.sum(total, axis=0, keepdims=True)
        return carry

    lax.fori_loop(0, width // block, channels, 0)


def depthwise_stage(latent, conv_scale, conv_shift, expand_weight, depth_kernel):
    row_count, col_count, feats = latent.shape
    width = expand_weight.shape[1]
    row_at, col_at = lax.axis_index("row"), lax.axis_index("col")
    flags = jnp.stack(
        [row_at > 0, row_at < lax.axis_size("row") - 1, col_at > 0, col_at < lax.axis_size("col") - 1]
    ).astype(jnp.float32)
    tall = extended(latent, (("row", 0),), 1)
    count = lax.axis_size("col")
    ahead = [(i, i + 1) for i in range(count - 1)]
    left = lax.ppermute(tall[:, col_count - 1 :], "col", ahead)
    right = lax.ppermute(tall[:, :1], "col", [(b, a) for a, b in ahead])
    blank = jnp.zeros((row_count + 2, PAD - 2, feats), latent.dtype)
    ext = jnp.concatenate([tall, right, blank, left], axis=1).reshape(-1, feats)
    vmem = pl.BlockSpec(memory_space=pltpu.VMEM)
    block = 256
    return pl.pallas_call(
        functools.partial(conv_kernel, row_count, col_count),
        out_shape=(
            jax.ShapeDtypeStruct((row_count * col_count, width), jnp.bfloat16),
            jax.ShapeDtypeStruct((1, width), jnp.float32),
        ),
        in_specs=[pl.BlockSpec(memory_space=pltpu.SMEM)] + [vmem] * 5,
        out_specs=(vmem, vmem),
        scratch_shapes=[
            pltpu.VMEM(ext.shape, jnp.bfloat16),
            pltpu.VMEM((row_count + 2, col_count + PAD, block), jnp.float32),
        ],
        compiler_params=pltpu.CompilerParams(vmem_limit_bytes=20 * 1024 * 1024),
        name="conv_stage",
    )(flags, ext, conv_scale[None], conv_shift[None], expand_weight, depth_kernel)


def per_device(
    latent,
    conv_scale,
    conv_shift,
    expand_weight,
    depth_kernel,
    squeeze_down,
    squeeze_up,
    project_weight,
    block_gain,
    block_projection,
    block_output,
    block_table,
    first_gain,
    first_expand,
    first_reduce,
    grid_gain,
    grid_projection,
    grid_output,
    grid_table,
    second_gain,
    second_expand,
    second_reduce,
):
    row_devices = lax.axis_size("row")
    col_devices = lax.axis_size("col")
    row_count, col_count, channels = latent.shape
    if compact(row_count, col_count) and squeeze_up.shape[0] == LANES:
        return whole_block(
            latent, conv_scale, conv_shift, depth_kernel, (block_table, grid_table),
            (block_gain, first_gain, grid_gain, second_gain),
            (expand_weight, squeeze_down, squeeze_up, project_weight),
            (block_projection, block_output, first_expand, first_reduce,
             grid_projection, grid_output, second_expand, second_reduce),
        )
    depthwise, local_sums = depthwise_stage(
        latent, conv_scale, conv_shift, expand_weight, depth_kernel
    )
    local_sums = local_sums.reshape(-1, LANES)
    channel_sums = axis_sum(axis_sum(local_sums, "row", 1), "col", 2).reshape(-1)
    pooled = channel_sums / (row_count * row_devices * col_count * col_devices)
    excite = squeeze_gate(pooled, squeeze_down, squeeze_up)
    gated = (depthwise.astype(jnp.float32) * excite).astype(jnp.bfloat16)
    conv_out = (
        latent.reshape(-1, channels).astype(jnp.float32)
        + jnp.dot(gated, project_weight, preferred_element_type=jnp.float32)
    ).astype(jnp.bfloat16).reshape(row_count, col_count, channels)

    def run_block(cells, layout, bias):
        return mixer(
            cells, layout, block_gain, block_projection, block_output, bias, first_gain,
            first_expand, first_reduce, block_table.shape[0],
        )

    def run_grid(cells, layout, bias):
        return mixer(
            cells, layout, grid_gain, grid_projection, grid_output, bias, second_gain,
            second_expand, second_reduce, grid_table.shape[0],
        )

    return split_sublayers(conv_out, run_block, run_grid, block_table, grid_table)


def solution(mesh):
    placed = (
        P("row", "col", None),
        P(),
        P(),
        P(),
        P(),
        P(),
        P(),
        P(),
        P(),
        P(),
        P(),
        P(),
        P(),
        P(),
        P(),
        P(),
        P(),
        P(),
        P(),
        P(),
        P(),
        P(),
    )
    return jax.shard_map(
        per_device, mesh=mesh, in_specs=placed, out_specs=P("row", "col", None), check_vma=False
    )
```
